32 devices in a mesh: src: 4 (over z), dst: 8 (over y, x, core).
Axes of the slice: x: 2, y: 2, z: 4, core: 2. Of those that a mesh axis runs over, the one named last changes fastest.
Arguments:
- src_emb: bfloat16 [65536, 128], P('src'), may hold values from -1.5 to 1.5
- dst_emb: bfloat16 [65536, 128], P('dst'), may hold values from -1.5 to 1.5
- out_emb: bfloat16 [65536, 128], P('dst'), may hold values from -1.5 to 1.5
- word_table: bfloat16 [32768, 128], P('dst'), may hold values from -1.5 to 1.5
- log_norm: float32 [65536], P('dst'), may hold values from 9 to 11
- block_mask: int32 [128, 128], P('src', 'dst'), may hold values from 0 to 1, as said below
- tokens: int32 [3, 8], replicated, may hold values from 0 to 32767
- alpha_start: float32 [8, 65536], P(None, 'src'), may hold values from 0.5 to 80
- beta_end: float32 [8, 65536], P(None, 'dst'), may hold values from 0.5 to 80
Outputs:
- alpha_end: float32 [8, 65536], P(None, 'dst')
- beta_start: float32 [8, 65536], P(None, 'src')
- block_counts: float32 [128, 128], P('src', 'dst')
The draws below stay inside these ranges and needn't reach their ends.
Inputs may be any that keep to these rules, and one draw needn't show every extreme that they name: block_mask[I, I] = 1 for every block I: a state may always move within its own block.
All inputs are finite; a program needn't handle non-finite values.
Results may differ from the reference program's by a relative error of at most 0.0032.
Values may be sent and summed in bfloat16 or wider, within the bound.
A program may use at most 384 MiB of HBM per device.

```python
import math
import jax
import jax.numpy as jnp
import numpy as np
from jax import lax

S = 65536
BLK = 512
E = 128
V = 32768
TRACES = 8
STEPS = 3
NB = 128


def draw_src_emb(key, part):
    values = jnp.clip(0.3 * jax.random.normal(jax.random.fold_in(key, 1), (S, E), jnp.float32), -1.5, 1.5)
    return values.astype(jnp.bfloat16)


def draw_dst_emb(key, part):
    values = jnp.clip(0.3 * jax.random.normal(jax.random.fold_in(key, 2), (S, E), jnp.float32), -1.5, 1.5)
    return values.astype(jnp.bfloat16)


def rising_vector(key, salt):
    position = jnp.arange(S, dtype=jnp.float32) / S
    ramp = jnp.exp(jnp.log(10.0) * position)
    rough = jnp.exp(jax.random.uniform(jax.random.fold_in(key, salt), (TRACES, S), jnp.float32, -0.69, 0.69))
    return ramp[None, :] * rough


def draw_alpha_start(key, part):
    return rising_vector(key, 11)


def draw_beta_end(key, part):
    return rising_vector(key, 13)


def draw_block_mask(key, part):
    coin_flips = jax.random.randint(key, (NB, NB), 0, 16)
    rows = jnp.arange(NB)[:, None]
    cols = jnp.arange(NB)[None, :]
    diagonal = rows == cols
    near = jnp.abs(rows - cols) <= NB // 8
    keep = diagonal | near & (coin_flips < 8) | (coin_flips == 0)
    return jnp.where(keep, 1, 0).astype(jnp.int32)


def place_ends(drawn, key, low, largest):
    longest = drawn.shape.index(max(drawn.shape))
    spots = []
    for shift in (0, 1):
        where = [jax.random.randint(jax.random.fold_in(key, axis), (), 0, length) for axis, length in enumerate(drawn.shape)]
        where[longest] = (where[longest] + shift) % drawn.shape[longest]
        spots.append(tuple(where))
    return drawn.at[spots[0]].set(low).at[spots[1]].set(largest)


def block_scale(key, dims, split, low, largest):
    level, own = 1.0, jax.random.fold_in(key, 6)
    for dim, shards_of in split:
        steps = jnp.exp(jax.random.uniform(jax.random.fold_in(own, dim), (shards_of,), jnp.float32, low / len(split), largest / len(split)))
        level = level * jnp.repeat(steps, dims[dim] // shards_of).reshape([-1 if axis == dim else 1 for axis in range(len(dims))])
    return level


def rank_bounds(number_of, slope):
    portions = [(1 << 20) // math.isqrt(grade ** slope) + 1 for grade in range(1, number_of + 1)]
    scale = 1 + sum(portions) // (1 << 30)
    return np.cumsum(np.array([max(1, weight // scale) for weight in portions]))


def ranked(rng, extent, number_of, skew):
    listing = rank_bounds(number_of, skew)
    pick = jax.random.randint(jax.random.fold_in(rng, 1), extent, 0, int(listing[number_of - 1]))
    grade = jnp.searchsorted(jnp.asarray(listing, jnp.int32), pick, side="right")
    return jax.random.permutation(jax.random.fold_in(rng, 2), number_of)[grade].astype(jnp.int32)


def gaussian(key, shape, deviation, most, shards=(), kind=jnp.bfloat16):
    values = deviation * jax.random.normal(key, shape, jnp.float32)
    if shards:
        values = values * block_scale(key, shape, shards, -0.22, 0.18)
    return jnp.clip(values, -most, most).astype(kind)


def setup_inputs(seed: int = 0) -> dict:
    key_of = jax.random.split(jax.random.key(seed), 10)
    src_emb = draw_src_emb(jax.random.fold_in(key_of[9], 71), 0)
    dst_emb = draw_dst_emb(jax.random.fold_in(key_of[9], 71), 0)
    out_emb = gaussian(key_of[2], (S, E), 0.3, 1.5, ((0, 8),))
    word_table = gaussian(key_of[3], (V, E), 0.3, 1.5, ((0, 8),))
    log_norm = jnp.clip(9.0 + 2.0 * jax.random.uniform(key_of[4], (S,), jnp.float32) ** block_scale(key_of[4], (S,), ((0, 8),), -0.2, 0.2), 9.0, 11.0)
    block_mask = draw_block_mask(jax.random.fold_in(key_of[9], 71), 0)
    tokens = place_ends(ranked(key_of[6], (STEPS, TRACES), V, 2), jax.random.fold_in(key_of[6], 3), 0, V - 1).astype(jnp.int32)
    alpha_start = draw_alpha_start(jax.random.fold_in(key_of[9], 71), 0)
    beta_end = draw_beta_end(jax.random.fold_in(key_of[9], 71), 0)
    return dict(src_emb=src_emb, dst_emb=dst_emb, out_emb=out_emb, word_table=word_table, log_norm=log_norm, block_mask=block_mask, tokens=tokens, alpha_start=alpha_start, beta_end=beta_end)


very_negative = -1e30


def block_tables(src_rows, dst_emb, mask_row):
    scores = jnp.dot(src_rows, dst_emb.T, preferred_element_type=jnp.float32)
    scores = scores.reshape(src_rows.shape[0], NB, BLK)
    block_top = jnp.max(scores, axis=2)
    block_sum = jnp.sum(jnp.exp(scores - block_top[:, :, None]), axis=2)
    allowed = (mask_row == 1)[None, :]
    row_best = jnp.max(jnp.where(allowed, block_top, very_negative), axis=1)
    row_mass = jnp.sum(jnp.where(allowed, block_sum * jnp.exp(block_top - row_best[:, None]), 0.0), axis=1)
    log_total = row_best + jnp.log(row_mass)
    factor = jnp.where(allowed, jnp.exp(block_top - log_total[:, None]), 0.0)
    transit = jnp.where(allowed[:, :, None], jnp.exp(scores - block_top[:, :, None]), 0.0).astype(jnp.bfloat16)
    return factor, transit


def sweep(src_emb, dst_emb, block_mask, alphas, weights):
    members = alphas.shape[0]
    traces = alphas.shape[1]
    src_blocks = src_emb.reshape(NB, BLK, E)
    alpha_blocks = alphas.reshape(members, traces, NB, BLK).transpose(2, 0, 1, 3)
    weight_cols = weights.reshape(members, traces, NB, BLK).astype(jnp.float32)

    def one_block(running, inputs):
        src_rows, mask_row, alpha_rows = inputs
        factor, transit = block_tables(src_rows, dst_emb, mask_row)
        transit_wide = transit.astype(jnp.float32)
        mix_terms = (alpha_rows[:, :, :, None] * factor[None, None]).astype(jnp.bfloat16)
        mix_wide = mix_terms.astype(jnp.float32)
        running = running + jnp.einsum("abin,inc->abnc", mix_wide, transit_wide)
        spread = jnp.einsum("inc,abnc->abin", transit_wide, weight_cols)
        partial_value = jnp.sum(factor[None, None] * spread, axis=3)
        block_terms = jnp.sum(mix_wide * spread, axis=2)
        return running, (partial_value, block_terms)

    zeros_start = jnp.zeros((members, traces, NB, BLK), jnp.float32)
    predicted, (partial_value, block_terms) = lax.scan(one_block, zeros_start, (src_blocks, block_mask, alpha_blocks))
    predicted = predicted.reshape(members, traces, S)
    partial_value = partial_value.transpose(1, 2, 0, 3).reshape(members, traces, S)
    return predicted, partial_value, block_terms


def normalize(vector):
    return vector / (jnp.sum(vector, axis=1, keepdims=True) / S)


def reference(src_emb, dst_emb, out_emb, word_table, log_norm, block_mask, tokens, alpha_start, beta_end):
    traces = tokens.shape[1]
    word_rows = word_table[tokens.reshape(-1)]
    logits = jnp.dot(word_rows, out_emb.T, preferred_element_type=jnp.float32)
    emission = jnp.exp(logits - log_norm[None, :]).reshape(STEPS, traces, S)
    alphas = [alpha_start]
    beta_store = {STEPS: beta_end}

    def weight_at(k):
        return (emission[k - 1] * beta_store[k]).astype(jnp.bfloat16)

    for k in range(1, STEPS):
        predicted, partial_value, _ = sweep(src_emb, dst_emb, block_mask, alphas[k - 1][None], weight_at(STEPS - k + 1)[None])
        alphas.append(normalize(predicted[0] * emission[k - 1]))
        beta_store[STEPS - k] = normalize(partial_value[0])
    final_alphas = jnp.stack(alphas)
    final_weights = jnp.stack([weight_at(t + 1) for t in range(STEPS)])
    predicted, partial_value, block_terms = sweep(src_emb, dst_emb, block_mask, final_alphas, final_weights)
    alpha_end = normalize(predicted[STEPS - 1] * emission[STEPS - 1])
    beta_start = normalize(partial_value[0])
    pair_total = jnp.sum(block_terms, axis=(0, 3))
    counts = jnp.sum(block_terms / pair_total[None, :, :, None], axis=(1, 2)) * (NB * NB / (STEPS * traces))
    return alpha_end, beta_start, counts
```

```python
import functools

import jax
import jax.numpy as jnp
from jax import lax
from jax.experimental import pallas as pl
from jax.experimental.pallas import tpu as pltpu
from jax.sharding import PartitionSpec as P

BLK = 512
STEPS = 3
LANES = 128
DEPTH = 8
very_negative = -1e30
GROUP = 4
HELD_BYTES = 40 * 1024 * 1024
TABLE_BYTES = 16 * 1024 * 1024
VMEM_BYTES = 16 * 1024 * 1024


def table_kernel(
    unit, cols, held, ids, count, src, dst, top, mass, near, far,
    buf_0, buf_1, scores_0, scores_1, best_0, best_1, sems,
):
    number = count[0]
    chunk = min(128, unit)
    pieces = unit // chunk
    top[...] = jnp.full_like(top, very_negative)
    mass[...] = jnp.zeros_like(mass)

    def place(slot):
        entry = ids[slot]
        return lax.div(entry, cols), lax.rem(entry, cols)

    def score(slot, scores, best, c):
        i, j = place(slot)
        d = dst[pl.ds(pl.multiple_of(j * BLK, BLK), BLK), :]
        value = lax.dot_general(
            d, src[pl.ds(pl.multiple_of(i * unit + c * chunk, chunk), chunk), :],
            (((1,), (1,)), ((), ())), preferred_element_type=jnp.float32,
        )
        scores[:, c * chunk:(c + 1) * chunk] = value
        best[:, c * chunk:(c + 1) * chunk] = jnp.max(value, axis=0, keepdims=True)

    def phase(slot, scores, best, later, scores_next, best_next, put):
        sums = []
        for c in range(pieces):
            score(later, scores_next, best_next, c)
            span = slice(c * chunk, (c + 1) * chunk)
            risen = jnp.exp(scores[:, span] - best[:, span])
            put(span, risen.astype(jnp.bfloat16))
            sums.append(jnp.sum(risen, axis=0, keepdims=True))
        i, j = place(slot)
        rows = pl.ds(pl.multiple_of(i * unit, unit), unit)
        top[pl.ds(j, 1), rows] = best[...]
        mass[pl.ds(j, 1), rows] = jnp.concatenate(sums, axis=1)

    def run(low, high, out):
        for c in range(pieces):
            score(low, scores_0, best_0, c)

        def body(p, carry):
            even = low + 2 * p
            odd = jnp.minimum(even + 1, high - 1)
            after = jnp.minimum(even + 2, high - 1)
            with_even, with_odd = out(p, even, odd, high)
            with_even(lambda put: phase(even, scores_0, best_0, odd, scores_1, best_1, put))
            with_odd(lambda put: phase(odd, scores_1, best_1, after, scores_0, best_0, put))
            return carry

        lax.fori_loop(0, lax.div(high - low + 1, 2), body, 0)

    def keep(p, even, odd, high):
        def store(slot):
            def put(span, value):
                near[slot, :, span] = value

            return put

        return lambda go: go(store(even)), lambda go: go(store(odd))

    def copy(slot, buf, b):
        return pltpu.make_async_copy(buf, far.at[slot - held], sems.at[b])

    def send(p, even, odd, high):
        def through(slot, buf, b, live):
            def put(span, value):
                buf[:, span] = value

            def go(step):
                @pl.when(p > 0)
                def _():
                    copy(slot, buf, b).wait()

                step(put)

                @pl.when(live)
                def _():
                    copy(slot, buf, b).start()

            return go

        return through(even, buf_0, 0, even < high), through(odd, buf_1, 1, even + 1 < high)

    @pl.when(number > held)
    def _():
        run(held, number, send)

    @pl.when(number > 0)
    def _():
        run(0, jnp.minimum(number, held), keep)

    @pl.when(number > held)
    def _():
        copy(held, buf_0, 0).wait()

    @pl.when((number > held) & (lax.rem(number - held, 2) == 0))
    def _():
        copy(held, buf_1, 1).wait()


def sweep_kernel(unit, cols, held, traces, kind, ids, count, *refs):
    if kind == 2:
        alpha, early, factor, weight, last, near, far, pred, carried, terms, buf, sems = refs
    elif kind == 1:
        alpha, factor, weight, near, far, pred, carried, terms, buf, sems = refs
    else:
        alpha, factor, weight, near, far, pred, carried, buf, sems = refs
    number = count[0]
    pred[...] = jnp.zeros_like(pred)
    carried[...] = jnp.zeros_like(carried)
    if kind:
        terms[...] = jnp.zeros_like(terms)

    def copy(slot):
        b = lax.rem(slot - held, DEPTH)
        return pltpu.make_async_copy(far.at[slot - held], buf.at[b], sems.at[b])

    for p in range(DEPTH):

        @pl.when(held + p < number)
        def _():
            copy(held + p).start()

    def group(slots, high, tile):
        found = []
        for slot in slots:
            real = jnp.minimum(slot, high - 1)
            entry = ids[real]
            i = lax.div(entry, cols)
            j = lax.rem(entry, cols)
            rows = pl.ds(pl.multiple_of(i * unit, unit), unit)
            places = pl.ds(pl.multiple_of(j * BLK, BLK), BLK)
            share = factor[pl.ds(j, 1), rows] * jnp.where(slot < high, 1.0, 0.0)
            mix = (alpha[:, rows] * share).astype(jnp.bfloat16)
            block = tile(real)
            ahead = lax.dot_general(
                mix, block, (((1,), (1,)), ((), ())), preferred_element_type=jnp.float32
            )
            spread = jnp.dot(weight[:, places], block, preferred_element_type=jnp.float32)
            values = []
            if kind == 1:
                values.append(mix.astype(jnp.float32) * spread)
            elif kind == 2:
                first = (early[:, rows] * share).astype(jnp.bfloat16)
                values.append(first.astype(jnp.float32) * spread)
                values.append(last[:, places].astype(jnp.float32) * ahead)
            values = [jnp.sum(v, axis=1, keepdims=True) for v in values]
            found.append((i, j, rows, places, ahead, share * spread, values))
        for i, j, rows, places, ahead, behind, values in found:
            pred[:, places] += ahead
            carried[:, rows] += behind
            for t, value in enumerate(values):
                hit = lax.broadcasted_iota(jnp.int32, terms.shape[2:], 1) == j
                terms[t, i] += jnp.where(hit, value, 0.0)

    near_count = jnp.minimum(number, held)

    def near_body(g, carry):
        group([g * GROUP + u for u in range(GROUP)], near_count, lambda slot: near[slot])
        return carry

    lax.fori_loop(0, lax.div(near_count + GROUP - 1, GROUP), near_body, 0)

    def far_body(g, carry):
        slots = [held + g * GROUP + u for u in range(GROUP)]
        for slot in slots:

            @pl.when(slot < number)
            def _():
                copy(slot).wait()

        group(slots, number, lambda slot: buf[lax.rem(slot - held, DEPTH)])
        for slot in slots:

            @pl.when(slot + DEPTH < number)
            def _():
                copy(slot + DEPTH).start()

        return carry

    far_count = number - near_count
    lax.fori_loop(0, lax.div(far_count + GROUP - 1, GROUP), far_body, 0)


class Lines:
    def __init__(self, lines):
        self.lines = lines
        self.place = {name: lax.axis_index(name) for name in lines}

    def peer(self, name, k):
        return lax.rem(self.place[name] + k, self.lines[name])

    def origin(self, name, k):
        return lax.rem(self.place[name] + self.lines[name] - k, self.lines[name])

    def greet(self):
        barrier = pltpu.get_barrier_semaphore()
        for name in self.lines:
            for k in range(1, self.lines[name]):
                pl.semaphore_signal(
                    barrier, inc=1, device_id={name: self.peer(name, k)},
                    device_id_type=pl.DeviceIdType.MESH,
                )

    def gather_in(self, more=0):
        total = sum(self.lines.values()) - len(self.lines) + more
        pl.semaphore_wait(pltpu.get_barrier_semaphore(), total)

    def send(self, name, source, landing, send, recv):
        copies = []
        for k in range(1, self.lines[name]):
            copy = pltpu.make_async_remote_copy(
                src_ref=source(self.peer(name, k)),
                dst_ref=landing.at[k],
                send_sem=send.at[k],
                recv_sem=recv.at[k],
                device_id={name: self.peer(name, k)},
                device_id_type=pl.DeviceIdType.MESH,
            )
            copy.start()
            copies.append(copy)
        return copies


def stats_kernel(
    lines, piece, top, mass, alpha, near, factor, spread_alpha,
    parts, land, merged, land_2, land_a, *sems,
):
    net = Lines(lines)
    net.greet()
    count = lines["dst"]
    for p in range(count):
        rows = slice(p * piece, (p + 1) * piece)
        best = jnp.max(top[:, rows], axis=0, keepdims=True)
        total = jnp.sum(mass[:, rows] * jnp.exp(top[:, rows] - best), axis=0, keepdims=True)
        parts[p] = jnp.where(
            total > 0.0, best + jnp.log(jnp.maximum(total, 1e-37)), very_negative
        )
    net.gather_in()
    first = net.send("dst", lambda peer: parts.at[peer], land, sems[0], sems[1])
    sent = net.send("dst", lambda peer: alpha, land_a, sems[4], sems[5])
    land[0] = parts[net.place["dst"]]
    for copy in first:
        copy.wait_recv()
    best = land[0]
    for k in range(1, count):
        best = jnp.maximum(best, land[k])
    total = jnp.zeros_like(best)
    for k in range(count):
        total = total + jnp.exp(land[k] - best)
    merged[...] = best + jnp.log(total)
    second = net.send("dst", lambda peer: merged, land_2, sems[2], sems[3])

    def finish(k, level):
        rows = pl.ds(pl.multiple_of(net.origin("dst", k) * piece, piece), piece)
        factor[:, rows] = jnp.exp(top[:, rows] - level)

    finish(0, merged[...])
    for k in range(count):
        rows = pl.ds(pl.multiple_of(net.origin("dst", k) * piece, piece), piece)
        if k:
            sent[k - 1].wait_recv()
        spread_alpha[:, rows] = (alpha[...] if k == 0 else land_a[k]).astype(jnp.float32)
    for k in range(1, count):
        second[k - 1].wait_recv()
        finish(k, land_2[k])
    for copy in first + second + sent:
        copy.wait_send()


def exchange_kernel(
    lines, piece, states, pred, carried, glow, glow_next, near, alpha, weights,
    out_f, out_b, in_f, in_b, red_f, red_b, land_f, land_b, *sems,
):
    net = Lines(lines)
    net.greet()
    shape = (pred.shape[0], LANES)
    total_f = jnp.broadcast_to(
        jnp.sum(pred[...] * glow[...], axis=1, keepdims=True), shape
    ).astype(jnp.bfloat16)
    total_b = jnp.broadcast_to(
        jnp.sum(carried[...], axis=1, keepdims=True), shape
    ).astype(jnp.bfloat16)
    payload = {"src": (out_f, pred, total_f), "dst": (out_b, carried, total_b)}
    for name, (out, value, total) in payload.items():
        for p in range(lines[name]):
            out[p, :, :piece] = value[:, p * piece:(p + 1) * piece].astype(jnp.bfloat16)
            out[p, :, piece:] = total
    net.gather_in()
    landing = {"src": in_f, "dst": in_b}
    first = {}
    for n, name in enumerate(("src", "dst")):
        out = payload[name][0]
        first[name] = net.send(
            name, lambda peer, out=out: out.at[peer], landing[name], sems[n], sems[2 + n]
        )
    second = {}
    order = (("src", "dst", red_f, land_f), ("dst", "src", red_b, land_b))
    for n, (name, other, red, land) in enumerate(order):
        value = payload[name][0][net.place[name]].astype(jnp.float32)
        for k in range(1, lines[name]):
            first[name][k - 1].wait_recv()
            value = value + landing[name][k].astype(jnp.float32)
        part, total = value[:, :piece], value[:, piece:]
        if name == "src":
            start = pl.multiple_of(net.place["src"] * piece, piece)
            part = part * glow[:, pl.ds(start, piece)]
        red[:, :piece] = part.astype(jnp.bfloat16)
        red[:, piece:] = total.astype(jnp.bfloat16)
        second[other] = net.send(
            other, lambda peer, red=red: red, land, sems[4 + n], sems[6 + n]
        )
    for name, red, land in (("dst", red_f, land_f), ("src", red_b, land_b)):
        total = red[:, piece:piece + 1].astype(jnp.float32)
        for k in range(1, lines[name]):
            second[name][k - 1].wait_recv()
            total = total + land[k, :, piece:piece + 1].astype(jnp.float32)
        scale = states / total
        for k in range(lines[name]):
            part = red[:, :piece] if k == 0 else land[k, :, :piece]
            start = pl.multiple_of(net.origin(name, k) * piece, piece)
            part = part.astype(jnp.float32) * scale
            if name == "dst":
                alpha[:, pl.ds(start, piece)] = part
            else:
                part = part * glow_next[:, pl.ds(start, piece)]
                weights[:, pl.ds(start, piece)] = part.astype(jnp.bfloat16)
    for copies in (*first.values(), *second.values()):
        for copy in copies:
            copy.wait_send()


def final_kernel(
    lines, piece, states, norm, pred, carried, glow, mid_terms, end_terms, owner,
    alpha, beta, counts,
    out_f, in_f, red_f, land_f, out_b, in_b, red_b, natural, land_b,
    sums, in_s, red_s, land_s, mine, in_c, *sems,
):
    net = Lines(lines)
    net.greet()
    src, dst = lines["src"], lines["dst"]
    traces = pred.shape[0]
    shape = (traces, LANES)
    number = net.place["dst"] * src + net.place["src"]
    to_src, to_dst = lax.div(number, dst), lax.rem(number, dst)
    held = net.place["src"] * dst + net.place["dst"]
    from_dst, from_src = lax.div(held, src), lax.rem(held, src)
    away = (to_src != net.place["src"]) | (to_dst != net.place["dst"])
    barrier = pltpu.get_barrier_semaphore()

    @pl.when(away)
    def _():
        for s, d in ((to_src, to_dst), (from_src, from_dst)):
            pl.semaphore_signal(
                barrier, inc=1, device_id={"src": s, "dst": d},
                device_id_type=pl.DeviceIdType.MESH,
            )

    terms = [mid_terms[0], end_terms[0], end_terms[1]]
    rows = [jnp.sum(pred[...] * glow[...], axis=1, keepdims=True)]
    rows.append(jnp.sum(carried[...], axis=1, keepdims=True))
    for t in terms:
        rows.append(jnp.sum(jnp.sum(t, axis=0), axis=1, keepdims=True))
    for n, row in enumerate(rows):
        sums[n] = jnp.broadcast_to(row, shape)
    for p in range(src):
        out_f[p] = pred[:, p * piece:(p + 1) * piece]
    for p in range(dst):
        out_b[p] = carried[:, p * piece:(p + 1) * piece]

    @pl.when(away)
    def _():
        net.gather_in(2)

    @pl.when(jnp.logical_not(away))
    def _():
        net.gather_in()

    first_s = net.send("src", lambda peer: sums, in_s, sems[0], sems[1])
    first_b = net.send("dst", lambda peer: out_b.at[peer], in_b, sems[2], sems[3])
    first_f = net.send("src", lambda peer: out_f.at[peer], in_f, sems[4], sems[5])

    total = sums[...]
    for k in range(1, src):
        first_s[k - 1].wait_recv()
        total = total + in_s[k]
    red_s[...] = total
    second_s = net.send("dst", lambda peer: red_s, land_s, sems[6], sems[7])

    value = out_f[net.place["src"]]
    for k in range(1, src):
        first_f[k - 1].wait_recv()
        value = value + in_f[k]
    start = pl.multiple_of(net.place["src"] * piece, piece)
    red_f[...] = value * glow[:, pl.ds(start, piece)]
    second_f = net.send("src", lambda peer: red_f, land_f, sems[8], sems[9])

    value = out_b[net.place["dst"]]
    for k in range(1, dst):
        first_b[k - 1].wait_recv()
        value = value + in_b[k]
    red_b[...] = value
    move = pltpu.make_async_remote_copy(
        src_ref=red_b, dst_ref=natural, send_sem=sems[10].at[0], recv_sem=sems[10].at[1],
        device_id={"src": to_src, "dst": to_dst}, device_id_type=pl.DeviceIdType.MESH,
    )

    @pl.when(away)
    def _():
        move.start()

    total = red_s[...]
    for k in range(1, dst):
        second_s[k - 1].wait_recv()
        total = total + land_s[k]
    level = jnp.zeros(mine.shape, jnp.float32)
    for t in range(len(terms)):
        share = norm / total[2 + t]
        level = level + jnp.sum(terms[t] * share[None], axis=1)
    mine[...] = level
    third_c = net.send("src", lambda peer: mine, in_c, sems[11], sems[12])

    @pl.when(away)
    def _():
        move.wait_recv()

    @pl.when(jnp.logical_not(away))
    def _():
        natural[...] = red_b[...]

    third_b = net.send("dst", lambda peer: natural, land_b, sems[13], sems[14])

    scale = states / total[0][:, :1]
    for k in range(src):
        if k:
            second_f[k - 1].wait_recv()
        part = red_f[...] if k == 0 else land_f[k]
        begin = pl.multiple_of(net.origin("src", k) * piece, piece)
        alpha[:, pl.ds(begin, piece)] = part * scale
    value = jnp.zeros(counts.shape, jnp.float32)
    for k in range(src):
        if k:
            third_c[k - 1].wait_recv()
        value = value + jnp.dot(
            owner[net.origin("src", k)], mine[...] if k == 0 else in_c[k],
            precision=lax.Precision.HIGHEST, preferred_element_type=jnp.float32,
        )
    counts[...] = value
    scale = states / total[1][:, :1]
    for k in range(dst):
        if k:
            third_b[k - 1].wait_recv()
        part = natural[...] if k == 0 else land_b[k]
        begin = pl.multiple_of(net.origin("dst", k) * piece, piece)
        beta[:, pl.ds(begin, piece)] = part * scale

    @pl.when(away)
    def _():
        move.wait_send()

    for copies in (first_s, first_b, first_f, second_s, second_f, third_c, third_b):
        for copy in copies:
            copy.wait_send()


def local(
    src_emb, dst_emb, out_emb, word_table, log_norm, block_mask, tokens, alpha_start, beta_end
):
    row_count, emb_width = src_emb.shape
    col_count = dst_emb.shape[0]
    traces = alpha_start.shape[0]
    src_count = lax.axis_size("src")
    dst_count = lax.axis_size("dst")
    states = row_count * src_count
    group = dst_count // src_count
    piece = col_count // src_count
    unit = min(BLK, piece)
    units = row_count // unit
    cols = col_count // BLK
    places = units * cols
    padded = -(-places // LANES) * LANES
    src_place = lax.axis_index("src")
    dst_place = lax.axis_index("dst")
    both = ("src", "dst")
    moves = [
        ((d // group) * dst_count + (d % group) * src_count + z, z * dst_count + d)
        for z in range(src_count)
        for d in range(dst_count)
    ]

    def spread_rows(mine):
        moved = lax.ppermute(mine, both, moves)
        return lax.all_gather(moved, "dst", axis=0, tiled=True)

    mine = lax.dynamic_slice_in_dim(src_emb, dst_place * piece, piece, 0)
    src_rows = spread_rows(mine)
    alpha_piece = lax.dynamic_slice_in_dim(alpha_start, dst_place * piece, piece, 1)
    alpha_moved = lax.ppermute(alpha_piece, both, moves)

    whole_mask = lax.all_gather(block_mask, "src", axis=0, tiled=True)
    unit_index = jnp.arange(units, dtype=jnp.int32)
    per_piece = piece // unit
    unit_state = (
        (unit_index // per_piece) * col_count + src_place * piece + (unit_index % per_piece) * unit
    )
    unit_block = unit_state // BLK
    owner = unit_block[:, None] == jnp.arange(whole_mask.shape[0], dtype=jnp.int32)[None, :]
    mask = jnp.sum(jnp.where(owner[:, :, None], whole_mask[None], 0), axis=1)
    flat = (mask == 1).reshape(places)
    index = jnp.arange(places, dtype=jnp.int32)
    before = jnp.sum(
        jnp.where((index[None, :] < index[:, None]) & flat[None, :], 1, 0), axis=1
    )
    ids = jnp.sum(
        jnp.where((before[None, :] == index[:, None]) & flat[None, :], index[None, :], 0), axis=1
    ).astype(jnp.int32)
    number = jnp.sum(flat.astype(jnp.int32)).reshape(1)

    smem = pl.BlockSpec(memory_space=pltpu.SMEM)
    vmem = pl.BlockSpec(memory_space=pltpu.VMEM)
    anywhere = pl.BlockSpec(memory_space=pl.ANY)
    guess = places // 5 + 1
    held = min(places, HELD_BYTES // (BLK * unit * 2))
    params = pltpu.CompilerParams(vmem_limit_bytes=VMEM_BYTES)
    top, mass, near, far = pl.pallas_call(
        functools.partial(table_kernel, unit, cols, held),
        out_shape=(
            jax.ShapeDtypeStruct((cols, row_count), jnp.float32),
            jax.ShapeDtypeStruct((cols, row_count), jnp.float32),
            pltpu.VMEM((held, BLK, unit), jnp.bfloat16),
            jax.ShapeDtypeStruct((max(places - held, 1), BLK, unit), jnp.bfloat16),
        ),
        in_specs=[smem, smem, vmem, vmem],
        out_specs=(vmem, vmem, vmem, anywhere),
        scratch_shapes=[pltpu.VMEM((BLK, unit), jnp.bfloat16)] * 2
        + [pltpu.VMEM((BLK, unit), jnp.float32)] * 2
        + [pltpu.VMEM((1, unit), jnp.float32)] * 2
        + [pltpu.SemaphoreType.DMA((2,))],
        compiler_params=pltpu.CompilerParams(vmem_limit_bytes=TABLE_BYTES),
        cost_estimate=pl.CostEstimate(
            flops=guess * BLK * unit * emb_width * 2,
            bytes_accessed=guess * BLK * unit,
            transcendentals=guess * BLK * unit,
        ),
        name="table",
    )(ids, number, src_rows, dst_emb)
    near = pltpu.with_memory_space_constraint(near, pltpu.VMEM)

    vocab_slice = word_table.shape[0]
    local_ids = tokens.reshape(-1) - dst_place * vocab_slice
    onehot = (local_ids[:, None] == jnp.arange(vocab_slice, dtype=jnp.int32)[None, :]).astype(
        jnp.bfloat16
    )
    looked = jnp.dot(onehot, word_table, preferred_element_type=jnp.float32)
    word_rows = lax.psum(looked.astype(jnp.bfloat16), "dst")
    logits = lax.dot_general(
        word_rows, out_emb, (((1,), (1,)), ((), ())), preferred_element_type=jnp.float32
    )
    emission = jnp.exp(logits - log_norm[None, :]).reshape(STEPS, traces, col_count)
    lines = {"src": src_count, "dst": dst_count}

    def f32(*shape):
        return jax.ShapeDtypeStruct(shape, jnp.float32)

    def room(*shape, dtype=jnp.float32):
        return pltpu.VMEM(shape, dtype)

    half = functools.partial(room, dtype=jnp.bfloat16)
    on_src = pltpu.SemaphoreType.DMA((src_count,))
    on_dst = pltpu.SemaphoreType.DMA((dst_count,))
    factor, alpha_rows = pl.pallas_call(
        functools.partial(stats_kernel, lines, piece),
        out_shape=(f32(cols, row_count), f32(traces, row_count)),
        in_specs=[vmem] * 4,
        out_specs=(vmem,) * 2,
        scratch_shapes=[
            room(dst_count, 1, piece),
            room(dst_count, 1, piece),
            room(1, piece),
            room(dst_count, 1, piece),
            half(dst_count, traces, piece),
        ]
        + [on_dst] * 6,
        compiler_params=pltpu.CompilerParams(
            collective_id=0, has_side_effects=True, vmem_limit_bytes=VMEM_BYTES
        ),
        name="stats",
    )(top, mass, alpha_moved.astype(jnp.bfloat16), near)

    lanes = -(-cols // LANES) * LANES

    def sweep(kind, alphas, weights):
        outs = [f32(traces, col_count), f32(traces, row_count)]
        if kind:
            outs.append(f32(kind, units, traces, lanes))
        return pl.pallas_call(
            functools.partial(sweep_kernel, unit, cols, held, traces, kind),
            out_shape=tuple(outs),
            in_specs=[smem, smem] + [vmem] * (len(alphas) + 2 + len(weights)) + [anywhere],
            out_specs=(vmem,) * len(outs),
            scratch_shapes=[
                pltpu.VMEM((DEPTH, BLK, unit), jnp.bfloat16),
                pltpu.SemaphoreType.DMA((DEPTH,)),
            ],
            compiler_params=params,
            cost_estimate=pl.CostEstimate(
                flops=guess * BLK * unit * traces * 4,
                bytes_accessed=guess * BLK * unit,
                transcendentals=0,
            ),
            name="sweep%d" % kind,
        )(ids, number, *alphas, factor, *weights, near, far)

    def exchange(ahead, behind, glow, glow_next):
        width = piece + LANES
        return pl.pallas_call(
            functools.partial(exchange_kernel, lines, piece, states),
            out_shape=(
                f32(traces, row_count),
                jax.ShapeDtypeStruct((traces, col_count), jnp.bfloat16),
            ),
            in_specs=[vmem] * 5,
            out_specs=(vmem, vmem),
            scratch_shapes=[
                half(src_count, traces, width),
                half(dst_count, traces, width),
                half(src_count, traces, width),
                half(dst_count, traces, width),
                half(traces, width),
                half(traces, width),
                half(dst_count, traces, width),
                half(src_count, traces, width),
            ]
            + [on_src, on_dst, on_src, on_dst, on_dst, on_src, on_dst, on_src],
            compiler_params=pltpu.CompilerParams(
                collective_id=1, has_side_effects=True, vmem_limit_bytes=VMEM_BYTES
            ),
            name="exchange",
        )(ahead, behind, glow, glow_next, near)

    last_weights = (emission[2] * beta_end).astype(jnp.bfloat16)
    pred, carried = sweep(0, [alpha_rows], [last_weights])
    alpha_1, weights_2 = exchange(pred, carried, emission[0], emission[1])
    pred, carried, middle_terms = sweep(1, [alpha_1], [weights_2])
    alpha_2, weights_1 = exchange(pred, carried, emission[1], emission[0])
    pred, carried, end_terms = sweep(2, [alpha_2, alpha_rows], [weights_1, last_weights])

    mask_rows = block_mask.shape[0]
    all_state = (
        (unit_index[None, :] // per_piece) * col_count
        + jnp.arange(src_count, dtype=jnp.int32)[:, None] * piece
        + (unit_index[None, :] % per_piece) * unit
    )
    row_block = src_place * mask_rows + jnp.arange(mask_rows, dtype=jnp.int32)
    chosen = (all_state // BLK)[:, None, :] == row_block[None, :, None]
    norm = mask_rows * src_count * cols * dst_count / (STEPS * traces)
    alpha_end, beta_start, block_counts = pl.pallas_call(
        functools.partial(final_kernel, lines, piece, states, norm),
        out_shape=(
            f32(traces, col_count), f32(traces, row_count), f32(mask_rows, lanes),
        ),
        in_specs=[vmem] * 6,
        out_specs=(vmem,) * 3,
        scratch_shapes=[
            room(src_count, traces, piece),
            room(src_count, traces, piece),
            room(traces, piece),
            room(src_count, traces, piece),
            room(dst_count, traces, piece),
            room(dst_count, traces, piece),
            room(traces, piece),
            room(traces, piece),
            room(dst_count, traces, piece),
            room(2 + STEPS, traces, LANES),
            room(src_count, 2 + STEPS, traces, LANES),
            room(2 + STEPS, traces, LANES),
            room(dst_count, 2 + STEPS, traces, LANES),
            room(units, lanes),
            room(src_count, units, lanes),
        ]
        + [on_src, on_src, on_dst, on_dst, on_src, on_src, on_dst, on_dst, on_src, on_src]
        + [pltpu.SemaphoreType.DMA((2,)), on_src, on_src, on_dst, on_dst],
        compiler_params=pltpu.CompilerParams(
            collective_id=2, has_side_effects=True, vmem_limit_bytes=VMEM_BYTES
        ),
        name="final",
    )(pred, carried, emission[2], middle_terms, end_terms, chosen.astype(jnp.float32))
    return (alpha_end, beta_start, block_counts[:, :cols])


def solution(mesh):
    return jax.shard_map(
        local,
        mesh=mesh,
        in_specs=(
            P("src", None),
            P("dst", None),
            P("dst", None),
            P("dst", None),
            P("dst"),
            P("src", "dst"),
            P(),
            P(None, "src"),
            P(None, "dst"),
        ),
        out_specs=(P(None, "dst"), P(None, "src"), P("src", "dst")),
        check_vma=False,
    )
```

```python
import functools

import jax
import jax.numpy as jnp
from jax import lax
from jax.experimental import pallas as pl
from jax.experimental.pallas import tpu as pltpu
from jax.sharding import PartitionSpec as P

BLK = 512
STEPS = 3
LANES = 128
DEPTH = 8
very_negative = -1e30
GROUP = 4
HELD_BYTES = 40 * 1024 * 1024
TABLE_BYTES = 16 * 1024 * 1024
VMEM_BYTES = 16 * 1024 * 1024


def table_kernel(
    unit, cols, held, ids, count, src, dst, top, mass, near, far,
    buf_0, buf_1, scores_0, scores_1, best_0, best_1, sems,
):
    number = count[0]
    src = src.reshape(top.shape[1], src.shape[-1])
    chunk = min(128, unit)
    pieces = unit // chunk
    top[...] = jnp.full_like(top, very_negative)
    mass[...] = jnp.zeros_like(mass)

    def place(slot):
        entry = ids[slot]
        return lax.div(entry, cols), lax.rem(entry, cols)

    def score(slot, scores, best, c):
        i, j = place(slot)
        d = dst[pl.ds(pl.multiple_of(j * BLK, BLK), BLK), :]
        value = lax.dot_general(
            d, src[pl.ds(pl.multiple_of(i * unit + c * chunk, chunk), chunk), :],
            (((1,), (1,)), ((), ())), preferred_element_type=jnp.float32,
        )
        scores[:, c * chunk:(c + 1) * chunk] = value
        best[:, c * chunk:(c + 1) * chunk] = jnp.max(value, axis=0, keepdims=True)

    def phase(slot, scores, best, later, scores_next, best_next, put):
        sums = []
        for c in range(pieces):
            score(later, scores_next, best_next, c)
            span = slice(c * chunk, (c + 1) * chunk)
            risen = jnp.exp(scores[:, span] - best[:, span])
            put(span, risen.astype(jnp.bfloat16))
            sums.append(jnp.sum(risen, axis=0, keepdims=True))
        i, j = place(slot)
        rows = pl.ds(pl.multiple_of(i * unit, unit), unit)
        top[pl.ds(j, 1), rows] = best[...]
        mass[pl.ds(j, 1), rows] = jnp.concatenate(sums, axis=1)

    def run(low, high, out):
        for c in range(pieces):
            score(low, scores_0, best_0, c)

        def body(p, carry):
            even = low + 2 * p
            odd = jnp.minimum(even + 1, high - 1)
            after = jnp.minimum(even + 2, high - 1)
            with_even, with_odd = out(p, even, odd, high)
            with_even(lambda put: phase(even, scores_0, best_0, odd, scores_1, best_1, put))
            with_odd(lambda put: phase(odd, scores_1, best_1, after, scores_0, best_0, put))
            return carry

        lax.fori_loop(0, lax.div(high - low + 1, 2), body, 0)

    def keep(p, even, odd, high):
        def store(slot):
            def put(span, value):
                near[slot, :, span] = value

            return put

        return lambda go: go(store(even)), lambda go: go(store(odd))

    def copy(slot, buf, b):
        return pltpu.make_async_copy(buf, far.at[slot - held], sems.at[b])

    def send(p, even, odd, high):
        def through(slot, buf, b, live):
            def put(span, value):
                buf[:, span] = value

            def go(step):
                @pl.when(p > 0)
                def _():
                    copy(slot, buf, b).wait()

                step(put)

                @pl.when(live)
                def _():
                    copy(slot, buf, b).start()

            return go

        return through(even, buf_0, 0, even < high), through(odd, buf_1, 1, even + 1 < high)

    @pl.when(number > held)
    def _():
        run(held, number, send)

    @pl.when(number > 0)
    def _():
        run(0, jnp.minimum(number, held), keep)

    @pl.when(number > held)
    def _():
        copy(held, buf_0, 0).wait()

    @pl.when((number > held) & (lax.rem(number - held, 2) == 0))
    def _():
        copy(held, buf_1, 1).wait()


def sweep_kernel(unit, cols, held, traces, kind, ids, count, *refs):
    if kind == 2:
        alpha, early, factor, weight, last, near, far, pred, carried, terms, buf, sems = refs
    elif kind == 1:
        alpha, factor, weight, near, far, pred, carried, terms, buf, sems = refs
    else:
        alpha, factor, weight, near, far, pred, carried, buf, sems = refs
    number = count[0]
    pred[...] = jnp.zeros_like(pred)
    carried[...] = jnp.zeros_like(carried)
    if kind:
        terms[...] = jnp.zeros_like(terms)

    def copy(slot):
        b = lax.rem(slot - held, DEPTH)
        return pltpu.make_async_copy(far.at[slot - held], buf.at[b], sems.at[b])

    for p in range(DEPTH):

        @pl.when(held + p < number)
        def _():
            copy(held + p).start()

    def group(slots, high, tile):
        found = []
        for slot in slots:
            real = jnp.minimum(slot, high - 1)
            entry = ids[real]
            i = lax.div(entry, cols)
            j = lax.rem(entry, cols)
            rows = pl.ds(pl.multiple_of(i * unit, unit), unit)
            places = pl.ds(pl.multiple_of(j * BLK, BLK), BLK)
            share = factor[pl.ds(j, 1), rows] * jnp.where(slot < high, 1.0, 0.0)
            mix = (alpha[:, rows] * share).astype(jnp.bfloat16)
            block = tile(real)
            ahead = lax.dot_general(
                mix, block, (((1,), (1,)), ((), ())), preferred_element_type=jnp.float32
            )
            spread = jnp.dot(weight[:, places], block, preferred_element_type=jnp.float32)
            values = []
            if kind == 1:
                values.append(mix.astype(jnp.float32) * spread)
            elif kind == 2:
                first = (early[:, rows] * share).astype(jnp.bfloat16)
                values.append(first.astype(jnp.float32) * spread)
                values.append(last[:, places].astype(jnp.float32) * ahead)
            values = [jnp.sum(v, axis=1, keepdims=True) for v in values]
            found.append((i, j, rows, places, ahead, share * spread, values))
        for i, j, rows, places, ahead, behind, values in found:
            pred[:, places] += ahead
            carried[:, rows] += behind
            for t, value in enumerate(values):
                hit = lax.broadcasted_iota(jnp.int32, terms.shape[2:], 1) == j
                terms[t, i] += jnp.where(hit, value, 0.0)

    near_count = jnp.minimum(number, held)

    def near_body(g, carry):
        group([g * GROUP + u for u in range(GROUP)], near_count, lambda slot: near[slot])
        return carry

    lax.fori_loop(0, lax.div(near_count + GROUP - 1, GROUP), near_body, 0)

    def far_body(g, carry):
        slots = [held + g * GROUP + u for u in range(GROUP)]
        for slot in slots:

            @pl.when(slot < number)
            def _():
                copy(slot).wait()

        group(slots, number, lambda slot: buf[lax.rem(slot - held, DEPTH)])
        for slot in slots:

            @pl.when(slot + DEPTH < number)
            def _():
                copy(slot + DEPTH).start()

        return carry

    far_count = number - near_count
    lax.fori_loop(0, lax.div(far_count + GROUP - 1, GROUP), far_body, 0)


class Lines:
    def __init__(self, lines):
        self.lines = lines
        self.place = {name: lax.axis_index(name) for name in lines}

    def peer(self, name, k):
        return lax.rem(self.place[name] + k, self.lines[name])

    def origin(self, name, k):
        return lax.rem(self.place[name] + self.lines[name] - k, self.lines[name])

    def greet(self):
        barrier = pltpu.get_barrier_semaphore()
        for name in self.lines:
            for k in range(1, self.lines[name]):
                pl.semaphore_signal(
                    barrier, inc=1, device_id={name: self.peer(name, k)},
                    device_id_type=pl.DeviceIdType.MESH,
                )

    def gather_in(self, more=0):
        total = sum(self.lines.values()) - len(self.lines) + more
        pl.semaphore_wait(pltpu.get_barrier_semaphore(), total)

    def send(self, name, source, landing, send, recv):
        copies = []
        for k in range(1, self.lines[name]):
            copy = pltpu.make_async_remote_copy(
                src_ref=source(self.peer(name, k)),
                dst_ref=landing.at[k],
                send_sem=send.at[k],
                recv_sem=recv.at[k],
                device_id={name: self.peer(name, k)},
                device_id_type=pl.DeviceIdType.MESH,
            )
            copy.start()
            copies.append(copy)
        return copies


def gather_kernel(
    lines, group, piece, states, source, mask, looked, out_emb, log_norm, start,
    rows, masks, emission, moved, land_w, local_sems, alpha_sems, *sems,
):
    net = Lines(lines)
    net.greet()
    src, dst = lines["src"], lines["dst"]
    z, d = net.place["src"], net.place["dst"]
    chips = dst // 2
    sibling = d + 1 - 2 * lax.rem(d, 2)
    held = z * dst + d
    to_dst, to_src = lax.div(held, src), lax.rem(held, src)
    number = d * src + z
    from_src, from_dst = lax.div(number, dst), lax.rem(number, dst)
    away = (to_src != z) | (to_dst != d)
    barrier = pltpu.get_barrier_semaphore()
    mesh_ids = pl.DeviceIdType.MESH
    mine = start.at[:, pl.ds(pl.multiple_of(d * piece, piece), piece)]

    @pl.when(away)
    def _():
        for s, t in ((to_src, to_dst), (from_src, from_dst)):
            pl.semaphore_signal(
                barrier, inc=1, device_id={"src": s, "dst": t}, device_id_type=mesh_ids
            )
        net.gather_in(2)

    @pl.when(jnp.logical_not(away))
    def _():
        net.gather_in()

    def plane(value):
        return pl.ds(value * group, group)

    def pass_on(source_ref, target_ref, send, recv, device):
        copy = pltpu.make_async_remote_copy(
            src_ref=source_ref, dst_ref=target_ref, send_sem=send, recv_sem=recv,
            device_id=device, device_id_type=mesh_ids,
        )
        copy.start()
        return copy

    along = []
    for k in range(1, src):
        other = net.peer("src", k)
        along.append(
            pass_on(
                source.at[:, other, d], rows.at[plane(z), d],
                sems[0].at[k], sems[1].at[k], {"src": other},
            )
        )
    words = net.send("dst", lambda peer: looked, land_w, sems[2], sems[3])
    masks[z] = mask[...]
    marks = [
        pass_on(
            mask, masks.at[z], sems[4].at[k], sems[5].at[k], {"src": net.peer("src", k)}
        )
        for k in range(1, src)
    ]
    move = pltpu.make_async_remote_copy(
        src_ref=mine, dst_ref=moved, send_sem=alpha_sems.at[0], recv_sem=alpha_sems.at[1],
        device_id={"src": to_src, "dst": to_dst}, device_id_type=mesh_ids,
    )
    stay = pltpu.make_async_copy(mine, moved, alpha_sems.at[2])

    @pl.when(away)
    def _():
        move.start()

    @pl.when(jnp.logical_not(away))
    def _():
        stay.start()

    own = pltpu.make_async_copy(source.at[:, z], rows.at[plane(z)], local_sems)
    own.start()

    across, beside = [], []
    for k in range(1, src):
        along[k - 1].wait_recv()
        here = plane(net.origin("src", k))
        block = rows.at[here, d]
        for m in range(1, chips):
            across.append(
                pass_on(
                    block, block, sems[6].at[k, m], sems[7].at[k, m],
                    {"dst": lax.rem(d + 2 * m, dst)},
                )
            )
        beside.append(
            pass_on(block, block, sems[8].at[k, 0], sems[9].at[k, 0], {"dst": sibling})
        )
        if k == 1:
            total = looked[...].astype(jnp.float32)
            for w in range(1, dst):
                words[w - 1].wait_recv()
                total = total + land_w[w].astype(jnp.float32)
            total = total.astype(jnp.bfloat16)
            cols = out_emb.shape[0]
            width = min(cols, 1024)
            for c in range(0, cols, width):
                logits = lax.dot_general(
                    total, out_emb[c:c + width, :], (((1,), (1,)), ((), ())),
                    preferred_element_type=jnp.float32,
                )
                emission[:, c:c + width] = jnp.exp(logits - log_norm[:, c:c + width])
    for k in range(1, src):
        here = plane(net.origin("src", k))
        for m in range(1, chips):
            across[(k - 1) * (chips - 1) + m - 1].wait_recv()
            block = rows.at[here, lax.rem(d + dst - 2 * m, dst)]
            beside.append(
                pass_on(block, block, sems[8].at[k, m], sems[9].at[k, m], {"dst": sibling})
            )
    own.wait()
    for copy in marks:
        copy.wait_recv()

    @pl.when(away)
    def _():
        move.wait_recv()
        move.wait_send()

    @pl.when(jnp.logical_not(away))
    def _():
        stay.wait()

    for copy in beside:
        copy.wait_recv()
    for copies in (along, words, marks, across, beside):
        for copy in copies:
            copy.wait_send()


def stats_kernel(
    lines, piece, top, mass, alpha, near, factor, spread_alpha,
    parts, land, merged, land_2, land_a, *sems,
):
    net = Lines(lines)
    net.greet()
    count = lines["dst"]
    for p in range(count):
        rows = slice(p * piece, (p + 1) * piece)
        best = jnp.max(top[:, rows], axis=0, keepdims=True)
        total = jnp.sum(mass[:, rows] * jnp.exp(top[:, rows] - best), axis=0, keepdims=True)
        parts[p] = jnp.where(
            total > 0.0, best + jnp.log(jnp.maximum(total, 1e-37)), very_negative
        )
    net.gather_in()
    first = net.send("dst", lambda peer: parts.at[peer], land, sems[0], sems[1])
    sent = net.send("dst", lambda peer: alpha, land_a, sems[4], sems[5])
    land[0] = parts[net.place["dst"]]
    for copy in first:
        copy.wait_recv()
    best = land[0]
    for k in range(1, count):
        best = jnp.maximum(best, land[k])
    total = jnp.zeros_like(best)
    for k in range(count):
        total = total + jnp.exp(land[k] - best)
    merged[...] = best + jnp.log(total)
    second = net.send("dst", lambda peer: merged, land_2, sems[2], sems[3])

    def finish(k, level):
        rows = pl.ds(pl.multiple_of(net.origin("dst", k) * piece, piece), piece)
        factor[:, rows] = jnp.exp(top[:, rows] - level)

    finish(0, merged[...])
    for k in range(count):
        rows = pl.ds(pl.multiple_of(net.origin("dst", k) * piece, piece), piece)
        if k:
            sent[k - 1].wait_recv()
        spread_alpha[:, rows] = (alpha[...] if k == 0 else land_a[k]).astype(jnp.float32)
    for k in range(1, count):
        second[k - 1].wait_recv()
        finish(k, land_2[k])
    for copy in first + second + sent:
        copy.wait_send()


def exchange_kernel(
    lines, piece, states, pred, carried, glow, glow_next, near, alpha, weights,
    out_f, out_b, in_f, in_b, red_f, red_b, land_f, land_b, *sems,
):
    net = Lines(lines)
    net.greet()
    shape = (pred.shape[0], LANES)
    total_f = jnp.broadcast_to(
        jnp.sum(pred[...] * glow[...], axis=1, keepdims=True), shape
    ).astype(jnp.bfloat16)
    total_b = jnp.broadcast_to(
        jnp.sum(carried[...], axis=1, keepdims=True), shape
    ).astype(jnp.bfloat16)
    payload = {"src": (out_f, pred, total_f), "dst": (out_b, carried, total_b)}
    for name, (out, value, total) in payload.items():
        for p in range(lines[name]):
            out[p, :, :piece] = value[:, p * piece:(p + 1) * piece].astype(jnp.bfloat16)
            out[p, :, piece:] = total
    net.gather_in()
    landing = {"src": in_f, "dst": in_b}
    first = {}
    for n, name in enumerate(("src", "dst")):
        out = payload[name][0]
        first[name] = net.send(
            name, lambda peer, out=out: out.at[peer], landing[name], sems[n], sems[2 + n]
        )
    second = {}
    order = (("src", "dst", red_f, land_f), ("dst", "src", red_b, land_b))
    for n, (name, other, red, land) in enumerate(order):
        value = payload[name][0][net.place[name]].astype(jnp.float32)
        for k in range(1, lines[name]):
            first[name][k - 1].wait_recv()
            value = value + landing[name][k].astype(jnp.float32)
        part, total = value[:, :piece], value[:, piece:]
        if name == "src":
            start = pl.multiple_of(net.place["src"] * piece, piece)
            part = part * glow[:, pl.ds(start, piece)]
        red[:, :piece] = part.astype(jnp.bfloat16)
        red[:, piece:] = total.astype(jnp.bfloat16)
        second[other] = net.send(
            other, lambda peer, red=red: red, land, sems[4 + n], sems[6 + n]
        )
    for name, red, land in (("dst", red_f, land_f), ("src", red_b, land_b)):
        total = red[:, piece:piece + 1].astype(jnp.float32)
        for k in range(1, lines[name]):
            second[name][k - 1].wait_recv()
            total = total + land[k, :, piece:piece + 1].astype(jnp.float32)
        scale = states / total
        for k in range(lines[name]):
            part = red[:, :piece] if k == 0 else land[k, :, :piece]
            start = pl.multiple_of(net.origin(name, k) * piece, piece)
            part = part.astype(jnp.float32) * scale
            if name == "dst":
                alpha[:, pl.ds(start, piece)] = part
            else:
                part = part * glow_next[:, pl.ds(start, piece)]
                weights[:, pl.ds(start, piece)] = part.astype(jnp.bfloat16)
    for copies in (*first.values(), *second.values()):
        for copy in copies:
            copy.wait_send()


def final_kernel(
    lines, piece, states, norm, pred, carried, glow, mid_terms, end_terms, owner,
    alpha, beta, counts,
    out_f, in_f, red_f, land_f, out_b, in_b, red_b, natural, land_b,
    sums, in_s, red_s, land_s, mine, in_c, *sems,
):
    net = Lines(lines)
    net.greet()
    src, dst = lines["src"], lines["dst"]
    traces = pred.shape[0]
    shape = (traces, LANES)
    number = net.place["dst"] * src + net.place["src"]
    to_src, to_dst = lax.div(number, dst), lax.rem(number, dst)
    held = net.place["src"] * dst + net.place["dst"]
    from_dst, from_src = lax.div(held, src), lax.rem(held, src)
    away = (to_src != net.place["src"]) | (to_dst != net.place["dst"])
    barrier = pltpu.get_barrier_semaphore()

    @pl.when(away)
    def _():
        for s, d in ((to_src, to_dst), (from_src, from_dst)):
            pl.semaphore_signal(
                barrier, inc=1, device_id={"src": s, "dst": d},
                device_id_type=pl.DeviceIdType.MESH,
            )

    terms = [mid_terms[0], end_terms[0], end_terms[1]]
    rows = [jnp.sum(pred[...] * glow[...], axis=1, keepdims=True)]
    rows.append(jnp.sum(carried[...], axis=1, keepdims=True))
    for t in terms:
        rows.append(jnp.sum(jnp.sum(t, axis=0), axis=1, keepdims=True))
    for n, row in enumerate(rows):
        sums[n] = jnp.broadcast_to(row, shape)
    for p in range(src):
        out_f[p] = pred[:, p * piece:(p + 1) * piece]
    for p in range(dst):
        out_b[p] = carried[:, p * piece:(p + 1) * piece]

    @pl.when(away)
    def _():
        net.gather_in(2)

    @pl.when(jnp.logical_not(away))
    def _():
        net.gather_in()

    first_s = net.send("src", lambda peer: sums, in_s, sems[0], sems[1])
    first_b = net.send("dst", lambda peer: out_b.at[peer], in_b, sems[2], sems[3])
    first_f = net.send("src", lambda peer: out_f.at[peer], in_f, sems[4], sems[5])

    total = sums[...]
    for k in range(1, src):
        first_s[k - 1].wait_recv()
        total = total + in_s[k]
    red_s[...] = total
    second_s = net.send("dst", lambda peer: red_s, land_s, sems[6], sems[7])

    value = out_f[net.place["src"]]
    for k in range(1, src):
        first_f[k - 1].wait_recv()
        value = value + in_f[k]
    start = pl.multiple_of(net.place["src"] * piece, piece)
    red_f[...] = value * glow[:, pl.ds(start, piece)]
    second_f = net.send("src", lambda peer: red_f, land_f, sems[8], sems[9])

    value = out_b[net.place["dst"]]
    for k in range(1, dst):
        first_b[k - 1].wait_recv()
        value = value + in_b[k]
    red_b[...] = value
    move = pltpu.make_async_remote_copy(
        src_ref=red_b, dst_ref=natural, send_sem=sems[10].at[0], recv_sem=sems[10].at[1],
        device_id={"src": to_src, "dst": to_dst}, device_id_type=pl.DeviceIdType.MESH,
    )

    @pl.when(away)
    def _():
        move.start()

    total = red_s[...]
    for k in range(1, dst):
        second_s[k - 1].wait_recv()
        total = total + land_s[k]
    level = jnp.zeros(mine.shape, jnp.float32)
    for t in range(len(terms)):
        share = norm / total[2 + t]
        level = level + jnp.sum(terms[t] * share[None], axis=1)
    mine[...] = level
    third_c = net.send("src", lambda peer: mine, in_c, sems[11], sems[12])

    @pl.when(away)
    def _():
        move.wait_recv()

    @pl.when(jnp.logical_not(away))
    def _():
        natural[...] = red_b[...]

    third_b = net.send("dst", lambda peer: natural, land_b, sems[13], sems[14])

    scale = states / total[0][:, :1]
    for k in range(src):
        if k:
            second_f[k - 1].wait_recv()
        part = red_f[...] if k == 0 else land_f[k]
        begin = pl.multiple_of(net.origin("src", k) * piece, piece)
        alpha[:, pl.ds(begin, piece)] = part * scale
    value = jnp.zeros(counts.shape, jnp.float32)
    for k in range(src):
        if k:
            third_c[k - 1].wait_recv()
        value = value + jnp.dot(
            owner[net.origin("src", k)], mine[...] if k == 0 else in_c[k],
            precision=lax.Precision.HIGHEST, preferred_element_type=jnp.float32,
        )
    counts[...] = value
    scale = states / total[1][:, :1]
    for k in range(dst):
        if k:
            third_b[k - 1].wait_recv()
        part = natural[...] if k == 0 else land_b[k]
        begin = pl.multiple_of(net.origin("dst", k) * piece, piece)
        beta[:, pl.ds(begin, piece)] = part * scale

    @pl.when(away)
    def _():
        move.wait_send()

    for copies in (first_s, first_b, first_f, second_s, second_f, third_c, third_b):
        for copy in copies:
            copy.wait_send()


def local(
    src_emb, dst_emb, out_emb, word_table, log_norm, block_mask, tokens, alpha_start, beta_end
):
    row_count, emb_width = src_emb.shape
    col_count = dst_emb.shape[0]
    traces = alpha_start.shape[0]
    src_count = lax.axis_size("src")
    dst_count = lax.axis_size("dst")
    states = row_count * src_count
    group = dst_count // src_count
    piece = col_count // src_count
    unit = min(BLK, piece)
    units = row_count // unit
    cols = col_count // BLK
    places = units * cols
    src_place = lax.axis_index("src")
    dst_place = lax.axis_index("dst")
    smem = pl.BlockSpec(memory_space=pltpu.SMEM)
    vmem = pl.BlockSpec(memory_space=pltpu.VMEM)
    anywhere = pl.BlockSpec(memory_space=pl.ANY)
    hbm = pl.BlockSpec(memory_space=pltpu.HBM)
    lines = {"src": src_count, "dst": dst_count}
    on_src = pltpu.SemaphoreType.DMA((src_count,))
    on_dst = pltpu.SemaphoreType.DMA((dst_count,))
    on_chips = pltpu.SemaphoreType.DMA((src_count, dst_count // 2))

    def f32(*shape):
        return jax.ShapeDtypeStruct(shape, jnp.float32)

    def room(*shape, dtype=jnp.float32):
        return pltpu.VMEM(shape, dtype)

    half = functools.partial(room, dtype=jnp.bfloat16)

    vocab_slice = word_table.shape[0]
    local_ids = tokens.reshape(-1) - dst_place * vocab_slice
    onehot = (local_ids[:, None] == jnp.arange(vocab_slice, dtype=jnp.int32)[None, :]).astype(
        jnp.bfloat16
    )
    looked = jnp.dot(onehot, word_table, preferred_element_type=jnp.float32)
    share = piece // dst_count
    gathered, masks, emission, alpha_moved = pl.pallas_call(
        functools.partial(gather_kernel, lines, group, piece, states),
        out_shape=(
            half(dst_count, dst_count, share, emb_width),
            jax.ShapeDtypeStruct((src_count,) + block_mask.shape, jnp.int32),
            f32(STEPS * traces, col_count),
            f32(traces, piece),
        ),
        in_specs=[hbm, vmem, vmem, vmem, vmem, hbm],
        out_specs=(vmem,) * 4,
        scratch_shapes=[
            half(dst_count, STEPS * traces, emb_width),
            pltpu.SemaphoreType.DMA,
            pltpu.SemaphoreType.DMA((3,)),
        ]
        + [on_src, on_src, on_dst, on_dst, on_src, on_src]
        + [on_chips] * 4,
        compiler_params=pltpu.CompilerParams(
            collective_id=3, has_side_effects=True, vmem_limit_bytes=TABLE_BYTES
        ),
        name="gather",
    )(
        pltpu.with_memory_space_constraint(
            src_emb.reshape(group, src_count, dst_count, share, emb_width), pltpu.HBM
        ),
        block_mask, looked.astype(jnp.bfloat16), out_emb, log_norm[None, :],
        pltpu.with_memory_space_constraint(alpha_start, pltpu.HBM),
    )
    gathered = pltpu.with_memory_space_constraint(gathered, pltpu.VMEM)
    emission = emission.reshape(STEPS, traces, col_count)
    whole_mask = masks.reshape(src_count * block_mask.shape[0], cols)
    unit_index = jnp.arange(units, dtype=jnp.int32)
    per_piece = piece // unit
    unit_state = (
        (unit_index // per_piece) * col_count + src_place * piece + (unit_index % per_piece) * unit
    )
    unit_block = unit_state // BLK
    owner = unit_block[:, None] == jnp.arange(whole_mask.shape[0], dtype=jnp.int32)[None, :]
    mask = jnp.sum(jnp.where(owner[:, :, None], whole_mask[None], 0), axis=1)
    flat = (mask == 1).reshape(places)
    index = jnp.arange(places, dtype=jnp.int32)
    before = jnp.sum(
        jnp.where((index[None, :] < index[:, None]) & flat[None, :], 1, 0), axis=1
    )
    ids = jnp.sum(
        jnp.where((before[None, :] == index[:, None]) & flat[None, :], index[None, :], 0), axis=1
    ).astype(jnp.int32)
    number = jnp.sum(flat.astype(jnp.int32)).reshape(1)

    guess = places // 5 + 1
    held = min(places, HELD_BYTES // (BLK * unit * 2))
    params = pltpu.CompilerParams(vmem_limit_bytes=VMEM_BYTES)
    top, mass, near, far = pl.pallas_call(
        functools.partial(table_kernel, unit, cols, held),
        out_shape=(
            jax.ShapeDtypeStruct((cols, row_count), jnp.float32),
            jax.ShapeDtypeStruct((cols, row_count), jnp.float32),
            pltpu.VMEM((held, BLK, unit), jnp.bfloat16),
            jax.ShapeDtypeStruct((max(places - held, 1), BLK, unit), jnp.bfloat16),
        ),
        in_specs=[smem, smem, vmem, vmem],
        out_specs=(vmem, vmem, vmem, anywhere),
        scratch_shapes=[pltpu.VMEM((BLK, unit), jnp.bfloat16)] * 2
        + [pltpu.VMEM((BLK, unit), jnp.float32)] * 2
        + [pltpu.VMEM((1, unit), jnp.float32)] * 2
        + [pltpu.SemaphoreType.DMA((2,))],
        compiler_params=pltpu.CompilerParams(vmem_limit_bytes=TABLE_BYTES),
        cost_estimate=pl.CostEstimate(
            flops=guess * BLK * unit * emb_width * 2,
            bytes_accessed=guess * BLK * unit,
            transcendentals=guess * BLK * unit,
        ),
        name="table",
    )(ids, number, gathered, dst_emb)
    near = pltpu.with_memory_space_constraint(near, pltpu.VMEM)

    factor, alpha_rows = pl.pallas_call(
        functools.partial(stats_kernel, lines, piece),
        out_shape=(f32(cols, row_count), f32(traces, row_count)),
        in_specs=[vmem] * 4,
        out_specs=(vmem,) * 2,
        scratch_shapes=[
            room(dst_count, 1, piece),
            room(dst_count, 1, piece),
            room(1, piece),
            room(dst_count, 1, piece),
            half(dst_count, traces, piece),
        ]
        + [on_dst] * 6,
        compiler_params=pltpu.CompilerParams(
            collective_id=0, has_side_effects=True, vmem_limit_bytes=VMEM_BYTES
        ),
        name="stats",
    )(top, mass, alpha_moved.astype(jnp.bfloat16), near)

    lanes = -(-cols // LANES) * LANES

    def sweep(kind, alphas, weights):
        outs = [f32(traces, col_count), f32(traces, row_count)]
        if kind:
            outs.append(f32(kind, units, traces, lanes))
        return pl.pallas_call(
            functools.partial(sweep_kernel, unit, cols, held, traces, kind),
            out_shape=tuple(outs),
            in_specs=[smem, smem] + [vmem] * (len(alphas) + 2 + len(weights)) + [anywhere],
            out_specs=(vmem,) * len(outs),
            scratch_shapes=[
                pltpu.VMEM((DEPTH, BLK, unit), jnp.bfloat16),
                pltpu.SemaphoreType.DMA((DEPTH,)),
            ],
            compiler_params=params,
            cost_estimate=pl.CostEstimate(
                flops=guess * BLK * unit * traces * 4,
                bytes_accessed=guess * BLK * unit,
                transcendentals=0,
            ),
            name="sweep%d" % kind,
        )(ids, number, *alphas, factor, *weights, near, far)

    def exchange(ahead, behind, glow, glow_next):
        width = piece + LANES
        return pl.pallas_call(
            functools.partial(exchange_kernel, lines, piece, states),
            out_shape=(
                f32(traces, row_count),
                jax.ShapeDtypeStruct((traces, col_count), jnp.bfloat16),
            ),
            in_specs=[vmem] * 5,
            out_specs=(vmem, vmem),
            scratch_shapes=[
                half(src_count, traces, width),
                half(dst_count, traces, width),
                half(src_count, traces, width),
                half(dst_count, traces, width),
                half(traces, width),
                half(traces, width),
                half(dst_count, traces, width),
                half(src_count, traces, width),
            ]
            + [on_src, on_dst, on_src, on_dst, on_dst, on_src, on_dst, on_src],
            compiler_params=pltpu.CompilerParams(
                collective_id=1, has_side_effects=True, vmem_limit_bytes=VMEM_BYTES
            ),
            name="exchange",
        )(ahead, behind, glow, glow_next, near)

    last_weights = (emission[2] * beta_end).astype(jnp.bfloat16)
    pred, carried = sweep(0, [alpha_rows], [last_weights])
    alpha_1, weights_2 = exchange(pred, carried, emission[0], emission[1])
    pred, carried, middle_terms = sweep(1, [alpha_1], [weights_2])
    alpha_2, weights_1 = exchange(pred, carried, emission[1], emission[0])
    pred, carried, end_terms = sweep(2, [alpha_2, alpha_rows], [weights_1, last_weights])

    mask_rows = block_mask.shape[0]
    all_state = (
        (unit_index[None, :] // per_piece) * col_count
        + jnp.arange(src_count, dtype=jnp.int32)[:, None] * piece
        + (unit_index[None, :] % per_piece) * unit
    )
    row_block = src_place * mask_rows + jnp.arange(mask_rows, dtype=jnp.int32)
    chosen = (all_state // BLK)[:, None, :] == row_block[None, :, None]
    norm = mask_rows * src_count * cols * dst_count / (STEPS * traces)
    alpha_end, beta_start, block_counts = pl.pallas_call(
        functools.partial(final_kernel, lines, piece, states, norm),
        out_shape=(
            f32(traces, col_count), f32(traces, row_count), f32(mask_rows, lanes),
        ),
        in_specs=[vmem] * 6,
        out_specs=(vmem,) * 3,
        scratch_shapes=[
            room(src_count, traces, piece),
            room(src_count, traces, piece),
            room(traces, piece),
            room(src_count, traces, piece),
            room(dst_count, traces, piece),
            room(dst_count, traces, piece),
            room(traces, piece),
            room(traces, piece),
            room(dst_count, traces, piece),
            room(2 + STEPS, traces, LANES),
            room(src_count, 2 + STEPS, traces, LANES),
            room(2 + STEPS, traces, LANES),
            room(dst_count, 2 + STEPS, traces, LANES),
            room(units, lanes),
            room(src_count, units, lanes),
        ]
        + [on_src, on_src, on_dst, on_dst, on_src, on_src, on_dst, on_dst, on_src, on_src]
        + [pltpu.SemaphoreType.DMA((2,)), on_src, on_src, on_dst, on_dst],
        compiler_params=pltpu.CompilerParams(
            collective_id=2, has_side_effects=True, vmem_limit_bytes=VMEM_BYTES
        ),
        name="final",
    )(pred, carried, emission[2], middle_terms, end_terms, chosen.astype(jnp.float32))
    return (alpha_end, beta_start, block_counts[:, :cols])


def solution(mesh):
    return jax.shard_map(
        local,
        mesh=mesh,
        in_specs=(
            P("src", None),
            P("dst", None),
            P("dst", None),
            P("dst", None),
            P("dst"),
            P("src", "dst"),
            P(),
            P(None, "src"),
            P(None, "dst"),
        ),
        out_specs=(P(None, "dst"), P(None, "src"), P("src", "dst")),
        check_vma=False,
    )
```

```python
import functools

import jax
import jax.numpy as jnp
import numpy as np
from jax import lax
from jax.experimental import pallas as pl
from jax.experimental.pallas import tpu as pltpu
from jax.sharding import PartitionSpec as P

BLK = 512
STEPS = 3
LANES = 128
DEPTH = 8
very_negative = -1e30
GROUP = 4
HELD_BYTES = 48 * 1024 * 1024
TABLE_BYTES = 14 * 1024 * 1024
VMEM_BYTES = 14 * 1024 * 1024


def table_kernel(
    unit, cols, held, ids, count, src_far, dst_far, top, mass, near, far, src, dst, load_sems,
    buf_0, buf_1, scores_0, scores_1, best_0, best_1, sems,
):
    number = count[0]
    loads = fetch([(src_far, src), (dst_far, dst)], load_sems)
    src = src.reshape(top.shape[1], src.shape[-1])
    chunk = min(128, unit)
    pieces = unit // chunk
    top[...] = jnp.full_like(top, very_negative)
    mass[...] = jnp.zeros_like(mass)
    for copy in loads:
        copy.wait()

    def place(slot):
        entry = ids[slot]
        return lax.div(entry, cols), lax.rem(entry, cols)

    def score(slot, scores, best, c):
        i, j = place(slot)
        d = dst[pl.ds(pl.multiple_of(j * BLK, BLK), BLK), :]
        value = lax.dot_general(
            d, src[pl.ds(pl.multiple_of(i * unit + c * chunk, chunk), chunk), :],
            (((1,), (1,)), ((), ())), preferred_element_type=jnp.float32,
        )
        scores[:, c * chunk:(c + 1) * chunk] = value
        best[:, c * chunk:(c + 1) * chunk] = jnp.max(value, axis=0, keepdims=True)

    def phase(slot, scores, best, later, scores_next, best_next, put):
        sums = []
        for c in range(pieces):
            score(later, scores_next, best_next, c)
            span = slice(c * chunk, (c + 1) * chunk)
            risen = jnp.exp(scores[:, span] - best[:, span])
            put(span, risen.astype(jnp.bfloat16))
            sums.append(jnp.sum(risen, axis=0, keepdims=True))
        i, j = place(slot)
        rows = pl.ds(pl.multiple_of(i * unit, unit), unit)
        top[pl.ds(j, 1), rows] = best[...]
        mass[pl.ds(j, 1), rows] = jnp.concatenate(sums, axis=1)

    def run(low, high, out):
        for c in range(pieces):
            score(low, scores_0, best_0, c)

        def body(p, carry):
            even = low + 2 * p
            odd = jnp.minimum(even + 1, high - 1)
            after = jnp.minimum(even + 2, high - 1)
            with_even, with_odd = out(p, even, odd, high)
            with_even(lambda put: phase(even, scores_0, best_0, odd, scores_1, best_1, put))
            with_odd(lambda put: phase(odd, scores_1, best_1, after, scores_0, best_0, put))
            return carry

        lax.fori_loop(0, lax.div(high - low + 1, 2), body, 0)

    def keep(p, even, odd, high):
        def store(slot):
            def put(span, value):
                near[slot, :, span] = value

            return put

        return lambda go: go(store(even)), lambda go: go(store(odd))

    def copy(slot, buf, b):
        return pltpu.make_async_copy(buf, far.at[slot - held], sems.at[b])

    def send(p, even, odd, high):
        def through(slot, buf, b, live):
            def put(span, value):
                buf[:, span] = value

            def go(step):
                @pl.when(p > 0)
                def _():
                    copy(slot, buf, b).wait()

                step(put)

                @pl.when(live)
                def _():
                    copy(slot, buf, b).start()

            return go

        return through(even, buf_0, 0, even < high), through(odd, buf_1, 1, even + 1 < high)

    @pl.when(number > held)
    def _():
        run(held, number, send)

    @pl.when(number > 0)
    def _():
        run(0, jnp.minimum(number, held), keep)

    @pl.when(number > held)
    def _():
        copy(held, buf_0, 0).wait()

    @pl.when((number > held) & (lax.rem(number - held, 2) == 0))
    def _():
        copy(held, buf_1, 1).wait()


def sweep_kernel(unit, cols, held, traces, kind, ids, count, *refs):
    if kind == 2:
        alpha, early, factor, weight, last, near, far, pred, carried, terms, buf, sems = refs
    elif kind == 1:
        alpha, factor, weight, near, far, pred, carried, terms, buf, sems = refs
    else:
        alpha, factor, weight, near, far, pred, carried, buf, sems = refs
    number = count[0]
    pred[...] = jnp.zeros_like(pred)
    carried[...] = jnp.zeros_like(carried)
    if kind:
        terms[...] = jnp.zeros_like(terms)

    def copy(slot):
        b = lax.rem(slot - held, DEPTH)
        return pltpu.make_async_copy(far.at[slot - held], buf.at[b], sems.at[b])

    for p in range(DEPTH):

        @pl.when(held + p < number)
        def _():
            copy(held + p).start()

    def group(slots, high, tile):
        found = []
        for slot in slots:
            real = jnp.minimum(slot, high - 1)
            entry = ids[real]
            i = lax.div(entry, cols)
            j = lax.rem(entry, cols)
            rows = pl.ds(pl.multiple_of(i * unit, unit), unit)
            places = pl.ds(pl.multiple_of(j * BLK, BLK), BLK)
            share = factor[pl.ds(j, 1), rows] * jnp.where(slot < high, 1.0, 0.0)
            mix = (alpha[:, rows] * share).astype(jnp.bfloat16)
            block = tile(real)
            ahead = lax.dot_general(
                mix, block, (((1,), (1,)), ((), ())), preferred_element_type=jnp.float32
            )
            spread = jnp.dot(weight[:, places], block, preferred_element_type=jnp.float32)
            values = []
            if kind == 1:
                values.append(mix.astype(jnp.float32) * spread)
            elif kind == 2:
                first = (early[:, rows] * share).astype(jnp.bfloat16)
                values.append(first.astype(jnp.float32) * spread)
                values.append(last[:, places].astype(jnp.float32) * ahead)
            values = [jnp.sum(v, axis=1, keepdims=True) for v in values]
            found.append((i, j, rows, places, ahead, share * spread, values))
        for i, j, rows, places, ahead, behind, values in found:
            pred[:, places] += ahead
            carried[:, rows] += behind
            for t, value in enumerate(values):
                hit = lax.broadcasted_iota(jnp.int32, terms.shape[2:], 1) == j
                terms[t, i] += jnp.where(hit, value, 0.0)

    near_count = jnp.minimum(number, held)

    def near_body(g, carry):
        group([g * GROUP + u for u in range(GROUP)], near_count, lambda slot: near[slot])
        return carry

    lax.fori_loop(0, lax.div(near_count + GROUP - 1, GROUP), near_body, 0)

    def far_body(g, carry):
        slots = [held + g * GROUP + u for u in range(GROUP)]
        for slot in slots:

            @pl.when(slot < number)
            def _():
                copy(slot).wait()

        group(slots, number, lambda slot: buf[lax.rem(slot - held, DEPTH)])
        for slot in slots:

            @pl.when(slot + DEPTH < number)
            def _():
                copy(slot + DEPTH).start()

        return carry

    far_count = number - near_count
    lax.fori_loop(0, lax.div(far_count + GROUP - 1, GROUP), far_body, 0)


class Lines:
    def __init__(self, lines):
        self.lines = lines
        self.place = {name: lax.axis_index(name) for name in lines}

    def peer(self, name, k):
        return lax.rem(self.place[name] + k, self.lines[name])

    def origin(self, name, k):
        return lax.rem(self.place[name] + self.lines[name] - k, self.lines[name])

    def greet(self):
        barrier = pltpu.get_barrier_semaphore()
        for name in self.lines:
            for k in range(1, self.lines[name]):
                pl.semaphore_signal(
                    barrier, inc=1, device_id={name: self.peer(name, k)},
                    device_id_type=pl.DeviceIdType.MESH,
                )

    def gather_in(self, more=0):
        total = sum(self.lines.values()) - len(self.lines) + more
        pl.semaphore_wait(pltpu.get_barrier_semaphore(), total)

    def send(self, name, source, landing, send, recv):
        copies = []
        for k in range(1, self.lines[name]):
            copy = pltpu.make_async_remote_copy(
                src_ref=source(self.peer(name, k)),
                dst_ref=landing.at[k],
                send_sem=send.at[k],
                recv_sem=recv.at[k],
                device_id={name: self.peer(name, k)},
                device_id_type=pl.DeviceIdType.MESH,
            )
            copy.start()
            copies.append(copy)
        return copies


def fetch(pairs, sems):
    copies = [
        pltpu.make_async_copy(source, target, sems.at[n])
        for n, (source, target) in enumerate(pairs)
    ]
    for copy in copies:
        copy.start()
    return copies


def gather_kernel(
    lines, group, piece, source, mask, looked, out_far, norm_far, end_far, start,
    rows, masks, emission_far, last_far, moved, land_w, out_emb, log_norm, end, emission, last,
    local_sems, alpha_sems, load_sems, *sems,
):
    net = Lines(lines)
    net.greet()
    loads = fetch([(out_far, out_emb), (norm_far, log_norm), (end_far, end)], load_sems)
    src, dst = lines["src"], lines["dst"]
    z, d = net.place["src"], net.place["dst"]
    chips = dst // 2
    sibling = d + 1 - 2 * lax.rem(d, 2)
    held = z * dst + d
    to_dst, to_src = lax.div(held, src), lax.rem(held, src)
    number = d * src + z
    from_src, from_dst = lax.div(number, dst), lax.rem(number, dst)
    away = (to_src != z) | (to_dst != d)
    barrier = pltpu.get_barrier_semaphore()
    mesh_ids = pl.DeviceIdType.MESH
    mine = start.at[:, pl.ds(pl.multiple_of(d * piece, piece), piece)]

    @pl.when(away)
    def _():
        for s, t in ((to_src, to_dst), (from_src, from_dst)):
            pl.semaphore_signal(
                barrier, inc=1, device_id={"src": s, "dst": t}, device_id_type=mesh_ids
            )
        net.gather_in(2)

    @pl.when(jnp.logical_not(away))
    def _():
        net.gather_in()

    def plane(value):
        return pl.ds(value * group, group)

    def pass_on(source_ref, target_ref, send, recv, device):
        copy = pltpu.make_async_remote_copy(
            src_ref=source_ref, dst_ref=target_ref, send_sem=send, recv_sem=recv,
            device_id=device, device_id_type=mesh_ids,
        )
        copy.start()
        return copy

    along = []
    for k in range(1, src):
        other = net.peer("src", k)
        along.append(
            pass_on(
                source.at[:, other, d], rows.at[plane(z), d],
                sems[0].at[k], sems[1].at[k], {"src": other},
            )
        )
    words = net.send("dst", lambda peer: looked, land_w, sems[2], sems[3])
    masks[z] = mask[...]
    marks = [
        pass_on(
            mask, masks.at[z], sems[4].at[k], sems[5].at[k], {"src": net.peer("src", k)}
        )
        for k in range(1, src)
    ]
    move = pltpu.make_async_remote_copy(
        src_ref=mine, dst_ref=moved, send_sem=alpha_sems.at[0], recv_sem=alpha_sems.at[1],
        device_id={"src": to_src, "dst": to_dst}, device_id_type=mesh_ids,
    )
    stay = pltpu.make_async_copy(mine, moved, alpha_sems.at[2])

    @pl.when(away)
    def _():
        move.start()

    @pl.when(jnp.logical_not(away))
    def _():
        stay.start()

    own = pltpu.make_async_copy(source.at[:, z], rows.at[plane(z)], local_sems)
    own.start()

    across, beside = [], []
    for k in range(1, src):
        along[k - 1].wait_recv()
        here = plane(net.origin("src", k))
        block = rows.at[here, d]
        for m in range(1, chips):
            across.append(
                pass_on(
                    block, block, sems[6].at[k, m], sems[7].at[k, m],
                    {"dst": lax.rem(d + 2 * m, dst)},
                )
            )
        beside.append(
            pass_on(block, block, sems[8].at[k, 0], sems[9].at[k, 0], {"dst": sibling})
        )
        if k == 1:
            total = looked[...].astype(jnp.float32)
            for w in range(1, dst):
                words[w - 1].wait_recv()
                total = total + land_w[w].astype(jnp.float32)
            total = total.astype(jnp.bfloat16)
            for copy in loads:
                copy.wait()
            cols = out_emb.shape[0]
            width = min(cols, 1024)
            for c in range(0, cols, width):
                logits = lax.dot_general(
                    total, out_emb[c:c + width, :], (((1,), (1,)), ((), ())),
                    preferred_element_type=jnp.float32,
                )
                risen = jnp.exp(logits - log_norm[:, c:c + width])
                emission[:, c:c + width] = risen
                tail = risen[risen.shape[0] - end.shape[0]:]
                last[:, c:c + width] = (tail * end[:, c:c + width]).astype(jnp.bfloat16)
            stores = fetch([(emission, emission_far), (last, last_far)], load_sems)
    for k in range(1, src):
        here = plane(net.origin("src", k))
        for m in range(1, chips):
            across[(k - 1) * (chips - 1) + m - 1].wait_recv()
            block = rows.at[here, lax.rem(d + dst - 2 * m, dst)]
            beside.append(
                pass_on(block, block, sems[8].at[k, m], sems[9].at[k, m], {"dst": sibling})
            )
    own.wait()
    for copy in stores:
        copy.wait()
    for copy in marks:
        copy.wait_recv()

    @pl.when(away)
    def _():
        move.wait_recv()
        move.wait_send()

    @pl.when(jnp.logical_not(away))
    def _():
        stay.wait()

    for copy in beside:
        copy.wait_recv()
    for copies in (along, words, marks, across, beside):
        for copy in copies:
            copy.wait_send()


def stats_kernel(
    lines, piece, top, mass, alpha, near, factor, spread_alpha,
    parts, land, merged, land_2, own, land_a, *sems,
):
    net = Lines(lines)
    net.greet()
    count = lines["dst"]
    own[...] = alpha[...].astype(jnp.bfloat16)
    for p in range(count):
        rows = slice(p * piece, (p + 1) * piece)
        best = jnp.max(top[:, rows], axis=0, keepdims=True)
        total = jnp.sum(mass[:, rows] * jnp.exp(top[:, rows] - best), axis=0, keepdims=True)
        parts[p] = jnp.where(
            total > 0.0, best + jnp.log(jnp.maximum(total, 1e-37)), very_negative
        )
    net.gather_in()
    first = net.send("dst", lambda peer: parts.at[peer], land, sems[0], sems[1])
    sent = net.send("dst", lambda peer: own, land_a, sems[4], sems[5])
    land[0] = parts[net.place["dst"]]
    for copy in first:
        copy.wait_recv()
    best = land[0]
    for k in range(1, count):
        best = jnp.maximum(best, land[k])
    total = jnp.zeros_like(best)
    for k in range(count):
        total = total + jnp.exp(land[k] - best)
    merged[...] = best + jnp.log(total)
    second = net.send("dst", lambda peer: merged, land_2, sems[2], sems[3])

    def finish(k, level):
        rows = pl.ds(pl.multiple_of(net.origin("dst", k) * piece, piece), piece)
        factor[:, rows] = jnp.exp(top[:, rows] - level)

    finish(0, merged[...])
    for k in range(count):
        rows = pl.ds(pl.multiple_of(net.origin("dst", k) * piece, piece), piece)
        if k:
            sent[k - 1].wait_recv()
        spread_alpha[:, rows] = (own[...] if k == 0 else land_a[k]).astype(jnp.float32)
    for k in range(1, count):
        second[k - 1].wait_recv()
        finish(k, land_2[k])
    for copy in first + second + sent:
        copy.wait_send()


def exchange_kernel(
    lines, piece, states, step, later, pred_far, carried_far, emission, near, alpha, weights,
    pred, carried, glow, glow_next, load_sems,
    out_f, out_b, in_f, in_b, red_f, red_b, land_f, land_b, *sems,
):
    net = Lines(lines)
    traces = pred.shape[0]
    net.greet()
    loads = fetch(
        [
            (pred_far, pred),
            (emission.at[pl.ds(step * traces, traces)], glow),
            (carried_far, carried),
            (emission.at[pl.ds(later * traces, traces)], glow_next),
        ],
        load_sems,
    )
    for copy in loads:
        copy.wait()
    shape = (pred.shape[0], LANES)
    total_f = jnp.broadcast_to(
        jnp.sum(pred[...] * glow[...], axis=1, keepdims=True), shape
    ).astype(jnp.bfloat16)
    total_b = jnp.broadcast_to(
        jnp.sum(carried[...], axis=1, keepdims=True), shape
    ).astype(jnp.bfloat16)
    payload = {"src": (out_f, pred, total_f), "dst": (out_b, carried, total_b)}
    for name, (out, value, total) in payload.items():
        for p in range(lines[name]):
            out[p, :, :piece] = value[:, p * piece:(p + 1) * piece].astype(jnp.bfloat16)
            out[p, :, piece:] = total
    net.gather_in()
    landing = {"src": in_f, "dst": in_b}
    first = {}
    for n, name in enumerate(("src", "dst")):
        out = payload[name][0]
        first[name] = net.send(
            name, lambda peer, out=out: out.at[peer], landing[name], sems[n], sems[2 + n]
        )
    second = {}
    order = (("src", "dst", red_f, land_f), ("dst", "src", red_b, land_b))
    for n, (name, other, red, land) in enumerate(order):
        value = payload[name][0][net.place[name]].astype(jnp.float32)
        for k in range(1, lines[name]):
            first[name][k - 1].wait_recv()
            value = value + landing[name][k].astype(jnp.float32)
        part, total = value[:, :piece], value[:, piece:]
        if name == "src":
            start = pl.multiple_of(net.place["src"] * piece, piece)
            part = part * glow[:, pl.ds(start, piece)]
        red[:, :piece] = part.astype(jnp.bfloat16)
        red[:, piece:] = total.astype(jnp.bfloat16)
        second[other] = net.send(
            other, lambda peer, red=red: red, land, sems[4 + n], sems[6 + n]
        )
    for name, red, land in (("dst", red_f, land_f), ("src", red_b, land_b)):
        total = red[:, piece:piece + 1].astype(jnp.float32)
        for k in range(1, lines[name]):
            second[name][k - 1].wait_recv()
            total = total + land[k, :, piece:piece + 1].astype(jnp.float32)
        scale = states / total
        for k in range(lines[name]):
            part = red[:, :piece] if k == 0 else land[k, :, :piece]
            start = pl.multiple_of(net.origin(name, k) * piece, piece)
            part = part.astype(jnp.float32) * scale
            if name == "dst":
                alpha[:, pl.ds(start, piece)] = part
            else:
                part = part * glow_next[:, pl.ds(start, piece)]
                weights[:, pl.ds(start, piece)] = part.astype(jnp.bfloat16)
    for copies in (*first.values(), *second.values()):
        for copy in copies:
            copy.wait_send()


def final_kernel(
    lines, piece, states, norm, pred_far, carried_far, emission, mid_far, end_far, owner,
    alpha, beta, counts, pred, carried, glow, mid_terms, end_terms, load_sems,
    out_f, in_f, red_f, land_f, out_b, in_b, red_b, natural, land_b,
    sums, in_s, red_s, land_s, mine, in_c, *sems,
):
    net = Lines(lines)
    net.greet()
    src, dst = lines["src"], lines["dst"]
    traces = pred.shape[0]
    loads = fetch(
        [
            (carried_far, carried),
            (pred_far, pred),
            (emission.at[pl.ds((STEPS - 1) * traces, traces)], glow),
            (mid_far, mid_terms),
            (end_far, end_terms),
        ],
        load_sems,
    )
    shape = (traces, LANES)
    number = net.place["dst"] * src + net.place["src"]
    to_src, to_dst = lax.div(number, dst), lax.rem(number, dst)
    held = net.place["src"] * dst + net.place["dst"]
    from_dst, from_src = lax.div(held, src), lax.rem(held, src)
    away = (to_src != net.place["src"]) | (to_dst != net.place["dst"])
    barrier = pltpu.get_barrier_semaphore()

    @pl.when(away)
    def _():
        for s, d in ((to_src, to_dst), (from_src, from_dst)):
            pl.semaphore_signal(
                barrier, inc=1, device_id={"src": s, "dst": d},
                device_id_type=pl.DeviceIdType.MESH,
            )

    for copy in loads:
        copy.wait()
    terms = [mid_terms[0], end_terms[0], end_terms[1]]
    rows = [jnp.sum(pred[...] * glow[...], axis=1, keepdims=True)]
    rows.append(jnp.sum(carried[...], axis=1, keepdims=True))
    for t in terms:
        rows.append(jnp.sum(jnp.sum(t, axis=0), axis=1, keepdims=True))
    for n, row in enumerate(rows):
        sums[n] = jnp.broadcast_to(row, shape)
    for p in range(src):
        out_f[p] = pred[:, p * piece:(p + 1) * piece]
    for p in range(dst):
        out_b[p] = carried[:, p * piece:(p + 1) * piece]

    @pl.when(away)
    def _():
        net.gather_in(2)

    @pl.when(jnp.logical_not(away))
    def _():
        net.gather_in()

    first_s = net.send("src", lambda peer: sums, in_s, sems[0], sems[1])
    first_b = net.send("dst", lambda peer: out_b.at[peer], in_b, sems[2], sems[3])
    first_f = net.send("src", lambda peer: out_f.at[peer], in_f, sems[4], sems[5])

    total = sums[...]
    for k in range(1, src):
        first_s[k - 1].wait_recv()
        total = total + in_s[k]
    red_s[...] = total
    second_s = net.send("dst", lambda peer: red_s, land_s, sems[6], sems[7])

    value = out_f[net.place["src"]]
    for k in range(1, src):
        first_f[k - 1].wait_recv()
        value = value + in_f[k]
    start = pl.multiple_of(net.place["src"] * piece, piece)
    red_f[...] = value * glow[:, pl.ds(start, piece)]
    second_f = net.send("src", lambda peer: red_f, land_f, sems[8], sems[9])

    value = out_b[net.place["dst"]]
    for k in range(1, dst):
        first_b[k - 1].wait_recv()
        value = value + in_b[k]
    red_b[...] = value
    move = pltpu.make_async_remote_copy(
        src_ref=red_b, dst_ref=natural, send_sem=sems[10].at[0], recv_sem=sems[10].at[1],
        device_id={"src": to_src, "dst": to_dst}, device_id_type=pl.DeviceIdType.MESH,
    )

    @pl.when(away)
    def _():
        move.start()

    total = red_s[...]
    for k in range(1, dst):
        second_s[k - 1].wait_recv()
        total = total + land_s[k]
    level = jnp.zeros(mine.shape, jnp.float32)
    for t in range(len(terms)):
        share = norm / total[2 + t]
        level = level + jnp.sum(terms[t] * share[None], axis=1)
    mine[...] = level
    third_c = net.send("src", lambda peer: mine, in_c, sems[11], sems[12])

    @pl.when(away)
    def _():
        move.wait_recv()

    @pl.when(jnp.logical_not(away))
    def _():
        natural[...] = red_b[...]

    third_b = net.send("dst", lambda peer: natural, land_b, sems[13], sems[14])

    scale = states / total[0][:, :1]
    for k in range(src):
        if k:
            second_f[k - 1].wait_recv()
        part = red_f[...] if k == 0 else land_f[k]
        begin = pl.multiple_of(net.origin("src", k) * piece, piece)
        alpha[:, pl.ds(begin, piece)] = part * scale
    value = jnp.zeros(counts.shape, jnp.float32)
    blocks = counts.shape[0]
    wanted = net.place["src"] * blocks + lax.broadcasted_iota(
        jnp.int32, (blocks, owner.shape[2]), 0
    )
    for k in range(src):
        if k:
            third_c[k - 1].wait_recv()
        owned = (owner[net.origin("src", k)] == wanted).astype(jnp.float32)
        value = value + jnp.dot(
            owned, mine[...] if k == 0 else in_c[k],
            precision=lax.Precision.HIGHEST, preferred_element_type=jnp.float32,
        )
    counts[...] = value
    scale = states / total[1][:, :1]
    for k in range(dst):
        if k:
            third_b[k - 1].wait_recv()
        part = natural[...] if k == 0 else land_b[k]
        begin = pl.multiple_of(net.origin("dst", k) * piece, piece)
        beta[:, pl.ds(begin, piece)] = part * scale

    @pl.when(away)
    def _():
        move.wait_send()

    for copies in (first_s, first_b, first_f, second_s, second_f, third_c, third_b):
        for copy in copies:
            copy.wait_send()


def local(
    src_emb, dst_emb, out_emb, word_table, log_norm, block_mask, tokens, alpha_start, beta_end
):
    row_count, emb_width = src_emb.shape
    col_count = dst_emb.shape[0]
    traces = alpha_start.shape[0]
    src_count = lax.axis_size("src")
    dst_count = lax.axis_size("dst")
    states = row_count * src_count
    group = dst_count // src_count
    piece = col_count // src_count
    unit = min(BLK, piece)
    units = row_count // unit
    cols = col_count // BLK
    places = units * cols
    src_place = lax.axis_index("src")
    dst_place = lax.axis_index("dst")
    smem = pl.BlockSpec(memory_space=pltpu.SMEM)
    vmem = pl.BlockSpec(memory_space=pltpu.VMEM)
    anywhere = pl.BlockSpec(memory_space=pl.ANY)
    hbm = pl.BlockSpec(memory_space=pltpu.HBM)
    lines = {"src": src_count, "dst": dst_count}
    on_src = pltpu.SemaphoreType.DMA((src_count,))
    on_dst = pltpu.SemaphoreType.DMA((dst_count,))
    on_chips = pltpu.SemaphoreType.DMA((src_count, dst_count // 2))

    def f32(*shape):
        return jax.ShapeDtypeStruct(shape, jnp.float32)

    def bf16(*shape):
        return jax.ShapeDtypeStruct(shape, jnp.bfloat16)

    def room(*shape, dtype=jnp.float32):
        return pltpu.VMEM(shape, dtype)

    half = functools.partial(room, dtype=jnp.bfloat16)

    def outside(array):
        return pltpu.with_memory_space_constraint(array, pltpu.HBM)

    vocab_slice = word_table.shape[0]
    local_ids = tokens.reshape(-1) - dst_place * vocab_slice
    onehot = (local_ids[:, None] == jnp.arange(vocab_slice, dtype=jnp.int32)[None, :]).astype(
        jnp.bfloat16
    )
    looked = jnp.dot(onehot, word_table, preferred_element_type=jnp.float32)
    share = piece // dst_count
    gathered, masks, emission, last_weights, alpha_moved = pl.pallas_call(
        functools.partial(gather_kernel, lines, group, piece),
        out_shape=(
            pltpu.HBM((dst_count, dst_count, share, emb_width), jnp.bfloat16),
            jax.ShapeDtypeStruct((src_count,) + block_mask.shape, jnp.int32),
            pltpu.HBM((STEPS * traces, col_count), jnp.float32),
            pltpu.HBM((traces, col_count), jnp.bfloat16),
            pltpu.HBM((traces, piece), jnp.float32),
        ),
        in_specs=[hbm, vmem, vmem, hbm, hbm, hbm, hbm],
        out_specs=(hbm, vmem, hbm, hbm, hbm),
        scratch_shapes=[
            half(dst_count, STEPS * traces, emb_width),
            half(col_count, emb_width),
            room(1, col_count),
            room(traces, col_count),
            room(STEPS * traces, col_count),
            half(traces, col_count),
            pltpu.SemaphoreType.DMA,
            pltpu.SemaphoreType.DMA((3,)),
            pltpu.SemaphoreType.DMA((3,)),
        ]
        + [on_src, on_src, on_dst, on_dst, on_src, on_src]
        + [on_chips] * 4,
        compiler_params=pltpu.CompilerParams(
            collective_id=3, has_side_effects=True, vmem_limit_bytes=TABLE_BYTES
        ),
        name="gather",
    )(
        outside(src_emb.reshape(group, src_count, dst_count, share, emb_width)),
        block_mask, looked.astype(jnp.bfloat16), outside(out_emb),
        outside(log_norm[None, :]), outside(beta_end), outside(alpha_start),
    )
    whole_mask = masks.reshape(src_count * block_mask.shape[0], cols)
    unit_index = jnp.arange(units, dtype=jnp.int32)
    per_piece = piece // unit
    unit_state = (
        (unit_index // per_piece) * col_count + src_place * piece + (unit_index % per_piece) * unit
    )
    unit_block = unit_state // BLK
    owner = unit_block[:, None] == jnp.arange(whole_mask.shape[0], dtype=jnp.int32)[None, :]
    mask = jnp.sum(jnp.where(owner[:, :, None], whole_mask[None], 0), axis=1)
    flat = (mask == 1).reshape(places)
    index = jnp.arange(places, dtype=jnp.int32)
    before = jnp.sum(
        jnp.where((index[None, :] < index[:, None]) & flat[None, :], 1, 0), axis=1
    )
    ids = jnp.sum(
        jnp.where((before[None, :] == index[:, None]) & flat[None, :], index[None, :], 0), axis=1
    ).astype(jnp.int32)
    number = jnp.sum(flat.astype(jnp.int32)).reshape(1)

    guess = places // 5 + 1
    held = min(places, HELD_BYTES // (BLK * unit * 2))
    params = pltpu.CompilerParams(vmem_limit_bytes=VMEM_BYTES)
    top, mass, near, far = pl.pallas_call(
        functools.partial(table_kernel, unit, cols, held),
        out_shape=(
            f32(cols, row_count),
            f32(cols, row_count),
            half(held, BLK, unit),
            jax.ShapeDtypeStruct((max(places - held, 1), BLK, unit), jnp.bfloat16),
        ),
        in_specs=[smem, smem, hbm, hbm],
        out_specs=(vmem, vmem, vmem, anywhere),
        scratch_shapes=[
            half(dst_count, dst_count, share, emb_width),
            half(col_count, emb_width),
            pltpu.SemaphoreType.DMA((2,)),
        ]
        + [pltpu.VMEM((BLK, unit), jnp.bfloat16)] * 2
        + [pltpu.VMEM((BLK, unit), jnp.float32)] * 2
        + [pltpu.VMEM((1, unit), jnp.float32)] * 2
        + [pltpu.SemaphoreType.DMA((2,))],
        compiler_params=pltpu.CompilerParams(vmem_limit_bytes=TABLE_BYTES),
        cost_estimate=pl.CostEstimate(
            flops=guess * BLK * unit * emb_width * 2,
            bytes_accessed=guess * BLK * unit,
            transcendentals=guess * BLK * unit,
        ),
        name="table",
    )(ids, number, outside(gathered), outside(dst_emb))
    near = pltpu.with_memory_space_constraint(near, pltpu.VMEM)

    factor, alpha_rows = pl.pallas_call(
        functools.partial(stats_kernel, lines, piece),
        out_shape=(f32(cols, row_count), f32(traces, row_count)),
        in_specs=[vmem] * 4,
        out_specs=(vmem,) * 2,
        scratch_shapes=[
            room(dst_count, 1, piece),
            room(dst_count, 1, piece),
            room(1, piece),
            room(dst_count, 1, piece),
            half(traces, piece),
            half(dst_count, traces, piece),
        ]
        + [on_dst] * 6,
        compiler_params=pltpu.CompilerParams(
            collective_id=0, has_side_effects=True, vmem_limit_bytes=VMEM_BYTES
        ),
        name="stats",
    )(top, mass, alpha_moved, near)

    lanes = -(-cols // LANES) * LANES

    def sweep(kind, alphas, weights):
        outs = [f32(traces, col_count), f32(traces, row_count)]
        if kind:
            outs.append(f32(kind, units, traces, lanes))
        return pl.pallas_call(
            functools.partial(sweep_kernel, unit, cols, held, traces, kind),
            out_shape=tuple(outs),
            in_specs=[smem, smem] + [vmem] * (len(alphas) + 2 + len(weights)) + [anywhere],
            out_specs=(vmem,) * len(outs),
            scratch_shapes=[
                pltpu.VMEM((DEPTH, BLK, unit), jnp.bfloat16),
                pltpu.SemaphoreType.DMA((DEPTH,)),
            ],
            compiler_params=params,
            cost_estimate=pl.CostEstimate(
                flops=guess * BLK * unit * traces * 4,
                bytes_accessed=guess * BLK * unit,
                transcendentals=0,
            ),
            name="sweep%d" % kind,
        )(ids, number, *alphas, factor, *weights, near, far)

    def exchange(ahead, behind, step, later):
        width = piece + LANES
        return pl.pallas_call(
            functools.partial(exchange_kernel, lines, piece, states, step, later),
            out_shape=(f32(traces, row_count), bf16(traces, col_count)),
            in_specs=[hbm] * 3 + [vmem],
            out_specs=(vmem, vmem),
            scratch_shapes=[
                room(traces, col_count),
                room(traces, row_count),
                room(traces, col_count),
                room(traces, col_count),
                pltpu.SemaphoreType.DMA((4,)),
                half(src_count, traces, width),
                half(dst_count, traces, width),
                half(src_count, traces, width),
                half(dst_count, traces, width),
                half(traces, width),
                half(traces, width),
                half(dst_count, traces, width),
                half(src_count, traces, width),
            ]
            + [on_src, on_dst, on_src, on_dst, on_dst, on_src, on_dst, on_src],
            compiler_params=pltpu.CompilerParams(
                collective_id=1 + 3 * step, has_side_effects=True, vmem_limit_bytes=VMEM_BYTES
            ),
            name="exchange",
        )(outside(ahead), outside(behind), outside(emission), near)

    pred, carried = sweep(0, [alpha_rows], [last_weights])
    alpha_1, weights_2 = exchange(pred, carried, 0, 1)
    pred, carried, middle_terms = sweep(1, [alpha_1], [weights_2])
    alpha_2, weights_1 = exchange(pred, carried, 1, 0)
    pred, carried, end_terms = sweep(2, [alpha_2, alpha_rows], [weights_1, last_weights])

    mask_rows = block_mask.shape[0]
    index = np.arange(units)
    all_state = (index // per_piece * col_count + index % per_piece * unit)[None, :] + (
        np.arange(src_count)[:, None] * piece
    )
    unit_blocks = jnp.asarray((all_state // BLK)[:, None, :], jnp.int32)
    norm = mask_rows * src_count * cols * dst_count / (STEPS * traces)
    alpha_end, beta_start, block_counts = pl.pallas_call(
        functools.partial(final_kernel, lines, piece, states, norm),
        out_shape=(
            f32(traces, col_count), f32(traces, row_count), f32(mask_rows, lanes),
        ),
        in_specs=[hbm] * 5 + [vmem],
        out_specs=(vmem,) * 3,
        scratch_shapes=[
            room(traces, col_count),
            room(traces, row_count),
            room(traces, col_count),
            room(1, units, traces, lanes),
            room(2, units, traces, lanes),
            pltpu.SemaphoreType.DMA((5,)),
            room(src_count, traces, piece),
            room(src_count, traces, piece),
            room(traces, piece),
            room(src_count, traces, piece),
            room(dst_count, traces, piece),
            room(dst_count, traces, piece),
            room(traces, piece),
            room(traces, piece),
            room(dst_count, traces, piece),
            room(2 + STEPS, traces, LANES),
            room(src_count, 2 + STEPS, traces, LANES),
            room(2 + STEPS, traces, LANES),
            room(dst_count, 2 + STEPS, traces, LANES),
            room(units, lanes),
            room(src_count, units, lanes),
        ]
        + [on_src, on_src, on_dst, on_dst, on_src, on_src, on_dst, on_dst, on_src, on_src]
        + [pltpu.SemaphoreType.DMA((2,)), on_src, on_src, on_dst, on_dst],
        compiler_params=pltpu.CompilerParams(
            collective_id=2, has_side_effects=True, vmem_limit_bytes=VMEM_BYTES
        ),
        name="final",
    )(
        outside(pred), outside(carried), outside(emission), outside(middle_terms),
        outside(end_terms), unit_blocks,
    )
    return (alpha_end, beta_start, block_counts[:, :cols])


def solution(mesh):
    return jax.shard_map(
        local,
        mesh=mesh,
        in_specs=(
            P("src", None),
            P("dst", None),
            P("dst", None),
            P("dst", None),
            P("dst"),
            P("src", "dst"),
            P(),
            P(None, "src"),
            P(None, "dst"),
        ),
        out_specs=(P(None, "dst"), P(None, "src"), P("src", "dst")),
        check_vma=False,
    )
```

```python
import functools

import jax
import jax.numpy as jnp
import numpy as np
from jax import lax
from jax.experimental import pallas as pl
from jax.experimental.pallas import tpu as pltpu
from jax.sharding import PartitionSpec as P

BLK = 512
STEPS = 3
LANES = 128
DEPTH = 8
very_negative = -1e30
GROUP = 4
HELD_BYTES = 48 * 1024 * 1024
TABLE_BYTES = 14 * 1024 * 1024
VMEM_BYTES = 14 * 1024 * 1024


def table_kernel(
    unit, cols, held, ids, count, src_far, dst_far, top, mass, near, far, src, dst, load_sems,
    buf_0, buf_1, scores_0, scores_1, best_0, best_1, sems,
):
    number = count[0]
    loads = fetch([(src_far, src), (dst_far, dst)], load_sems)
    src = src.reshape(top.shape[1], src.shape[-1])
    chunk = min(128, unit)
    pieces = unit // chunk
    top[...] = jnp.full_like(top, very_negative)
    mass[...] = jnp.zeros_like(mass)
    for copy in loads:
        copy.wait()

    def place(slot):
        entry = ids[slot]
        return lax.div(entry, cols), lax.rem(entry, cols)

    def score(slot, scores, best, c):
        i, j = place(slot)
        d = dst[pl.ds(pl.multiple_of(j * BLK, BLK), BLK), :]
        value = lax.dot_general(
            d, src[pl.ds(pl.multiple_of(i * unit + c * chunk, chunk), chunk), :],
            (((1,), (1,)), ((), ())), preferred_element_type=jnp.float32,
        )
        scores[:, c * chunk:(c + 1) * chunk] = value
        best[:, c * chunk:(c + 1) * chunk] = jnp.max(value, axis=0, keepdims=True)

    def phase(slot, scores, best, later, scores_next, best_next, put):
        sums = []
        for c in range(pieces):
            score(later, scores_next, best_next, c)
            span = slice(c * chunk, (c + 1) * chunk)
            risen = jnp.exp(scores[:, span] - best[:, span])
            put(span, risen.astype(jnp.bfloat16))
            sums.append(jnp.sum(risen, axis=0, keepdims=True))
        i, j = place(slot)
        rows = pl.ds(pl.multiple_of(i * unit, unit), unit)
        top[pl.ds(j, 1), rows] = best[...]
        mass[pl.ds(j, 1), rows] = jnp.concatenate(sums, axis=1)

    def run(low, high, out):
        for c in range(pieces):
            score(low, scores_0, best_0, c)

        def body(p, carry):
            even = low + 2 * p
            odd = jnp.minimum(even + 1, high - 1)
            after = jnp.minimum(even + 2, high - 1)
            with_even, with_odd = out(p, even, odd, high)
            with_even(lambda put: phase(even, scores_0, best_0, odd, scores_1, best_1, put))
            with_odd(lambda put: phase(odd, scores_1, best_1, after, scores_0, best_0, put))
            return carry

        lax.fori_loop(0, lax.div(high - low + 1, 2), body, 0)

    def keep(p, even, odd, high):
        def store(slot):
            def put(span, value):
                near[slot, :, span] = value

            return put

        return lambda go: go(store(even)), lambda go: go(store(odd))

    def copy(slot, buf, b):
        return pltpu.make_async_copy(buf, far.at[slot - held], sems.at[b])

    def send(p, even, odd, high):
        def through(slot, buf, b, live):
            def put(span, value):
                buf[:, span] = value

            def go(step):
                @pl.when(p > 0)
                def _():
                    copy(slot, buf, b).wait()

                step(put)

                @pl.when(live)
                def _():
                    copy(slot, buf, b).start()

            return go

        return through(even, buf_0, 0, even < high), through(odd, buf_1, 1, even + 1 < high)

    @pl.when(number > held)
    def _():
        run(held, number, send)

    @pl.when(number > 0)
    def _():
        run(0, jnp.minimum(number, held), keep)

    @pl.when(number > held)
    def _():
        copy(held, buf_0, 0).wait()

    @pl.when((number > held) & (lax.rem(number - held, 2) == 0))
    def _():
        copy(held, buf_1, 1).wait()


def sweep_kernel(unit, cols, held, traces, kind, ids, count, *refs):
    if kind == 2:
        alpha, early, factor, weight, last, near, far, pred, carried, terms, buf, sems = refs
    elif kind == 1:
        alpha, factor, weight, near, far, pred, carried, terms, buf, sems = refs
    else:
        alpha, factor, weight, near, far, pred, carried, buf, sems = refs
    number = count[0]
    pred[...] = jnp.zeros_like(pred)
    carried[...] = jnp.zeros_like(carried)
    if kind:
        terms[...] = jnp.zeros_like(terms)

    def copy(slot):
        b = lax.rem(slot - held, DEPTH)
        return pltpu.make_async_copy(far.at[slot - held], buf.at[b], sems.at[b])

    for p in range(DEPTH):

        @pl.when(held + p < number)
        def _():
            copy(held + p).start()

    def group(slots, high, tile):
        found = []
        for slot in slots:
            real = jnp.minimum(slot, high - 1)
            entry = ids[real]
            i = lax.div(entry, cols)
            j = lax.rem(entry, cols)
            rows = pl.ds(pl.multiple_of(i * unit, unit), unit)
            places = pl.ds(pl.multiple_of(j * BLK, BLK), BLK)
            share = factor[pl.ds(j, 1), rows] * jnp.where(slot < high, 1.0, 0.0)
            mix = (alpha[:, rows] * share).astype(jnp.bfloat16)
            block = tile(real)
            ahead = lax.dot_general(
                mix, block, (((1,), (1,)), ((), ())), preferred_element_type=jnp.float32
            )
            spread = jnp.dot(weight[:, places], block, preferred_element_type=jnp.float32)
            values = []
            if kind == 1:
                values.append(mix.astype(jnp.float32) * spread)
            elif kind == 2:
                first = (early[:, rows] * share).astype(jnp.bfloat16)
                values.append(first.astype(jnp.float32) * spread)
                values.append(last[:, places].astype(jnp.float32) * ahead)
            values = [jnp.sum(v, axis=1, keepdims=True) for v in values]
            found.append((i, j, rows, places, ahead, share * spread, values))
        for i, j, rows, places, ahead, behind, values in found:
            pred[:, places] += ahead
            carried[:, rows] += behind
            for t, value in enumerate(values):
                hit = lax.broadcasted_iota(jnp.int32, terms.shape[2:], 1) == j
                terms[t, i] += jnp.where(hit, value, 0.0)

    near_count = jnp.minimum(number, held)

    def near_body(g, carry):
        group([g * GROUP + u for u in range(GROUP)], near_count, lambda slot: near[slot])
        return carry

    lax.fori_loop(0, lax.div(near_count + GROUP - 1, GROUP), near_body, 0)

    def far_body(g, carry):
        slots = [held + g * GROUP + u for u in range(GROUP)]
        for slot in slots:

            @pl.when(slot < number)
            def _():
                copy(slot).wait()

        group(slots, number, lambda slot: buf[lax.rem(slot - held, DEPTH)])
        for slot in slots:

            @pl.when(slot + DEPTH < number)
            def _():
                copy(slot + DEPTH).start()

        return carry

    far_count = number - near_count
    lax.fori_loop(0, lax.div(far_count + GROUP - 1, GROUP), far_body, 0)


class Lines:
    def __init__(self, lines):
        self.lines = lines
        self.place = {name: lax.axis_index(name) for name in lines}

    def peer(self, name, k):
        return lax.rem(self.place[name] + k, self.lines[name])

    def origin(self, name, k):
        return lax.rem(self.place[name] + self.lines[name] - k, self.lines[name])

    def greet(self):
        barrier = pltpu.get_barrier_semaphore()
        for name in self.lines:
            for k in range(1, self.lines[name]):
                pl.semaphore_signal(
                    barrier, inc=1, device_id={name: self.peer(name, k)},
                    device_id_type=pl.DeviceIdType.MESH,
                )

    def gather_in(self, more=0):
        total = sum(self.lines.values()) - len(self.lines) + more
        pl.semaphore_wait(pltpu.get_barrier_semaphore(), total)

    def send(self, name, source, landing, send, recv):
        copies = []
        for k in range(1, self.lines[name]):
            copy = pltpu.make_async_remote_copy(
                src_ref=source(self.peer(name, k)),
                dst_ref=landing.at[k],
                send_sem=send.at[k],
                recv_sem=recv.at[k],
                device_id={name: self.peer(name, k)},
                device_id_type=pl.DeviceIdType.MESH,
            )
            copy.start()
            copies.append(copy)
        return copies


def fetch(pairs, sems):
    copies = [
        pltpu.make_async_copy(source, target, sems.at[n])
        for n, (source, target) in enumerate(pairs)
    ]
    for copy in copies:
        copy.start()
    return copies


def gather_kernel(
    lines, group, piece, source, mask, looked, out_far, norm_far, end_far, start,
    rows_far, masks, emission_far, last_far, moved, rows, land_w, out_emb, log_norm, end, emission, last,
    local_sems, alpha_sems, load_sems, *sems,
):
    net = Lines(lines)
    net.greet()
    loads = fetch([(out_far, out_emb), (norm_far, log_norm), (end_far, end)], load_sems)
    src, dst = lines["src"], lines["dst"]
    z, d = net.place["src"], net.place["dst"]
    chips = dst // 2
    sibling = d + 1 - 2 * lax.rem(d, 2)
    held = z * dst + d
    to_dst, to_src = lax.div(held, src), lax.rem(held, src)
    number = d * src + z
    from_src, from_dst = lax.div(number, dst), lax.rem(number, dst)
    away = (to_src != z) | (to_dst != d)
    barrier = pltpu.get_barrier_semaphore()
    mesh_ids = pl.DeviceIdType.MESH
    mine = start.at[:, pl.ds(pl.multiple_of(d * piece, piece), piece)]

    @pl.when(away)
    def _():
        for s, t in ((to_src, to_dst), (from_src, from_dst)):
            pl.semaphore_signal(
                barrier, inc=1, device_id={"src": s, "dst": t}, device_id_type=mesh_ids
            )
        net.gather_in(2)

    @pl.when(jnp.logical_not(away))
    def _():
        net.gather_in()

    def plane(value):
        return pl.ds(value * group, group)

    def pass_on(source_ref, target_ref, send, recv, device):
        copy = pltpu.make_async_remote_copy(
            src_ref=source_ref, dst_ref=target_ref, send_sem=send, recv_sem=recv,
            device_id=device, device_id_type=mesh_ids,
        )
        copy.start()
        return copy

    order = sorted(range(1, src), key=lambda k: min(k, src - k))
    along = []

    def next_round():
        k = order[len(along)]
        other = net.peer("src", k)
        along.append(
            pass_on(
                source.at[:, other, d], rows.at[plane(z), d],
                sems[0].at[k], sems[1].at[k], {"src": other},
            )
        )

    next_round()
    words = net.send("dst", lambda peer: looked, land_w, sems[2], sems[3])
    masks[z] = mask[...]
    marks = [
        pass_on(
            mask, masks.at[z], sems[4].at[k], sems[5].at[k], {"src": net.peer("src", k)}
        )
        for k in range(1, src)
    ]
    move = pltpu.make_async_remote_copy(
        src_ref=mine, dst_ref=moved, send_sem=alpha_sems.at[0], recv_sem=alpha_sems.at[1],
        device_id={"src": to_src, "dst": to_dst}, device_id_type=mesh_ids,
    )
    stay = pltpu.make_async_copy(mine, moved, alpha_sems.at[2])

    @pl.when(away)
    def _():
        move.start()

    @pl.when(jnp.logical_not(away))
    def _():
        stay.start()

    own = pltpu.make_async_copy(source.at[:, z], rows_far.at[plane(z)], local_sems.at[0])
    own.start()

    across, beside = [], []
    for n, k in enumerate(order):
        along[n].wait_recv()
        if n + 1 < len(order):
            next_round()
        here = plane(net.origin("src", k))
        block = rows.at[here, d]
        for m in range(1, chips):
            across.append(
                pass_on(
                    block, block, sems[6].at[k, m], sems[7].at[k, m],
                    {"dst": lax.rem(d + 2 * m, dst)},
                )
            )
        beside.append(
            pass_on(block, block, sems[8].at[k, 0], sems[9].at[k, 0], {"dst": sibling})
        )
        if n == 0:
            total = looked[...].astype(jnp.float32)
            for w in range(1, dst):
                words[w - 1].wait_recv()
                total = total + land_w[w].astype(jnp.float32)
            total = total.astype(jnp.bfloat16)
            for copy in loads:
                copy.wait()
            cols = out_emb.shape[0]
            width = min(cols, 1024)
            for c in range(0, cols, width):
                logits = lax.dot_general(
                    total, out_emb[c:c + width, :], (((1,), (1,)), ((), ())),
                    preferred_element_type=jnp.float32,
                )
                risen = jnp.exp(logits - log_norm[:, c:c + width])
                emission[:, c:c + width] = risen
                tail = risen[risen.shape[0] - end.shape[0]:]
                last[:, c:c + width] = (tail * end[:, c:c + width]).astype(jnp.bfloat16)
            stores = fetch([(emission, emission_far), (last, last_far)], load_sems)
    for n, k in enumerate(order):
        here = plane(net.origin("src", k))
        for m in range(1, chips):
            across[n * (chips - 1) + m - 1].wait_recv()
            block = rows.at[here, lax.rem(d + dst - 2 * m, dst)]
            beside.append(
                pass_on(block, block, sems[8].at[k, m], sems[9].at[k, m], {"dst": sibling})
            )
    out = [own]
    for n, k in enumerate(order):
        here = plane(net.origin("src", k))
        beside[n].wait_recv()
        first = len(order) + n * (chips - 1)
        for copy in beside[first:first + chips - 1]:
            copy.wait_recv()
        copy = pltpu.make_async_copy(rows.at[here], rows_far.at[here], local_sems.at[n + 1])
        copy.start()
        out.append(copy)
    for copy in stores:
        copy.wait()
    for copy in marks:
        copy.wait_recv()

    @pl.when(away)
    def _():
        move.wait_recv()
        move.wait_send()

    @pl.when(jnp.logical_not(away))
    def _():
        stay.wait()

    for copy in out:
        copy.wait()
    for copies in (along, words, marks, across, beside):
        for copy in copies:
            copy.wait_send()


def stats_kernel(
    lines, piece, top, mass, alpha, near, factor, spread_alpha,
    parts, land, merged, land_2, own, land_a, *sems,
):
    net = Lines(lines)
    net.greet()
    count = lines["dst"]
    own[...] = alpha[...].astype(jnp.bfloat16)
    for p in range(count):
        rows = slice(p * piece, (p + 1) * piece)
        best = jnp.max(top[:, rows], axis=0, keepdims=True)
        total = jnp.sum(mass[:, rows] * jnp.exp(top[:, rows] - best), axis=0, keepdims=True)
        parts[p] = jnp.where(
            total > 0.0, best + jnp.log(jnp.maximum(total, 1e-37)), very_negative
        )
    net.gather_in()
    first = net.send("dst", lambda peer: parts.at[peer], land, sems[0], sems[1])
    sent = net.send("dst", lambda peer: own, land_a, sems[4], sems[5])
    land[0] = parts[net.place["dst"]]
    for copy in first:
        copy.wait_recv()
    best = land[0]
    for k in range(1, count):
        best = jnp.maximum(best, land[k])
    total = jnp.zeros_like(best)
    for k in range(count):
        total = total + jnp.exp(land[k] - best)
    merged[...] = best + jnp.log(total)
    second = net.send("dst", lambda peer: merged, land_2, sems[2], sems[3])

    def finish(k, level):
        rows = pl.ds(pl.multiple_of(net.origin("dst", k) * piece, piece), piece)
        factor[:, rows] = jnp.exp(top[:, rows] - level)

    finish(0, merged[...])
    for k in range(count):
        rows = pl.ds(pl.multiple_of(net.origin("dst", k) * piece, piece), piece)
        if k:
            sent[k - 1].wait_recv()
        spread_alpha[:, rows] = (own[...] if k == 0 else land_a[k]).astype(jnp.float32)
    for k in range(1, count):
        second[k - 1].wait_recv()
        finish(k, land_2[k])
    for copy in first + second + sent:
        copy.wait_send()


def exchange_kernel(
    lines, piece, states, step, later, pred_far, carried_far, emission, near, alpha, weights,
    pred, carried, glow, glow_next, load_sems,
    out_f, out_b, in_f, in_b, red_f, red_b, land_f, land_b, *sems,
):
    net = Lines(lines)
    traces = pred.shape[0]
    net.greet()
    loads = fetch(
        [
            (pred_far, pred),
            (emission.at[pl.ds(step * traces, traces)], glow),
            (carried_far, carried),
            (emission.at[pl.ds(later * traces, traces)], glow_next),
        ],
        load_sems,
    )
    for copy in loads:
        copy.wait()
    shape = (pred.shape[0], LANES)
    total_f = jnp.broadcast_to(
        jnp.sum(pred[...] * glow[...], axis=1, keepdims=True), shape
    ).astype(jnp.bfloat16)
    total_b = jnp.broadcast_to(
        jnp.sum(carried[...], axis=1, keepdims=True), shape
    ).astype(jnp.bfloat16)
    payload = {"src": (out_f, pred, total_f), "dst": (out_b, carried, total_b)}
    for name, (out, value, total) in payload.items():
        for p in range(lines[name]):
            out[p, :, :piece] = value[:, p * piece:(p + 1) * piece].astype(jnp.bfloat16)
            out[p, :, piece:] = total
    net.gather_in()
    landing = {"src": in_f, "dst": in_b}
    first = {}
    for n, name in enumerate(("src", "dst")):
        out = payload[name][0]
        first[name] = net.send(
            name, lambda peer, out=out: out.at[peer], landing[name], sems[n], sems[2 + n]
        )
    second = {}
    order = (("src", "dst", red_f, land_f), ("dst", "src", red_b, land_b))
    for n, (name, other, red, land) in enumerate(order):
        value = payload[name][0][net.place[name]].astype(jnp.float32)
        for k in range(1, lines[name]):
            first[name][k - 1].wait_recv()
            value = value + landing[name][k].astype(jnp.float32)
        part, total = value[:, :piece], value[:, piece:]
        if name == "src":
            start = pl.multiple_of(net.place["src"] * piece, piece)
            part = part * glow[:, pl.ds(start, piece)]
        red[:, :piece] = part.astype(jnp.bfloat16)
        red[:, piece:] = total.astype(jnp.bfloat16)
        second[other] = net.send(
            other, lambda peer, red=red: red, land, sems[4 + n], sems[6 + n]
        )
    for name, red, land in (("dst", red_f, land_f), ("src", red_b, land_b)):
        total = red[:, piece:piece + 1].astype(jnp.float32)
        for k in range(1, lines[name]):
            second[name][k - 1].wait_recv()
            total = total + land[k, :, piece:piece + 1].astype(jnp.float32)
        scale = states / total
        for k in range(lines[name]):
            part = red[:, :piece] if k == 0 else land[k, :, :piece]
            start = pl.multiple_of(net.origin(name, k) * piece, piece)
            part = part.astype(jnp.float32) * scale
            if name == "dst":
                alpha[:, pl.ds(start, piece)] = part
            else:
                part = part * glow_next[:, pl.ds(start, piece)]
                weights[:, pl.ds(start, piece)] = part.astype(jnp.bfloat16)
    for copies in (*first.values(), *second.values()):
        for copy in copies:
            copy.wait_send()


def final_kernel(
    lines, piece, states, norm, pred_far, carried_far, emission, mid_far, end_far, owner,
    alpha, beta, counts, pred, carried, glow, mid_terms, end_terms, load_sems,
    out_f, in_f, red_f, land_f, out_b, in_b, red_b, natural, land_b,
    sums, in_s, red_s, land_s, mine, in_c, *sems,
):
    net = Lines(lines)
    net.greet()
    src, dst = lines["src"], lines["dst"]
    traces = pred.shape[0]
    loads = fetch(
        [
            (carried_far, carried),
            (pred_far, pred),
            (emission.at[pl.ds((STEPS - 1) * traces, traces)], glow),
            (mid_far, mid_terms),
            (end_far, end_terms),
        ],
        load_sems,
    )
    shape = (traces, LANES)
    number = net.place["dst"] * src + net.place["src"]
    to_src, to_dst = lax.div(number, dst), lax.rem(number, dst)
    held = net.place["src"] * dst + net.place["dst"]
    from_dst, from_src = lax.div(held, src), lax.rem(held, src)
    away = (to_src != net.place["src"]) | (to_dst != net.place["dst"])
    barrier = pltpu.get_barrier_semaphore()

    @pl.when(away)
    def _():
        for s, d in ((to_src, to_dst), (from_src, from_dst)):
            pl.semaphore_signal(
                barrier, inc=1, device_id={"src": s, "dst": d},
                device_id_type=pl.DeviceIdType.MESH,
            )

    for copy in loads:
        copy.wait()
    terms = [mid_terms[0], end_terms[0], end_terms[1]]
    rows = [jnp.sum(pred[...] * glow[...], axis=1, keepdims=True)]
    rows.append(jnp.sum(carried[...], axis=1, keepdims=True))
    for t in terms:
        rows.append(jnp.sum(jnp.sum(t, axis=0), axis=1, keepdims=True))
    for n, row in enumerate(rows):
        sums[n] = jnp.broadcast_to(row, shape)
    for p in range(src):
        out_f[p] = pred[:, p * piece:(p + 1) * piece]
    for p in range(dst):
        out_b[p] = carried[:, p * piece:(p + 1) * piece]

    @pl.when(away)
    def _():
        net.gather_in(2)

    @pl.when(jnp.logical_not(away))
    def _():
        net.gather_in()

    first_s = net.send("src", lambda peer: sums, in_s, sems[0], sems[1])
    first_b = net.send("dst", lambda peer: out_b.at[peer], in_b, sems[2], sems[3])
    first_f = net.send("src", lambda peer: out_f.at[peer], in_f, sems[4], sems[5])

    total = sums[...]
    for k in range(1, src):
        first_s[k - 1].wait_recv()
        total = total + in_s[k]
    red_s[...] = total
    second_s = net.send("dst", lambda peer: red_s, land_s, sems[6], sems[7])

    value = out_b[net.place["dst"]]
    for k in range(1, dst):
        first_b[k - 1].wait_recv()
        value = value + in_b[k]
    red_b[...] = value
    move = pltpu.make_async_remote_copy(
        src_ref=red_b, dst_ref=natural, send_sem=sems[10].at[0], recv_sem=sems[10].at[1],
        device_id={"src": to_src, "dst": to_dst}, device_id_type=pl.DeviceIdType.MESH,
    )

    @pl.when(away)
    def _():
        move.start()

    value = out_f[net.place["src"]]
    for k in range(1, src):
        first_f[k - 1].wait_recv()
        value = value + in_f[k]
    start = pl.multiple_of(net.place["src"] * piece, piece)
    red_f[...] = value * glow[:, pl.ds(start, piece)]
    total = red_s[...]
    for k in range(1, dst):
        second_s[k - 1].wait_recv()
        total = total + land_s[k]
    level = jnp.zeros(mine.shape, jnp.float32)
    for t in range(len(terms)):
        share = norm / total[2 + t]
        level = level + jnp.sum(terms[t] * share[None], axis=1)
    mine[...] = level
    third_c = net.send("src", lambda peer: mine, in_c, sems[11], sems[12])

    @pl.when(away)
    def _():
        move.wait_recv()

    @pl.when(jnp.logical_not(away))
    def _():
        natural[...] = red_b[...]

    third_b = net.send("dst", lambda peer: natural, land_b, sems[13], sems[14])
    second_f = net.send("src", lambda peer: red_f, land_f, sems[8], sems[9])

    scale = states / total[0][:, :1]
    for k in range(src):
        if k:
            second_f[k - 1].wait_recv()
        part = red_f[...] if k == 0 else land_f[k]
        begin = pl.multiple_of(net.origin("src", k) * piece, piece)
        alpha[:, pl.ds(begin, piece)] = part * scale
    value = jnp.zeros(counts.shape, jnp.float32)
    blocks = counts.shape[0]
    wanted = net.place["src"] * blocks + lax.broadcasted_iota(
        jnp.int32, (blocks, owner.shape[2]), 0
    )
    for k in range(src):
        if k:
            third_c[k - 1].wait_recv()
        owned = (owner[net.origin("src", k)] == wanted).astype(jnp.float32)
        value = value + jnp.dot(
            owned, mine[...] if k == 0 else in_c[k],
            precision=lax.Precision.HIGHEST, preferred_element_type=jnp.float32,
        )
    counts[...] = value
    scale = states / total[1][:, :1]
    for k in range(dst):
        if k:
            third_b[k - 1].wait_recv()
        part = natural[...] if k == 0 else land_b[k]
        begin = pl.multiple_of(net.origin("dst", k) * piece, piece)
        beta[:, pl.ds(begin, piece)] = part * scale

    @pl.when(away)
    def _():
        move.wait_send()

    for copies in (first_s, first_b, first_f, second_s, second_f, third_c, third_b):
        for copy in copies:
            copy.wait_send()


def local(
    src_emb, dst_emb, out_emb, word_table, log_norm, block_mask, tokens, alpha_start, beta_end
):
    row_count, emb_width = src_emb.shape
    col_count = dst_emb.shape[0]
    traces = alpha_start.shape[0]
    src_count = lax.axis_size("src")
    dst_count = lax.axis_size("dst")
    states = row_count * src_count
    group = dst_count // src_count
    piece = col_count // src_count
    unit = min(BLK, piece)
    units = row_count // unit
    cols = col_count // BLK
    places = units * cols
    src_place = lax.axis_index("src")
    dst_place = lax.axis_index("dst")
    smem = pl.BlockSpec(memory_space=pltpu.SMEM)
    vmem = pl.BlockSpec(memory_space=pltpu.VMEM)
    anywhere = pl.BlockSpec(memory_space=pl.ANY)
    hbm = pl.BlockSpec(memory_space=pltpu.HBM)
    lines = {"src": src_count, "dst": dst_count}
    on_src = pltpu.SemaphoreType.DMA((src_count,))
    on_dst = pltpu.SemaphoreType.DMA((dst_count,))
    on_chips = pltpu.SemaphoreType.DMA((src_count, dst_count // 2))

    def f32(*shape):
        return jax.ShapeDtypeStruct(shape, jnp.float32)

    def bf16(*shape):
        return jax.ShapeDtypeStruct(shape, jnp.bfloat16)

    def room(*shape, dtype=jnp.float32):
        return pltpu.VMEM(shape, dtype)

    half = functools.partial(room, dtype=jnp.bfloat16)

    def outside(array):
        return pltpu.with_memory_space_constraint(array, pltpu.HBM)

    vocab_slice = word_table.shape[0]
    local_ids = tokens.reshape(-1) - dst_place * vocab_slice
    onehot = (local_ids[:, None] == jnp.arange(vocab_slice, dtype=jnp.int32)[None, :]).astype(
        jnp.bfloat16
    )
    looked = jnp.dot(onehot, word_table, preferred_element_type=jnp.float32)
    share = piece // dst_count
    gathered, masks, emission, last_weights, alpha_moved = pl.pallas_call(
        functools.partial(gather_kernel, lines, group, piece),
        out_shape=(
            pltpu.HBM((dst_count, dst_count, share, emb_width), jnp.bfloat16),
            jax.ShapeDtypeStruct((src_count,) + block_mask.shape, jnp.int32),
            pltpu.HBM((STEPS * traces, col_count), jnp.float32),
            pltpu.HBM((traces, col_count), jnp.bfloat16),
            pltpu.HBM((traces, piece), jnp.float32),
        ),
        in_specs=[hbm, vmem, vmem, hbm, hbm, hbm, hbm],
        out_specs=(hbm, vmem, hbm, hbm, hbm),
        scratch_shapes=[
            half(dst_count, dst_count, share, emb_width),
            half(dst_count, STEPS * traces, emb_width),
            half(col_count, emb_width),
            room(1, col_count),
            room(traces, col_count),
            room(STEPS * traces, col_count),
            half(traces, col_count),
            on_src,
            pltpu.SemaphoreType.DMA((3,)),
            pltpu.SemaphoreType.DMA((3,)),
        ]
        + [on_src, on_src, on_dst, on_dst, on_src, on_src]
        + [on_chips] * 4,
        compiler_params=pltpu.CompilerParams(
            collective_id=3, has_side_effects=True, vmem_limit_bytes=TABLE_BYTES
        ),
        name="gather",
    )(
        outside(src_emb.reshape(group, src_count, dst_count, share, emb_width)),
        block_mask, looked.astype(jnp.bfloat16), outside(out_emb),
        outside(log_norm[None, :]), outside(beta_end), outside(alpha_start),
    )
    whole_mask = masks.reshape(src_count * block_mask.shape[0], cols)
    unit_index = jnp.arange(units, dtype=jnp.int32)
    per_piece = piece // unit
    unit_state = (
        (unit_index // per_piece) * col_count + src_place * piece + (unit_index % per_piece) * unit
    )
    unit_block = unit_state // BLK
    owner = unit_block[:, None] == jnp.arange(whole_mask.shape[0], dtype=jnp.int32)[None, :]
    mask = jnp.sum(jnp.where(owner[:, :, None], whole_mask[None], 0), axis=1)
    flat = (mask == 1).reshape(places)
    index = jnp.arange(places, dtype=jnp.int32)
    before = jnp.sum(
        jnp.where((index[None, :] < index[:, None]) & flat[None, :], 1, 0), axis=1
    )
    ids = jnp.sum(
        jnp.where((before[None, :] == index[:, None]) & flat[None, :], index[None, :], 0), axis=1
    ).astype(jnp.int32)
    number = jnp.sum(flat.astype(jnp.int32)).reshape(1)

    guess = places // 5 + 1
    held = min(places, HELD_BYTES // (BLK * unit * 2))
    params = pltpu.CompilerParams(vmem_limit_bytes=VMEM_BYTES)
    top, mass, near, far = pl.pallas_call(
        functools.partial(table_kernel, unit, cols, held),
        out_shape=(
            f32(cols, row_count),
            f32(cols, row_count),
            half(held, BLK, unit),
            jax.ShapeDtypeStruct((max(places - held, 1), BLK, unit), jnp.bfloat16),
        ),
        in_specs=[smem, smem, hbm, hbm],
        out_specs=(vmem, vmem, vmem, anywhere),
        scratch_shapes=[
            half(dst_count, dst_count, share, emb_width),
            half(col_count, emb_width),
            pltpu.SemaphoreType.DMA((2,)),
        ]
        + [pltpu.VMEM((BLK, unit), jnp.bfloat16)] * 2
        + [pltpu.VMEM((BLK, unit), jnp.float32)] * 2
        + [pltpu.VMEM((1, unit), jnp.float32)] * 2
        + [pltpu.SemaphoreType.DMA((2,))],
        compiler_params=pltpu.CompilerParams(vmem_limit_bytes=TABLE_BYTES),
        cost_estimate=pl.CostEstimate(
            flops=guess * BLK * unit * emb_width * 2,
            bytes_accessed=guess * BLK * unit,
            transcendentals=guess * BLK * unit,
        ),
        name="table",
    )(ids, number, outside(gathered), outside(dst_emb))
    near = pltpu.with_memory_space_constraint(near, pltpu.VMEM)

    factor, alpha_rows = pl.pallas_call(
        functools.partial(stats_kernel, lines, piece),
        out_shape=(f32(cols, row_count), f32(traces, row_count)),
        in_specs=[vmem] * 4,
        out_specs=(vmem,) * 2,
        scratch_shapes=[
            room(dst_count, 1, piece),
            room(dst_count, 1, piece),
            room(1, piece),
            room(dst_count, 1, piece),
            half(traces, piece),
            half(dst_count, traces, piece),
        ]
        + [on_dst] * 6,
        compiler_params=pltpu.CompilerParams(
            collective_id=0, has_side_effects=True, vmem_limit_bytes=VMEM_BYTES
        ),
        name="stats",
    )(top, mass, alpha_moved, near)

    lanes = -(-cols // LANES) * LANES

    def sweep(kind, alphas, weights):
        outs = [f32(traces, col_count), f32(traces, row_count)]
        if kind:
            outs.append(f32(kind, units, traces, lanes))
        return pl.pallas_call(
            functools.partial(sweep_kernel, unit, cols, held, traces, kind),
            out_shape=tuple(outs),
            in_specs=[smem, smem] + [vmem] * (len(alphas) + 2 + len(weights)) + [anywhere],
            out_specs=(vmem,) * len(outs),
            scratch_shapes=[
                pltpu.VMEM((DEPTH, BLK, unit), jnp.bfloat16),
                pltpu.SemaphoreType.DMA((DEPTH,)),
            ],
            compiler_params=params,
            cost_estimate=pl.CostEstimate(
                flops=guess * BLK * unit * traces * 4,
                bytes_accessed=guess * BLK * unit,
                transcendentals=0,
            ),
            name="sweep%d" % kind,
        )(ids, number, *alphas, factor, *weights, near, far)

    def exchange(ahead, behind, step, later):
        width = piece + LANES
        return pl.pallas_call(
            functools.partial(exchange_kernel, lines, piece, states, step, later),
            out_shape=(f32(traces, row_count), bf16(traces, col_count)),
            in_specs=[hbm] * 3 + [vmem],
            out_specs=(vmem, vmem),
            scratch_shapes=[
                room(traces, col_count),
                room(traces, row_count),
                room(traces, col_count),
                room(traces, col_count),
                pltpu.SemaphoreType.DMA((4,)),
                half(src_count, traces, width),
                half(dst_count, traces, width),
                half(src_count, traces, width),
                half(dst_count, traces, width),
                half(traces, width),
                half(traces, width),
                half(dst_count, traces, width),
                half(src_count, traces, width),
            ]
            + [on_src, on_dst, on_src, on_dst, on_dst, on_src, on_dst, on_src],
            compiler_params=pltpu.CompilerParams(
                collective_id=1 + 3 * step, has_side_effects=True, vmem_limit_bytes=VMEM_BYTES
            ),
            name="exchange",
        )(outside(ahead), outside(behind), outside(emission), near)

    pred, carried = sweep(0, [alpha_rows], [last_weights])
    alpha_1, weights_2 = exchange(pred, carried, 0, 1)
    pred, carried, middle_terms = sweep(1, [alpha_1], [weights_2])
    alpha_2, weights_1 = exchange(pred, carried, 1, 0)
    pred, carried, end_terms = sweep(2, [alpha_2, alpha_rows], [weights_1, last_weights])

    mask_rows = block_mask.shape[0]
    index = np.arange(units)
    all_state = (index // per_piece * col_count + index % per_piece * unit)[None, :] + (
        np.arange(src_count)[:, None] * piece
    )
    unit_blocks = jnp.asarray((all_state // BLK)[:, None, :], jnp.int32)
    norm = mask_rows * src_count * cols * dst_count / (STEPS * traces)
    alpha_end, beta_start, block_counts = pl.pallas_call(
        functools.partial(final_kernel, lines, piece, states, norm),
        out_shape=(
            f32(traces, col_count), f32(traces, row_count), f32(mask_rows, lanes),
        ),
        in_specs=[hbm] * 5 + [vmem],
        out_specs=(vmem,) * 3,
        scratch_shapes=[
            room(traces, col_count),
            room(traces, row_count),
            room(traces, col_count),
            room(1, units, traces, lanes),
            room(2, units, traces, lanes),
            pltpu.SemaphoreType.DMA((5,)),
            room(src_count, traces, piece),
            room(src_count, traces, piece),
            room(traces, piece),
            room(src_count, traces, piece),
            room(dst_count, traces, piece),
            room(dst_count, traces, piece),
            room(traces, piece),
            room(traces, piece),
            room(dst_count, traces, piece),
            room(2 + STEPS, traces, LANES),
            room(src_count, 2 + STEPS, traces, LANES),
            room(2 + STEPS, traces, LANES),
            room(dst_count, 2 + STEPS, traces, LANES),
            room(units, lanes),
            room(src_count, units, lanes),
        ]
        + [on_src, on_src, on_dst, on_dst, on_src, on_src, on_dst, on_dst, on_src, on_src]
        + [pltpu.SemaphoreType.DMA((2,)), on_src, on_src, on_dst, on_dst],
        compiler_params=pltpu.CompilerParams(
            collective_id=2, has_side_effects=True, vmem_limit_bytes=VMEM_BYTES
        ),
        name="final",
    )(
        outside(pred), outside(carried), outside(emission), outside(middle_terms),
        outside(end_terms), unit_blocks,
    )
    return (alpha_end, beta_start, block_counts[:, :cols])


def solution(mesh):
    return jax.shard_map(
        local,
        mesh=mesh,
        in_specs=(
            P("src", None),
            P("dst", None),
            P("dst", None),
            P("dst", None),
            P("dst"),
            P("src", "dst"),
            P(),
            P(None, "src"),
            P(None, "dst"),
        ),
        out_specs=(P(None, "dst"), P(None, "src"), P("src", "dst")),
        check_vma=False,
    )
```

```python
import functools

import jax
import jax.numpy as jnp
import numpy as np
from jax import lax
from jax.experimental import pallas as pl
from jax.experimental.pallas import tpu as pltpu
from jax.sharding import PartitionSpec as P

BLK = 512
STEPS = 3
LANES = 128
DEPTH = 8
very_negative = -1e30
GROUP = 4
HELD_BYTES = 48 * 1024 * 1024
TABLE_BYTES = 14 * 1024 * 1024
VMEM_BYTES = 14 * 1024 * 1024


def table_kernel(
    unit, cols, held, ids, count, src_far, dst_far, top, mass, near, far, src, dst, load_sems,
    buf_0, buf_1, scores_0, scores_1, best_0, best_1, sems,
):
    number = count[0]
    loads = fetch([(src_far, src), (dst_far, dst)], load_sems)
    src = src.reshape(top.shape[1], src.shape[-1])
    chunk = min(128, unit)
    pieces = unit // chunk
    top[...] = jnp.full_like(top, very_negative)
    mass[...] = jnp.zeros_like(mass)
    for copy in loads:
        copy.wait()

    def place(slot):
        entry = ids[slot]
        return lax.div(entry, cols), lax.rem(entry, cols)

    def score(slot, scores, best, c):
        i, j = place(slot)
        d = dst[pl.ds(pl.multiple_of(j * BLK, BLK), BLK), :]
        value = lax.dot_general(
            d, src[pl.ds(pl.multiple_of(i * unit + c * chunk, chunk), chunk), :],
            (((1,), (1,)), ((), ())), preferred_element_type=jnp.float32,
        )
        scores[:, c * chunk:(c + 1) * chunk] = value
        best[:, c * chunk:(c + 1) * chunk] = jnp.max(value, axis=0, keepdims=True)

    def phase(slot, scores, best, later, scores_next, best_next, put):
        sums = []
        for c in range(pieces):
            score(later, scores_next, best_next, c)
            span = slice(c * chunk, (c + 1) * chunk)
            risen = jnp.exp(scores[:, span] - best[:, span])
            put(span, risen.astype(jnp.bfloat16))
            sums.append(jnp.sum(risen, axis=0, keepdims=True))
        i, j = place(slot)
        rows = pl.ds(pl.multiple_of(i * unit, unit), unit)
        top[pl.ds(j, 1), rows] = best[...]
        mass[pl.ds(j, 1), rows] = jnp.concatenate(sums, axis=1)

    def run(low, high, out):
        for c in range(pieces):
            score(low, scores_0, best_0, c)

        def body(p, carry):
            even = low + 2 * p
            odd = jnp.minimum(even + 1, high - 1)
            after = jnp.minimum(even + 2, high - 1)
            with_even, with_odd = out(p, even, odd, high)
            with_even(lambda put: phase(even, scores_0, best_0, odd, scores_1, best_1, put))
            with_odd(lambda put: phase(odd, scores_1, best_1, after, scores_0, best_0, put))
            return carry

        lax.fori_loop(0, lax.div(high - low + 1, 2), body, 0)

    def keep(p, even, odd, high):
        def store(slot):
            def put(span, value):
                near[slot, :, span] = value

            return put

        return lambda go: go(store(even)), lambda go: go(store(odd))

    def copy(slot, buf, b):
        return pltpu.make_async_copy(buf, far.at[slot - held], sems.at[b])

    def send(p, even, odd, high):
        def through(slot, buf, b, live):
            def put(span, value):
                buf[:, span] = value

            def go(step):
                @pl.when(p > 0)
                def _():
                    copy(slot, buf, b).wait()

                step(put)

                @pl.when(live)
                def _():
                    copy(slot, buf, b).start()

            return go

        return through(even, buf_0, 0, even < high), through(odd, buf_1, 1, even + 1 < high)

    @pl.when(number > held)
    def _():
        run(held, number, send)

    @pl.when(number > 0)
    def _():
        run(0, jnp.minimum(number, held), keep)

    @pl.when(number > held)
    def _():
        copy(held, buf_0, 0).wait()

    @pl.when((number > held) & (lax.rem(number - held, 2) == 0))
    def _():
        copy(held, buf_1, 1).wait()


def sweep_kernel(unit, cols, held, traces, kind, ids, count, *refs):
    if kind == 2:
        alpha, early, factor, weight, last, near, far, pred, carried, terms, buf, sems = refs
    elif kind == 1:
        alpha, factor, weight, near, far, pred, carried, terms, buf, sems = refs
    else:
        alpha, factor, weight, near, far, pred, carried, buf, sems = refs
    number = count[0]
    pred[...] = jnp.zeros_like(pred)
    carried[...] = jnp.zeros_like(carried)
    if kind:
        terms[...] = jnp.zeros_like(terms)

    def copy(slot):
        b = lax.rem(slot - held, DEPTH)
        return pltpu.make_async_copy(far.at[slot - held], buf.at[b], sems.at[b])

    for p in range(DEPTH):

        @pl.when(held + p < number)
        def _():
            copy(held + p).start()

    def group(slots, high, tile):
        found = []
        for slot in slots:
            real = jnp.minimum(slot, high - 1)
            entry = ids[real]
            i = lax.div(entry, cols)
            j = lax.rem(entry, cols)
            rows = pl.ds(pl.multiple_of(i * unit, unit), unit)
            places = pl.ds(pl.multiple_of(j * BLK, BLK), BLK)
            share = factor[pl.ds(j, 1), rows] * jnp.where(slot < high, 1.0, 0.0)
            mix = (alpha[:, rows] * share).astype(jnp.bfloat16)
            block = tile(real)
            ahead = lax.dot_general(
                mix, block, (((1,), (1,)), ((), ())), preferred_element_type=jnp.float32
            )
            spread = jnp.dot(weight[:, places], block, preferred_element_type=jnp.float32)
            values = []
            if kind == 1:
                values.append(mix.astype(jnp.float32) * spread)
            elif kind == 2:
                first = (early[:, rows] * share).astype(jnp.bfloat16)
                values.append(first.astype(jnp.float32) * spread)
                values.append(last[:, places].astype(jnp.float32) * ahead)
            values = [jnp.sum(v, axis=1, keepdims=True) for v in values]
            found.append((i, j, rows, places, ahead, share * spread, values))
        for i, j, rows, places, ahead, behind, values in found:
            pred[:, places] += ahead
            carried[:, rows] += behind
            for t, value in enumerate(values):
                hit = lax.broadcasted_iota(jnp.int32, terms.shape[2:], 1) == j
                terms[t, i] += jnp.where(hit, value, 0.0)

    near_count = jnp.minimum(number, held)

    def near_body(g, carry):
        group([g * GROUP + u for u in range(GROUP)], near_count, lambda slot: near[slot])
        return carry

    lax.fori_loop(0, lax.div(near_count + GROUP - 1, GROUP), near_body, 0)

    def far_body(g, carry):
        slots = [held + g * GROUP + u for u in range(GROUP)]
        for slot in slots:

            @pl.when(slot < number)
            def _():
                copy(slot).wait()

        group(slots, number, lambda slot: buf[lax.rem(slot - held, DEPTH)])
        for slot in slots:

            @pl.when(slot + DEPTH < number)
            def _():
                copy(slot + DEPTH).start()

        return carry

    far_count = number - near_count
    lax.fori_loop(0, lax.div(far_count + GROUP - 1, GROUP), far_body, 0)


class Lines:
    def __init__(self, lines):
        self.lines = lines
        self.place = {name: lax.axis_index(name) for name in lines}

    def peer(self, name, k):
        return lax.rem(self.place[name] + k, self.lines[name])

    def origin(self, name, k):
        return lax.rem(self.place[name] + self.lines[name] - k, self.lines[name])

    def greet(self):
        barrier = pltpu.get_barrier_semaphore()
        for name in self.lines:
            for k in range(1, self.lines[name]):
                pl.semaphore_signal(
                    barrier, inc=1, device_id={name: self.peer(name, k)},
                    device_id_type=pl.DeviceIdType.MESH,
                )

    def gather_in(self, more=0):
        total = sum(self.lines.values()) - len(self.lines) + more
        pl.semaphore_wait(pltpu.get_barrier_semaphore(), total)

    def send(self, name, source, landing, send, recv):
        copies = []
        for k in range(1, self.lines[name]):
            copy = pltpu.make_async_remote_copy(
                src_ref=source(self.peer(name, k)),
                dst_ref=landing.at[k],
                send_sem=send.at[k],
                recv_sem=recv.at[k],
                device_id={name: self.peer(name, k)},
                device_id_type=pl.DeviceIdType.MESH,
            )
            copy.start()
            copies.append(copy)
        return copies


def fetch(pairs, sems):
    copies = [
        pltpu.make_async_copy(source, target, sems.at[n])
        for n, (source, target) in enumerate(pairs)
    ]
    for copy in copies:
        copy.start()
    return copies


def gather_kernel(
    lines, group, piece, source, mask, looked, out_far, norm_far, end_far, start,
    rows_far, masks, emission_far, last_far, moved, rows, land_w, out_emb, log_norm, end, emission, last,
    local_sems, alpha_sems, load_sems, *sems,
):
    net = Lines(lines)
    net.greet()
    loads = fetch([(out_far, out_emb), (norm_far, log_norm), (end_far, end)], load_sems)
    src, dst = lines["src"], lines["dst"]
    z, d = net.place["src"], net.place["dst"]
    chips = dst // 2
    sibling = d + 1 - 2 * lax.rem(d, 2)
    held = z * dst + d
    to_dst, to_src = lax.div(held, src), lax.rem(held, src)
    number = d * src + z
    from_src, from_dst = lax.div(number, dst), lax.rem(number, dst)
    away = (to_src != z) | (to_dst != d)
    barrier = pltpu.get_barrier_semaphore()
    mesh_ids = pl.DeviceIdType.MESH
    mine = start.at[:, pl.ds(pl.multiple_of(d * piece, piece), piece)]

    @pl.when(away)
    def _():
        for s, t in ((to_src, to_dst), (from_src, from_dst)):
            pl.semaphore_signal(
                barrier, inc=1, device_id={"src": s, "dst": t}, device_id_type=mesh_ids
            )
        net.gather_in(2)

    @pl.when(jnp.logical_not(away))
    def _():
        net.gather_in()

    def plane(value):
        return pl.ds(value * group, group)

    def pass_on(source_ref, target_ref, send, recv, device):
        copy = pltpu.make_async_remote_copy(
            src_ref=source_ref, dst_ref=target_ref, send_sem=send, recv_sem=recv,
            device_id=device, device_id_type=mesh_ids,
        )
        copy.start()
        return copy

    order = sorted(range(1, src), key=lambda k: min(k, src - k))
    along = []

    def next_round():
        k = order[len(along)]
        other = net.peer("src", k)
        along.append(
            pass_on(
                source.at[:, other, d], rows.at[plane(z), d],
                sems[0].at[k], sems[1].at[k], {"src": other},
            )
        )

    next_round()
    words = net.send("dst", lambda peer: looked, land_w, sems[2], sems[3])
    masks[z] = mask[...]
    marks = [
        pass_on(
            mask, masks.at[z], sems[4].at[k], sems[5].at[k], {"src": net.peer("src", k)}
        )
        for k in range(1, src)
    ]
    move = pltpu.make_async_remote_copy(
        src_ref=mine, dst_ref=moved, send_sem=alpha_sems.at[0], recv_sem=alpha_sems.at[1],
        device_id={"src": to_src, "dst": to_dst}, device_id_type=mesh_ids,
    )
    stay = pltpu.make_async_copy(mine, moved, alpha_sems.at[2])

    @pl.when(away)
    def _():
        move.start()

    @pl.when(jnp.logical_not(away))
    def _():
        stay.start()

    own = pltpu.make_async_copy(source.at[:, z], rows.at[plane(z)], local_sems.at[0])
    own.start()

    across, beside = [], []
    for n, k in enumerate(order):
        along[n].wait_recv()
        if n + 1 < len(order):
            next_round()
        here = plane(net.origin("src", k))
        block = rows.at[here, d]
        for m in range(1, chips):
            across.append(
                pass_on(
                    block, block, sems[6].at[k, m], sems[7].at[k, m],
                    {"dst": lax.rem(d + 2 * m, dst)},
                )
            )
        beside.append(
            pass_on(block, block, sems[8].at[k, 0], sems[9].at[k, 0], {"dst": sibling})
        )
        if n == 0:
            total = looked[...].astype(jnp.float32)
            for w in range(1, dst):
                words[w - 1].wait_recv()
                total = total + land_w[w].astype(jnp.float32)
            total = total.astype(jnp.bfloat16)
            for copy in loads:
                copy.wait()
            cols = out_emb.shape[0]
            width = min(cols, 1024)
            for c in range(0, cols, width):
                logits = lax.dot_general(
                    total, out_emb[c:c + width, :], (((1,), (1,)), ((), ())),
                    preferred_element_type=jnp.float32,
                )
                risen = jnp.exp(logits - log_norm[:, c:c + width])
                emission[:, c:c + width] = risen
                tail = risen[risen.shape[0] - end.shape[0]:]
                last[:, c:c + width] = (tail * end[:, c:c + width]).astype(jnp.bfloat16)
            stores = fetch([(emission, emission_far), (last, last_far)], load_sems)
    for n, k in enumerate(order):
        here = plane(net.origin("src", k))
        for m in range(1, chips):
            across[n * (chips - 1) + m - 1].wait_recv()
            block = rows.at[here, lax.rem(d + dst - 2 * m, dst)]
            beside.append(
                pass_on(block, block, sems[8].at[k, m], sems[9].at[k, m], {"dst": sibling})
            )
    own.wait()
    out = [pltpu.make_async_copy(rows.at[plane(z)], rows_far.at[plane(z)], local_sems.at[0])]
    out[0].start()
    for n, k in enumerate(order):
        here = plane(net.origin("src", k))
        beside[n].wait_recv()
        first = len(order) + n * (chips - 1)
        for copy in beside[first:first + chips - 1]:
            copy.wait_recv()
        copy = pltpu.make_async_copy(rows.at[here], rows_far.at[here], local_sems.at[n + 1])
        copy.start()
        out.append(copy)
    for copy in stores:
        copy.wait()
    for copy in marks:
        copy.wait_recv()

    @pl.when(away)
    def _():
        move.wait_recv()
        move.wait_send()

    @pl.when(jnp.logical_not(away))
    def _():
        stay.wait()

    for copy in out:
        copy.wait()
    for copies in (along, words, marks, across, beside):
        for copy in copies:
            copy.wait_send()


def stats_kernel(
    lines, piece, top, mass, alpha, near, factor, spread_alpha,
    parts, land, merged, land_2, own, land_a, *sems,
):
    net = Lines(lines)
    net.greet()
    count = lines["dst"]
    own[...] = alpha[...].astype(jnp.bfloat16)
    for p in range(count):
        rows = slice(p * piece, (p + 1) * piece)
        best = jnp.max(top[:, rows], axis=0, keepdims=True)
        total = jnp.sum(mass[:, rows] * jnp.exp(top[:, rows] - best), axis=0, keepdims=True)
        parts[p] = jnp.where(
            total > 0.0, best + jnp.log(jnp.maximum(total, 1e-37)), very_negative
        )
    net.gather_in()
    first = net.send("dst", lambda peer: parts.at[peer], land, sems[0], sems[1])
    sent = net.send("dst", lambda peer: own, land_a, sems[4], sems[5])
    land[0] = parts[net.place["dst"]]
    for copy in first:
        copy.wait_recv()
    best = land[0]
    for k in range(1, count):
        best = jnp.maximum(best, land[k])
    total = jnp.zeros_like(best)
    for k in range(count):
        total = total + jnp.exp(land[k] - best)
    merged[...] = best + jnp.log(total)
    second = net.send("dst", lambda peer: merged, land_2, sems[2], sems[3])

    def finish(k, level):
        rows = pl.ds(pl.multiple_of(net.origin("dst", k) * piece, piece), piece)
        factor[:, rows] = jnp.exp(top[:, rows] - level)

    finish(0, merged[...])
    for k in range(count):
        rows = pl.ds(pl.multiple_of(net.origin("dst", k) * piece, piece), piece)
        if k:
            sent[k - 1].wait_recv()
        spread_alpha[:, rows] = (own[...] if k == 0 else land_a[k]).astype(jnp.float32)
    for k in range(1, count):
        second[k - 1].wait_recv()
        finish(k, land_2[k])
    for copy in first + second + sent:
        copy.wait_send()


def exchange_kernel(
    lines, piece, states, step, later, pred_far, carried_far, emission, near, alpha, weights,
    pred, carried, glow, glow_next, load_sems,
    out_f, out_b, in_f, in_b, red_f, red_b, land_f, land_b, *sems,
):
    net = Lines(lines)
    traces = pred.shape[0]
    net.greet()
    loads = fetch(
        [
            (pred_far, pred),
            (emission.at[pl.ds(step * traces, traces)], glow),
            (carried_far, carried),
            (emission.at[pl.ds(later * traces, traces)], glow_next),
        ],
        load_sems,
    )
    for copy in loads:
        copy.wait()
    shape = (pred.shape[0], LANES)
    total_f = jnp.broadcast_to(
        jnp.sum(pred[...] * glow[...], axis=1, keepdims=True), shape
    ).astype(jnp.bfloat16)
    total_b = jnp.broadcast_to(
        jnp.sum(carried[...], axis=1, keepdims=True), shape
    ).astype(jnp.bfloat16)
    payload = {"src": (out_f, pred, total_f), "dst": (out_b, carried, total_b)}
    for name, (out, value, total) in payload.items():
        for p in range(lines[name]):
            out[p, :, :piece] = value[:, p * piece:(p + 1) * piece].astype(jnp.bfloat16)
            out[p, :, piece:] = total
    net.gather_in()
    landing = {"src": in_f, "dst": in_b}
    first = {}
    for n, name in enumerate(("src", "dst")):
        out = payload[name][0]
        first[name] = net.send(
            name, lambda peer, out=out: out.at[peer], landing[name], sems[n], sems[2 + n]
        )
    second = {}
    order = (("src", "dst", red_f, land_f), ("dst", "src", red_b, land_b))
    for n, (name, other, red, land) in enumerate(order):
        value = payload[name][0][net.place[name]].astype(jnp.float32)
        for k in range(1, lines[name]):
            first[name][k - 1].wait_recv()
            value = value + landing[name][k].astype(jnp.float32)
        part, total = value[:, :piece], value[:, piece:]
        if name == "src":
            start = pl.multiple_of(net.place["src"] * piece, piece)
            part = part * glow[:, pl.ds(start, piece)]
        red[:, :piece] = part.astype(jnp.bfloat16)
        red[:, piece:] = total.astype(jnp.bfloat16)
        second[other] = net.send(
            other, lambda peer, red=red: red, land, sems[4 + n], sems[6 + n]
        )
    for name, red, land in (("dst", red_f, land_f), ("src", red_b, land_b)):
        total = red[:, piece:piece + 1].astype(jnp.float32)
        for k in range(1, lines[name]):
            second[name][k - 1].wait_recv()
            total = total + land[k, :, piece:piece + 1].astype(jnp.float32)
        scale = states / total
        for k in range(lines[name]):
            part = red[:, :piece] if k == 0 else land[k, :, :piece]
            start = pl.multiple_of(net.origin(name, k) * piece, piece)
            part = part.astype(jnp.float32) * scale
            if name == "dst":
                alpha[:, pl.ds(start, piece)] = part
            else:
                part = part * glow_next[:, pl.ds(start, piece)]
                weights[:, pl.ds(start, piece)] = part.astype(jnp.bfloat16)
    for copies in (*first.values(), *second.values()):
        for copy in copies:
            copy.wait_send()


def final_kernel(
    lines, piece, states, norm, pred_far, carried_far, emission, mid_far, end_far, owner,
    alpha, beta, counts, pred, carried, glow, mid_terms, end_terms, load_sems,
    out_f, in_f, red_f, land_f, out_b, in_b, red_b, natural, land_b,
    sums, in_s, red_s, land_s, mine, in_c, *sems,
):
    net = Lines(lines)
    net.greet()
    src, dst = lines["src"], lines["dst"]
    traces = pred.shape[0]
    loads = fetch(
        [
            (carried_far, carried),
            (pred_far, pred),
            (emission.at[pl.ds((STEPS - 1) * traces, traces)], glow),
            (mid_far, mid_terms),
            (end_far, end_terms),
        ],
        load_sems,
    )
    shape = (traces, LANES)
    number = net.place["dst"] * src + net.place["src"]
    to_src, to_dst = lax.div(number, dst), lax.rem(number, dst)
    held = net.place["src"] * dst + net.place["dst"]
    from_dst, from_src = lax.div(held, src), lax.rem(held, src)
    away = (to_src != net.place["src"]) | (to_dst != net.place["dst"])
    barrier = pltpu.get_barrier_semaphore()

    @pl.when(away)
    def _():
        for s, d in ((to_src, to_dst), (from_src, from_dst)):
            pl.semaphore_signal(
                barrier, inc=1, device_id={"src": s, "dst": d},
                device_id_type=pl.DeviceIdType.MESH,
            )

    for copy in loads:
        copy.wait()
    terms = [mid_terms[0], end_terms[0], end_terms[1]]
    rows = [jnp.sum(pred[...] * glow[...], axis=1, keepdims=True)]
    rows.append(jnp.sum(carried[...], axis=1, keepdims=True))
    for t in terms:
        rows.append(jnp.sum(jnp.sum(t, axis=0), axis=1, keepdims=True))
    for n, row in enumerate(rows):
        sums[n] = jnp.broadcast_to(row, shape)
    for p in range(src):
        out_f[p] = pred[:, p * piece:(p + 1) * piece]
    for p in range(dst):
        out_b[p] = carried[:, p * piece:(p + 1) * piece]

    @pl.when(away)
    def _():
        net.gather_in(2)

    @pl.when(jnp.logical_not(away))
    def _():
        net.gather_in()

    first_s = net.send("src", lambda peer: sums, in_s, sems[0], sems[1])
    first_b = net.send("dst", lambda peer: out_b.at[peer], in_b, sems[2], sems[3])
    first_f = net.send("src", lambda peer: out_f.at[peer], in_f, sems[4], sems[5])

    total = sums[...]
    for k in range(1, src):
        first_s[k - 1].wait_recv()
        total = total + in_s[k]
    red_s[...] = total
    second_s = net.send("dst", lambda peer: red_s, land_s, sems[6], sems[7])

    value = out_b[net.place["dst"]]
    for k in range(1, dst):
        first_b[k - 1].wait_recv()
        value = value + in_b[k]
    red_b[...] = value
    move = pltpu.make_async_remote_copy(
        src_ref=red_b, dst_ref=natural, send_sem=sems[10].at[0], recv_sem=sems[10].at[1],
        device_id={"src": to_src, "dst": to_dst}, device_id_type=pl.DeviceIdType.MESH,
    )

    @pl.when(away)
    def _():
        move.start()

    value = out_f[net.place["src"]]
    for k in range(1, src):
        first_f[k - 1].wait_recv()
        value = value + in_f[k]
    start = pl.multiple_of(net.place["src"] * piece, piece)
    red_f[...] = value * glow[:, pl.ds(start, piece)]
    total = red_s[...]
    for k in range(1, dst):
        second_s[k - 1].wait_recv()
        total = total + land_s[k]
    level = jnp.zeros(mine.shape, jnp.float32)
    for t in range(len(terms)):
        share = norm / total[2 + t]
        level = level + jnp.sum(terms[t] * share[None], axis=1)
    mine[...] = level
    third_c = net.send("src", lambda peer: mine, in_c, sems[11], sems[12])

    @pl.when(away)
    def _():
        move.wait_recv()

    @pl.when(jnp.logical_not(away))
    def _():
        natural[...] = red_b[...]

    third_b = net.send("dst", lambda peer: natural, land_b, sems[13], sems[14])
    second_f = net.send("src", lambda peer: red_f, land_f, sems[8], sems[9])

    scale = states / total[0][:, :1]
    for k in range(src):
        if k:
            second_f[k - 1].wait_recv()
        part = red_f[...] if k == 0 else land_f[k]
        begin = pl.multiple_of(net.origin("src", k) * piece, piece)
        alpha[:, pl.ds(begin, piece)] = part * scale
    value = jnp.zeros(counts.shape, jnp.float32)
    blocks = counts.shape[0]
    wanted = net.place["src"] * blocks + lax.broadcasted_iota(
        jnp.int32, (blocks, owner.shape[2]), 0
    )
    for k in range(src):
        if k:
            third_c[k - 1].wait_recv()
        owned = (owner[net.origin("src", k)] == wanted).astype(jnp.float32)
        value = value + jnp.dot(
            owned, mine[...] if k == 0 else in_c[k],
            precision=lax.Precision.HIGHEST, preferred_element_type=jnp.float32,
        )
    counts[...] = value
    scale = states / total[1][:, :1]
    for k in range(dst):
        if k:
            third_b[k - 1].wait_recv()
        part = natural[...] if k == 0 else land_b[k]
        begin = pl.multiple_of(net.origin("dst", k) * piece, piece)
        beta[:, pl.ds(begin, piece)] = part * scale

    @pl.when(away)
    def _():
        move.wait_send()

    for copies in (first_s, first_b, first_f, second_s, second_f, third_c, third_b):
        for copy in copies:
            copy.wait_send()


def local(
    src_emb, dst_emb, out_emb, word_table, log_norm, block_mask, tokens, alpha_start, beta_end
):
    row_count, emb_width = src_emb.shape
    col_count = dst_emb.shape[0]
    traces = alpha_start.shape[0]
    src_count = lax.axis_size("src")
    dst_count = lax.axis_size("dst")
    states = row_count * src_count
    group = dst_count // src_count
    piece = col_count // src_count
    unit = min(BLK, piece)
    units = row_count // unit
    cols = col_count // BLK
    places = units * cols
    src_place = lax.axis_index("src")
    dst_place = lax.axis_index("dst")
    smem = pl.BlockSpec(memory_space=pltpu.SMEM)
    vmem = pl.BlockSpec(memory_space=pltpu.VMEM)
    anywhere = pl.BlockSpec(memory_space=pl.ANY)
    hbm = pl.BlockSpec(memory_space=pltpu.HBM)
    lines = {"src": src_count, "dst": dst_count}
    on_src = pltpu.SemaphoreType.DMA((src_count,))
    on_dst = pltpu.SemaphoreType.DMA((dst_count,))
    on_chips = pltpu.SemaphoreType.DMA((src_count, dst_count // 2))

    def f32(*shape):
        return jax.ShapeDtypeStruct(shape, jnp.float32)

    def bf16(*shape):
        return jax.ShapeDtypeStruct(shape, jnp.bfloat16)

    def room(*shape, dtype=jnp.float32):
        return pltpu.VMEM(shape, dtype)

    half = functools.partial(room, dtype=jnp.bfloat16)

    def outside(array):
        return pltpu.with_memory_space_constraint(array, pltpu.HBM)

    vocab_slice = word_table.shape[0]
    local_ids = tokens.reshape(-1) - dst_place * vocab_slice
    onehot = (local_ids[:, None] == jnp.arange(vocab_slice, dtype=jnp.int32)[None, :]).astype(
        jnp.bfloat16
    )
    looked = jnp.dot(onehot, word_table, preferred_element_type=jnp.float32)
    share = piece // dst_count
    gathered, masks, emission, last_weights, alpha_moved = pl.pallas_call(
        functools.partial(gather_kernel, lines, group, piece),
        out_shape=(
            pltpu.HBM((dst_count, dst_count, share, emb_width), jnp.bfloat16),
            jax.ShapeDtypeStruct((src_count,) + block_mask.shape, jnp.int32),
            pltpu.HBM((STEPS * traces, col_count), jnp.float32),
            pltpu.HBM((traces, col_count), jnp.bfloat16),
            pltpu.HBM((traces, piece), jnp.float32),
        ),
        in_specs=[hbm, vmem, vmem, hbm, hbm, hbm, hbm],
        out_specs=(hbm, vmem, hbm, hbm, hbm),
        scratch_shapes=[
            half(dst_count, dst_count, share, emb_width),
            half(dst_count, STEPS * traces, emb_width),
            half(col_count, emb_width),
            room(1, col_count),
            room(traces, col_count),
            room(STEPS * traces, col_count),
            half(traces, col_count),
            on_src,
            pltpu.SemaphoreType.DMA((3,)),
            pltpu.SemaphoreType.DMA((3,)),
        ]
        + [on_src, on_src, on_dst, on_dst, on_src, on_src]
        + [on_chips] * 4,
        compiler_params=pltpu.CompilerParams(
            collective_id=3, has_side_effects=True, vmem_limit_bytes=TABLE_BYTES
        ),
        name="gather",
    )(
        outside(src_emb.reshape(group, src_count, dst_count, share, emb_width)),
        block_mask, looked.astype(jnp.bfloat16), outside(out_emb),
        outside(log_norm[None, :]), outside(beta_end), outside(alpha_start),
    )
    whole_mask = masks.reshape(src_count * block_mask.shape[0], cols)
    unit_index = jnp.arange(units, dtype=jnp.int32)
    per_piece = piece // unit
    unit_state = (
        (unit_index // per_piece) * col_count + src_place * piece + (unit_index % per_piece) * unit
    )
    unit_block = unit_state // BLK
    owner = unit_block[:, None] == jnp.arange(whole_mask.shape[0], dtype=jnp.int32)[None, :]
    mask = jnp.sum(jnp.where(owner[:, :, None], whole_mask[None], 0), axis=1)
    flat = (mask == 1).reshape(places)
    index = jnp.arange(places, dtype=jnp.int32)
    before = jnp.sum(
        jnp.where((index[None, :] < index[:, None]) & flat[None, :], 1, 0), axis=1
    )
    ids = jnp.sum(
        jnp.where((before[None, :] == index[:, None]) & flat[None, :], index[None, :], 0), axis=1
    ).astype(jnp.int32)
    number = jnp.sum(flat.astype(jnp.int32)).reshape(1)

    guess = places // 5 + 1
    held = min(places, HELD_BYTES // (BLK * unit * 2))
    params = pltpu.CompilerParams(vmem_limit_bytes=VMEM_BYTES)
    top, mass, near, far = pl.pallas_call(
        functools.partial(table_kernel, unit, cols, held),
        out_shape=(
            f32(cols, row_count),
            f32(cols, row_count),
            half(held, BLK, unit),
            jax.ShapeDtypeStruct((max(places - held, 1), BLK, unit), jnp.bfloat16),
        ),
        in_specs=[smem, smem, hbm, hbm],
        out_specs=(vmem, vmem, vmem, anywhere),
        scratch_shapes=[
            half(dst_count, dst_count, share, emb_width),
            half(col_count, emb_width),
            pltpu.SemaphoreType.DMA((2,)),
        ]
        + [pltpu.VMEM((BLK, unit), jnp.bfloat16)] * 2
        + [pltpu.VMEM((BLK, unit), jnp.float32)] * 2
        + [pltpu.VMEM((1, unit), jnp.float32)] * 2
        + [pltpu.SemaphoreType.DMA((2,))],
        compiler_params=pltpu.CompilerParams(vmem_limit_bytes=TABLE_BYTES),
        cost_estimate=pl.CostEstimate(
            flops=guess * BLK * unit * emb_width * 2,
            bytes_accessed=guess * BLK * unit,
            transcendentals=guess * BLK * unit,
        ),
        name="table",
    )(ids, number, outside(gathered), outside(dst_emb))
    near = pltpu.with_memory_space_constraint(near, pltpu.VMEM)

    factor, alpha_rows = pl.pallas_call(
        functools.partial(stats_kernel, lines, piece),
        out_shape=(f32(cols, row_count), f32(traces, row_count)),
        in_specs=[vmem] * 4,
        out_specs=(vmem,) * 2,
        scratch_shapes=[
            room(dst_count, 1, piece),
            room(dst_count, 1, piece),
            room(1, piece),
            room(dst_count, 1, piece),
            half(traces, piece),
            half(dst_count, traces, piece),
        ]
        + [on_dst] * 6,
        compiler_params=pltpu.CompilerParams(
            collective_id=0, has_side_effects=True, vmem_limit_bytes=VMEM_BYTES
        ),
        name="stats",
    )(top, mass, alpha_moved, near)

    lanes = -(-cols // LANES) * LANES

    def sweep(kind, alphas, weights):
        outs = [f32(traces, col_count), f32(traces, row_count)]
        if kind:
            outs.append(f32(kind, units, traces, lanes))
        return pl.pallas_call(
            functools.partial(sweep_kernel, unit, cols, held, traces, kind),
            out_shape=tuple(outs),
            in_specs=[smem, smem] + [vmem] * (len(alphas) + 2 + len(weights)) + [anywhere],
            out_specs=(vmem,) * len(outs),
            scratch_shapes=[
                pltpu.VMEM((DEPTH, BLK, unit), jnp.bfloat16),
                pltpu.SemaphoreType.DMA((DEPTH,)),
            ],
            compiler_params=params,
            cost_estimate=pl.CostEstimate(
                flops=guess * BLK * unit * traces * 4,
                bytes_accessed=guess * BLK * unit,
                transcendentals=0,
            ),
            name="sweep%d" % kind,
        )(ids, number, *alphas, factor, *weights, near, far)

    def exchange(ahead, behind, step, later):
        width = piece + LANES
        return pl.pallas_call(
            functools.partial(exchange_kernel, lines, piece, states, step, later),
            out_shape=(f32(traces, row_count), bf16(traces, col_count)),
            in_specs=[hbm] * 3 + [vmem],
            out_specs=(vmem, vmem),
            scratch_shapes=[
                room(traces, col_count),
                room(traces, row_count),
                room(traces, col_count),
                room(traces, col_count),
                pltpu.SemaphoreType.DMA((4,)),
                half(src_count, traces, width),
                half(dst_count, traces, width),
                half(src_count, traces, width),
                half(dst_count, traces, width),
                half(traces, width),
                half(traces, width),
                half(dst_count, traces, width),
                half(src_count, traces, width),
            ]
            + [on_src, on_dst, on_src, on_dst, on_dst, on_src, on_dst, on_src],
            compiler_params=pltpu.CompilerParams(
                collective_id=1 + 3 * step, has_side_effects=True, vmem_limit_bytes=VMEM_BYTES
            ),
            name="exchange",
        )(outside(ahead), outside(behind), outside(emission), near)

    pred, carried = sweep(0, [alpha_rows], [last_weights])
    alpha_1, weights_2 = exchange(pred, carried, 0, 1)
    pred, carried, middle_terms = sweep(1, [alpha_1], [weights_2])
    alpha_2, weights_1 = exchange(pred, carried, 1, 0)
    pred, carried, end_terms = sweep(2, [alpha_2, alpha_rows], [weights_1, last_weights])

    mask_rows = block_mask.shape[0]
    index = np.arange(units)
    all_state = (index // per_piece * col_count + index % per_piece * unit)[None, :] + (
        np.arange(src_count)[:, None] * piece
    )
    unit_blocks = jnp.asarray((all_state // BLK)[:, None, :], jnp.int32)
    norm = mask_rows * src_count * cols * dst_count / (STEPS * traces)
    alpha_end, beta_start, block_counts = pl.pallas_call(
        functools.partial(final_kernel, lines, piece, states, norm),
        out_shape=(
            f32(traces, col_count), f32(traces, row_count), f32(mask_rows, lanes),
        ),
        in_specs=[hbm] * 5 + [vmem],
        out_specs=(vmem,) * 3,
        scratch_shapes=[
            room(traces, col_count),
            room(traces, row_count),
            room(traces, col_count),
            room(1, units, traces, lanes),
            room(2, units, traces, lanes),
            pltpu.SemaphoreType.DMA((5,)),
            room(src_count, traces, piece),
            room(src_count, traces, piece),
            room(traces, piece),
            room(src_count, traces, piece),
            room(dst_count, traces, piece),
            room(dst_count, traces, piece),
            room(traces, piece),
            room(traces, piece),
            room(dst_count, traces, piece),
            room(2 + STEPS, traces, LANES),
            room(src_count, 2 + STEPS, traces, LANES),
            room(2 + STEPS, traces, LANES),
            room(dst_count, 2 + STEPS, traces, LANES),
            room(units, lanes),
            room(src_count, units, lanes),
        ]
        + [on_src, on_src, on_dst, on_dst, on_src, on_src, on_dst, on_dst, on_src, on_src]
        + [pltpu.SemaphoreType.DMA((2,)), on_src, on_src, on_dst, on_dst],
        compiler_params=pltpu.CompilerParams(
            collective_id=2, has_side_effects=True, vmem_limit_bytes=VMEM_BYTES
        ),
        name="final",
    )(
        outside(pred), outside(carried), outside(emission), outside(middle_terms),
        outside(end_terms), unit_blocks,
    )
    return (alpha_end, beta_start, block_counts[:, :cols])


def solution(mesh):
    return jax.shard_map(
        local,
        mesh=mesh,
        in_specs=(
            P("src", None),
            P("dst", None),
            P("dst", None),
            P("dst", None),
            P("dst"),
            P("src", "dst"),
            P(),
            P(None, "src"),
            P(None, "dst"),
        ),
        out_specs=(P(None, "dst"), P(None, "src"), P("src", "dst")),
        check_vma=False,
    )
```

```python
import functools

import jax
import jax.numpy as jnp
import numpy as np
from jax import lax
from jax.experimental import pallas as pl
from jax.experimental.pallas import tpu as pltpu
from jax.sharding import PartitionSpec as P

BLK = 512
STEPS = 3
LANES = 128
DEPTH = 8
WRITES = 4
very_negative = -1e30
GROUP = 6
HELD_BYTES = 48 * 1024 * 1024
TABLE_BYTES = 14 * 1024 * 1024
VMEM_BYTES = 14 * 1024 * 1024


def table_kernel(
    unit, cols, held, ids, count, src_far, dst_far, top, mass, near, far, src, dst, load_sems,
    buf, scores_0, scores_1, best_0, best_1, sems,
):
    number = count[0]
    loads = fetch([(src_far, src), (dst_far, dst)], load_sems)
    src = src.reshape(top.shape[1], src.shape[-1])
    chunk = min(256, unit)
    tall = BLK // 4
    blocks = [
        (slice(q * tall, (q + 1) * tall), slice(c * chunk, (c + 1) * chunk))
        for c in range(unit // chunk)
        for q in range(BLK // tall)
    ]
    top[...] = jnp.full_like(top, very_negative)
    mass[...] = jnp.zeros_like(mass)
    for copy in loads:
        copy.wait()

    def place(slot):
        entry = ids[slot]
        return lax.div(entry, cols), lax.rem(entry, cols)

    def fold(values, join):
        merged = {}
        for (_, span), value in zip(blocks, values):
            old = merged.get(span.start)
            merged[span.start] = value if old is None else join(old, value)
        return list(merged.values())

    def score(slot, scores, where):
        i, j = place(slot)
        down, span = where
        d = dst[pl.ds(pl.multiple_of(j * BLK + down.start, tall), tall), :]
        value = lax.dot_general(
            d, src[pl.ds(pl.multiple_of(i * unit + span.start, chunk), chunk), :],
            (((1,), (1,)), ((), ())), preferred_element_type=jnp.float32,
        )
        scores[down, span] = value
        return jnp.max(value.reshape(tall // 8, 8, chunk), axis=0)

    def settle(best, tops):
        tops = [jnp.max(t, axis=0, keepdims=True) for t in fold(tops, jnp.maximum)]
        best[...] = jnp.concatenate(tops, axis=1)

    def phase(slot, scores, best, later, scores_next, best_next, put):
        level = best[...]
        tops, sums = [], []
        for where in blocks:
            tops.append(score(later, scores_next, where))
            risen = jnp.exp(scores[where] - level[:, where[1]])
            put(where, risen.astype(jnp.bfloat16))
            sums.append(jnp.sum(risen.reshape(tall // 8, 8, chunk), axis=0))
        i, j = place(slot)
        rows = pl.ds(pl.multiple_of(i * unit, unit), unit)
        top[pl.ds(j, 1), rows] = level
        sums = [jnp.sum(t, axis=0, keepdims=True) for t in fold(sums, jnp.add)]
        mass[pl.ds(j, 1), rows] = jnp.concatenate(sums, axis=1)
        settle(best_next, tops)

    def run(low, high, out):
        settle(best_0, [score(low, scores_0, where) for where in blocks])

        def body(p, carry):
            even = low + 2 * p
            odd = jnp.minimum(even + 1, high - 1)
            after = jnp.minimum(even + 2, high - 1)
            with_even, with_odd = out(p, even, odd, high)
            with_even(lambda put: phase(even, scores_0, best_0, odd, scores_1, best_1, put))
            with_odd(lambda put: phase(odd, scores_1, best_1, after, scores_0, best_0, put))
            return carry

        lax.fori_loop(0, lax.div(high - low + 1, 2), body, 0)

    def keep(p, even, odd, high):
        def store(slot):
            def put(where, value):
                near[(slot, *where)] = value

            return put

        return lambda go: go(store(even)), lambda go: go(store(odd))

    def copy(slot):
        b = lax.rem(slot - held, WRITES)
        return pltpu.make_async_copy(buf.at[b], far.at[slot - held], sems.at[b])

    def send(p, even, odd, high):
        def through(slot, live):
            b = lax.rem(slot - held, WRITES)

            def put(where, value):
                buf[(b, *where)] = value

            def go(step):
                @pl.when(slot - held >= WRITES)
                def _():
                    copy(slot - WRITES).wait()

                step(put)

                @pl.when(live)
                def _():
                    copy(slot).start()

            return go

        return through(even, even < high), through(even + 1, even + 1 < high)

    @pl.when(number > held)
    def _():
        run(held, number, send)

    @pl.when(number > 0)
    def _():
        run(0, jnp.minimum(number, held), keep)

    sent = number - held + lax.rem(jnp.maximum(number - held, 0), 2)
    for back in range(1, WRITES + 1):

        @pl.when((number > held) & (sent - back >= 0) & (sent - back < number - held))
        def _():
            copy(held + sent - back).wait()


def sweep_kernel(unit, cols, held, traces, kind, ids, count, *refs):
    if kind == 2:
        alpha, early, factor, weight, last, near, far, pred, carried, terms, buf, sems = refs
    elif kind == 1:
        alpha, factor, weight, near, far, pred, carried, terms, buf, sems = refs
    else:
        alpha, factor, weight, near, far, pred, carried, buf, sems = refs
    number = count[0]
    pred[...] = jnp.zeros_like(pred)
    carried[...] = jnp.zeros_like(carried)
    if kind:
        terms[...] = jnp.zeros_like(terms)

    def copy(slot):
        b = lax.rem(slot - held, DEPTH)
        return pltpu.make_async_copy(far.at[slot - held], buf.at[b], sems.at[b])

    for p in range(DEPTH):

        @pl.when(held + p < number)
        def _():
            copy(held + p).start()

    def group(slots, high, tile):
        begun, found = [], []
        for slot in slots:
            real = jnp.minimum(slot, high - 1)
            entry = ids[real]
            i = lax.div(entry, cols)
            j = lax.rem(entry, cols)
            rows = pl.ds(pl.multiple_of(i * unit, unit), unit)
            places = pl.ds(pl.multiple_of(j * BLK, BLK), BLK)
            share = factor[pl.ds(j, 1), rows] * jnp.where(slot < high, 1.0, 0.0)
            mix = (alpha[:, rows] * share).astype(jnp.bfloat16)
            block = tile(real)
            spread = jnp.dot(weight[:, places], block, preferred_element_type=jnp.float32)
            begun.append((i, j, rows, places, share, mix, block, spread))
        for i, j, rows, places, share, mix, block, spread in begun:
            ahead = lax.dot_general(
                mix, block, (((1,), (1,)), ((), ())), preferred_element_type=jnp.float32
            )
            values = []
            if kind == 1:
                values.append(mix.astype(jnp.float32) * spread)
            elif kind == 2:
                first = (early[:, rows] * share).astype(jnp.bfloat16)
                values.append(first.astype(jnp.float32) * spread)
                values.append(last[:, places].astype(jnp.float32) * ahead)
            values = [jnp.sum(v, axis=1, keepdims=True) for v in values]
            found.append((i, j, rows, places, ahead, share * spread, values))
        for i, j, rows, places, ahead, behind, values in found:
            pred[:, places] += ahead
            carried[:, rows] += behind
            for t, value in enumerate(values):
                hit = lax.broadcasted_iota(jnp.int32, terms.shape[2:], 1) == j
                terms[t, i] += jnp.where(hit, value, 0.0)

    near_count = jnp.minimum(number, held)

    def near_body(g, carry):
        group([g * GROUP + u for u in range(GROUP)], near_count, lambda slot: near[slot])
        return carry

    lax.fori_loop(0, lax.div(near_count + GROUP - 1, GROUP), near_body, 0)

    def far_body(g, carry):
        slots = [held + g * GROUP + u for u in range(GROUP)]
        for slot in slots:

            @pl.when(slot < number)
            def _():
                copy(slot).wait()

        group(slots, number, lambda slot: buf[lax.rem(slot - held, DEPTH)])
        for slot in slots:

            @pl.when(slot + DEPTH < number)
            def _():
                copy(slot + DEPTH).start()

        return carry

    far_count = number - near_count
    lax.fori_loop(0, lax.div(far_count + GROUP - 1, GROUP), far_body, 0)


class Lines:
    def __init__(self, lines):
        self.lines = lines
        self.place = {name: lax.axis_index(name) for name in lines}

    def peer(self, name, k):
        return lax.rem(self.place[name] + k, self.lines[name])

    def origin(self, name, k):
        return lax.rem(self.place[name] + self.lines[name] - k, self.lines[name])

    def greet(self):
        barrier = pltpu.get_barrier_semaphore()
        for name in self.lines:
            for k in range(1, self.lines[name]):
                pl.semaphore_signal(
                    barrier, inc=1, device_id={name: self.peer(name, k)},
                    device_id_type=pl.DeviceIdType.MESH,
                )

    def gather_in(self, more=0):
        total = sum(self.lines.values()) - len(self.lines) + more
        pl.semaphore_wait(pltpu.get_barrier_semaphore(), total)

    def send(self, name, source, landing, send, recv):
        copies = []
        for k in range(1, self.lines[name]):
            copy = pltpu.make_async_remote_copy(
                src_ref=source(self.peer(name, k)),
                dst_ref=landing.at[k],
                send_sem=send.at[k],
                recv_sem=recv.at[k],
                device_id={name: self.peer(name, k)},
                device_id_type=pl.DeviceIdType.MESH,
            )
            copy.start()
            copies.append(copy)
        return copies


def fetch(pairs, sems):
    copies = [
        pltpu.make_async_copy(source, target, sems.at[n])
        for n, (source, target) in enumerate(pairs)
    ]
    for copy in copies:
        copy.start()
    return copies


def gather_kernel(
    lines, group, piece, source, mask, looked, out_far, norm_far, end_far, start,
    rows_far, masks, emission_far, last_far, moved, rows, land_w, out_emb, log_norm, end, emission, last,
    local_sems, alpha_sems, load_sems, *sems,
):
    net = Lines(lines)
    net.greet()
    loads = fetch([(out_far, out_emb), (norm_far, log_norm), (end_far, end)], load_sems)
    src, dst = lines["src"], lines["dst"]
    z, d = net.place["src"], net.place["dst"]
    chips = dst // 2
    sibling = d + 1 - 2 * lax.rem(d, 2)
    held = z * dst + d
    to_dst, to_src = lax.div(held, src), lax.rem(held, src)
    number = d * src + z
    from_src, from_dst = lax.div(number, dst), lax.rem(number, dst)
    away = (to_src != z) | (to_dst != d)
    barrier = pltpu.get_barrier_semaphore()
    mesh_ids = pl.DeviceIdType.MESH
    mine = start.at[:, pl.ds(pl.multiple_of(d * piece, piece), piece)]

    @pl.when(away)
    def _():
        for s, t in ((to_src, to_dst), (from_src, from_dst)):
            pl.semaphore_signal(
                barrier, inc=1, device_id={"src": s, "dst": t}, device_id_type=mesh_ids
            )
        net.gather_in(2)

    @pl.when(jnp.logical_not(away))
    def _():
        net.gather_in()

    def plane(value):
        return pl.ds(value * group, group)

    def pass_on(source_ref, target_ref, send, recv, device):
        copy = pltpu.make_async_remote_copy(
            src_ref=source_ref, dst_ref=target_ref, send_sem=send, recv_sem=recv,
            device_id=device, device_id_type=mesh_ids,
        )
        copy.start()
        return copy

    order = sorted(range(1, src), key=lambda k: min(k, src - k))
    along = []

    def next_round():
        k = order[len(along)]
        other = net.peer("src", k)
        along.append(
            pass_on(
                source.at[:, other, d], rows.at[plane(z), d],
                sems[0].at[k], sems[1].at[k], {"src": other},
            )
        )

    next_round()
    words = net.send("dst", lambda peer: looked, land_w, sems[2], sems[3])
    masks[z] = mask[...]
    marks = [
        pass_on(
            mask, masks.at[z], sems[4].at[k], sems[5].at[k], {"src": net.peer("src", k)}
        )
        for k in range(1, src)
    ]
    move = pltpu.make_async_remote_copy(
        src_ref=mine, dst_ref=moved, send_sem=alpha_sems.at[0], recv_sem=alpha_sems.at[1],
        device_id={"src": to_src, "dst": to_dst}, device_id_type=mesh_ids,
    )
    stay = pltpu.make_async_copy(mine, moved, alpha_sems.at[2])

    @pl.when(away)
    def _():
        move.start()

    @pl.when(jnp.logical_not(away))
    def _():
        stay.start()

    own = pltpu.make_async_copy(source.at[:, z], rows.at[plane(z)], local_sems.at[0])
    own.start()

    across, beside = [], []
    for n, k in enumerate(order):
        along[n].wait_recv()
        if n + 1 < len(order):
            next_round()
        here = plane(net.origin("src", k))
        block = rows.at[here, d]
        for m in range(1, chips):
            across.append(
                pass_on(
                    block, block, sems[6].at[k, m], sems[7].at[k, m],
                    {"dst": lax.rem(d + 2 * m, dst)},
                )
            )
        beside.append(
            pass_on(block, block, sems[8].at[k, 0], sems[9].at[k, 0], {"dst": sibling})
        )
        if n == 0:
            total = looked[...].astype(jnp.float32)
            for w in range(1, dst):
                words[w - 1].wait_recv()
                total = total + land_w[w].astype(jnp.float32)
            total = total.astype(jnp.bfloat16)
            for copy in loads:
                copy.wait()
            cols = out_emb.shape[0]
            width = min(cols, 1024)
            for c in range(0, cols, width):
                logits = lax.dot_general(
                    total, out_emb[c:c + width, :], (((1,), (1,)), ((), ())),
                    preferred_element_type=jnp.float32,
                )
                risen = jnp.exp(logits - log_norm[:, c:c + width])
                emission[:, c:c + width] = risen
                tail = risen[risen.shape[0] - end.shape[0]:]
                last[:, c:c + width] = (tail * end[:, c:c + width]).astype(jnp.bfloat16)
            stores = fetch([(emission, emission_far), (last, last_far)], load_sems)
    for n, k in enumerate(order):
        here = plane(net.origin("src", k))
        for m in range(1, chips):
            across[n * (chips - 1) + m - 1].wait_recv()
            block = rows.at[here, lax.rem(d + dst - 2 * m, dst)]
            beside.append(
                pass_on(block, block, sems[8].at[k, m], sems[9].at[k, m], {"dst": sibling})
            )
    own.wait()
    out = [pltpu.make_async_copy(rows.at[plane(z)], rows_far.at[plane(z)], local_sems.at[0])]
    out[0].start()
    for n, k in enumerate(order):
        here = plane(net.origin("src", k))
        beside[n].wait_recv()
        first = len(order) + n * (chips - 1)
        for copy in beside[first:first + chips - 1]:
            copy.wait_recv()
        copy = pltpu.make_async_copy(rows.at[here], rows_far.at[here], local_sems.at[n + 1])
        copy.start()
        out.append(copy)
    for copy in stores:
        copy.wait()
    for copy in marks:
        copy.wait_recv()

    @pl.when(away)
    def _():
        move.wait_recv()
        move.wait_send()

    @pl.when(jnp.logical_not(away))
    def _():
        stay.wait()

    for copy in out:
        copy.wait()
    for copies in (along, words, marks, across, beside):
        for copy in copies:
            copy.wait_send()


def stats_kernel(
    lines, piece, top, mass, alpha, near, factor, spread_alpha,
    parts, land, merged, land_2, own, land_a, *sems,
):
    net = Lines(lines)
    net.greet()
    count = lines["dst"]
    own[...] = alpha[...].astype(jnp.bfloat16)
    for p in range(count):
        rows = slice(p * piece, (p + 1) * piece)
        best = jnp.max(top[:, rows], axis=0, keepdims=True)
        total = jnp.sum(mass[:, rows] * jnp.exp(top[:, rows] - best), axis=0, keepdims=True)
        parts[p] = jnp.where(
            total > 0.0, best + jnp.log(jnp.maximum(total, 1e-37)), very_negative
        )
    net.gather_in()
    first = net.send("dst", lambda peer: parts.at[peer], land, sems[0], sems[1])
    sent = net.send("dst", lambda peer: own, land_a, sems[4], sems[5])
    land[0] = parts[net.place["dst"]]
    for copy in first:
        copy.wait_recv()
    best = land[0]
    for k in range(1, count):
        best = jnp.maximum(best, land[k])
    total = jnp.zeros_like(best)
    for k in range(count):
        total = total + jnp.exp(land[k] - best)
    merged[...] = best + jnp.log(total)
    second = net.send("dst", lambda peer: merged, land_2, sems[2], sems[3])

    def finish(k, level):
        rows = pl.ds(pl.multiple_of(net.origin("dst", k) * piece, piece), piece)
        factor[:, rows] = jnp.exp(top[:, rows] - level)

    finish(0, merged[...])
    for k in range(count):
        rows = pl.ds(pl.multiple_of(net.origin("dst", k) * piece, piece), piece)
        if k:
            sent[k - 1].wait_recv()
        spread_alpha[:, rows] = (own[...] if k == 0 else land_a[k]).astype(jnp.float32)
    for k in range(1, count):
        second[k - 1].wait_recv()
        finish(k, land_2[k])
    for copy in first + second + sent:
        copy.wait_send()


def exchange_kernel(
    lines, piece, states, step, later, pred_far, carried_far, emission, near, alpha, weights,
    pred, carried, glow, glow_next, load_sems,
    out_f, out_b, in_f, in_b, red_f, red_b, land_f, land_b, *sems,
):
    net = Lines(lines)
    traces = pred.shape[0]
    net.greet()
    loads = fetch(
        [
            (pred_far, pred),
            (emission.at[pl.ds(step * traces, traces)], glow),
            (carried_far, carried),
            (emission.at[pl.ds(later * traces, traces)], glow_next),
        ],
        load_sems,
    )
    for copy in loads:
        copy.wait()
    shape = (pred.shape[0], LANES)
    total_f = jnp.broadcast_to(
        jnp.sum(pred[...] * glow[...], axis=1, keepdims=True), shape
    ).astype(jnp.bfloat16)
    total_b = jnp.broadcast_to(
        jnp.sum(carried[...], axis=1, keepdims=True), shape
    ).astype(jnp.bfloat16)
    payload = {"src": (out_f, pred, total_f), "dst": (out_b, carried, total_b)}
    for name, (out, value, total) in payload.items():
        for p in range(lines[name]):
            out[p, :, :piece] = value[:, p * piece:(p + 1) * piece].astype(jnp.bfloat16)
            out[p, :, piece:] = total
    net.gather_in()
    landing = {"src": in_f, "dst": in_b}
    first = {}
    for n, name in enumerate(("src", "dst")):
        out = payload[name][0]
        first[name] = net.send(
            name, lambda peer, out=out: out.at[peer], landing[name], sems[n], sems[2 + n]
        )
    second = {}
    order = (("src", "dst", red_f, land_f), ("dst", "src", red_b, land_b))
    for n, (name, other, red, land) in enumerate(order):
        value = payload[name][0][net.place[name]].astype(jnp.float32)
        for k in range(1, lines[name]):
            first[name][k - 1].wait_recv()
            value = value + landing[name][k].astype(jnp.float32)
        part, total = value[:, :piece], value[:, piece:]
        if name == "src":
            start = pl.multiple_of(net.place["src"] * piece, piece)
            part = part * glow[:, pl.ds(start, piece)]
        red[:, :piece] = part.astype(jnp.bfloat16)
        red[:, piece:] = total.astype(jnp.bfloat16)
        second[other] = net.send(
            other, lambda peer, red=red: red, land, sems[4 + n], sems[6 + n]
        )
    for name, red, land in (("dst", red_f, land_f), ("src", red_b, land_b)):
        total = red[:, piece:piece + 1].astype(jnp.float32)
        for k in range(1, lines[name]):
            second[name][k - 1].wait_recv()
            total = total + land[k, :, piece:piece + 1].astype(jnp.float32)
        scale = states / total
        for k in range(lines[name]):
            part = red[:, :piece] if k == 0 else land[k, :, :piece]
            start = pl.multiple_of(net.origin(name, k) * piece, piece)
            part = part.astype(jnp.float32) * scale
            if name == "dst":
                alpha[:, pl.ds(start, piece)] = part
            else:
                part = part * glow_next[:, pl.ds(start, piece)]
                weights[:, pl.ds(start, piece)] = part.astype(jnp.bfloat16)
    for copies in (*first.values(), *second.values()):
        for copy in copies:
            copy.wait_send()


def final_kernel(
    lines, piece, states, norm, pred_far, carried_far, emission, mid_far, end_far, owner,
    alpha, beta, counts, pred, carried, glow, mid_terms, end_terms, load_sems,
    out_f, in_f, red_f, land_f, out_b, in_b, red_b, natural, land_b,
    sums, in_s, red_s, land_s, mine, in_c, *sems,
):
    net = Lines(lines)
    net.greet()
    src, dst = lines["src"], lines["dst"]
    traces = pred.shape[0]
    loads = fetch(
        [
            (carried_far, carried),
            (pred_far, pred),
            (emission.at[pl.ds((STEPS - 1) * traces, traces)], glow),
            (mid_far, mid_terms),
            (end_far, end_terms),
        ],
        load_sems,
    )
    shape = (traces, LANES)
    number = net.place["dst"] * src + net.place["src"]
    to_src, to_dst = lax.div(number, dst), lax.rem(number, dst)
    held = net.place["src"] * dst + net.place["dst"]
    from_dst, from_src = lax.div(held, src), lax.rem(held, src)
    away = (to_src != net.place["src"]) | (to_dst != net.place["dst"])
    barrier = pltpu.get_barrier_semaphore()

    @pl.when(away)
    def _():
        for s, d in ((to_src, to_dst), (from_src, from_dst)):
            pl.semaphore_signal(
                barrier, inc=1, device_id={"src": s, "dst": d},
                device_id_type=pl.DeviceIdType.MESH,
            )

    for copy in loads:
        copy.wait()
    terms = [mid_terms[0], end_terms[0], end_terms[1]]
    rows = [jnp.sum(pred[...] * glow[...], axis=1, keepdims=True)]
    rows.append(jnp.sum(carried[...], axis=1, keepdims=True))
    for t in terms:
        rows.append(jnp.sum(jnp.sum(t, axis=0), axis=1, keepdims=True))
    for n, row in enumerate(rows):
        sums[n] = jnp.broadcast_to(row, shape)
    for p in range(src):
        out_f[p] = pred[:, p * piece:(p + 1) * piece]
    for p in range(dst):
        out_b[p] = carried[:, p * piece:(p + 1) * piece]

    @pl.when(away)
    def _():
        net.gather_in(2)

    @pl.when(jnp.logical_not(away))
    def _():
        net.gather_in()

    first_s = net.send("src", lambda peer: sums, in_s, sems[0], sems[1])
    first_b = net.send("dst", lambda peer: out_b.at[peer], in_b, sems[2], sems[3])
    first_f = net.send("src", lambda peer: out_f.at[peer], in_f, sems[4], sems[5])

    total = sums[...]
    for k in range(1, src):
        first_s[k - 1].wait_recv()
        total = total + in_s[k]
    red_s[...] = total
    second_s = net.send("dst", lambda peer: red_s, land_s, sems[6], sems[7])

    value = out_b[net.place["dst"]]
    for k in range(1, dst):
        first_b[k - 1].wait_recv()
        value = value + in_b[k]
    red_b[...] = value
    move = pltpu.make_async_remote_copy(
        src_ref=red_b, dst_ref=natural, send_sem=sems[10].at[0], recv_sem=sems[10].at[1],
        device_id={"src": to_src, "dst": to_dst}, device_id_type=pl.DeviceIdType.MESH,
    )

    @pl.when(away)
    def _():
        move.start()

    value = out_f[net.place["src"]]
    for k in range(1, src):
        first_f[k - 1].wait_recv()
        value = value + in_f[k]
    start = pl.multiple_of(net.place["src"] * piece, piece)
    red_f[...] = value * glow[:, pl.ds(start, piece)]
    total = red_s[...]
    for k in range(1, dst):
        second_s[k - 1].wait_recv()
        total = total + land_s[k]
    level = jnp.zeros(mine.shape, jnp.float32)
    for t in range(len(terms)):
        share = norm / total[2 + t]
        level = level + jnp.sum(terms[t] * share[None], axis=1)
    mine[...] = level
    third_c = net.send("src", lambda peer: mine, in_c, sems[11], sems[12])

    @pl.when(away)
    def _():
        move.wait_recv()

    @pl.when(jnp.logical_not(away))
    def _():
        natural[...] = red_b[...]

    third_b = net.send("dst", lambda peer: natural, land_b, sems[13], sems[14])
    second_f = net.send("src", lambda peer: red_f, land_f, sems[8], sems[9])

    scale = states / total[0][:, :1]
    for k in range(src):
        if k:
            second_f[k - 1].wait_recv()
        part = red_f[...] if k == 0 else land_f[k]
        begin = pl.multiple_of(net.origin("src", k) * piece, piece)
        alpha[:, pl.ds(begin, piece)] = part * scale
    value = jnp.zeros(counts.shape, jnp.float32)
    blocks = counts.shape[0]
    wanted = net.place["src"] * blocks + lax.broadcasted_iota(
        jnp.int32, (blocks, owner.shape[2]), 0
    )
    for k in range(src):
        if k:
            third_c[k - 1].wait_recv()
        owned = (owner[net.origin("src", k)] == wanted).astype(jnp.float32)
        value = value + jnp.dot(
            owned, mine[...] if k == 0 else in_c[k],
            precision=lax.Precision.HIGHEST, preferred_element_type=jnp.float32,
        )
    counts[...] = value
    scale = states / total[1][:, :1]
    for k in range(dst):
        if k:
            third_b[k - 1].wait_recv()
        part = natural[...] if k == 0 else land_b[k]
        begin = pl.multiple_of(net.origin("dst", k) * piece, piece)
        beta[:, pl.ds(begin, piece)] = part * scale

    @pl.when(away)
    def _():
        move.wait_send()

    for copies in (first_s, first_b, first_f, second_s, second_f, third_c, third_b):
        for copy in copies:
            copy.wait_send()


def local(
    src_emb, dst_emb, out_emb, word_table, log_norm, block_mask, tokens, alpha_start, beta_end
):
    row_count, emb_width = src_emb.shape
    col_count = dst_emb.shape[0]
    traces = alpha_start.shape[0]
    src_count = lax.axis_size("src")
    dst_count = lax.axis_size("dst")
    states = row_count * src_count
    group = dst_count // src_count
    piece = col_count // src_count
    unit = min(BLK, piece)
    units = row_count // unit
    cols = col_count // BLK
    places = units * cols
    src_place = lax.axis_index("src")
    dst_place = lax.axis_index("dst")
    smem = pl.BlockSpec(memory_space=pltpu.SMEM)
    vmem = pl.BlockSpec(memory_space=pltpu.VMEM)
    anywhere = pl.BlockSpec(memory_space=pl.ANY)
    hbm = pl.BlockSpec(memory_space=pltpu.HBM)
    lines = {"src": src_count, "dst": dst_count}
    on_src = pltpu.SemaphoreType.DMA((src_count,))
    on_dst = pltpu.SemaphoreType.DMA((dst_count,))
    on_chips = pltpu.SemaphoreType.DMA((src_count, dst_count // 2))

    def f32(*shape):
        return jax.ShapeDtypeStruct(shape, jnp.float32)

    def bf16(*shape):
        return jax.ShapeDtypeStruct(shape, jnp.bfloat16)

    def room(*shape, dtype=jnp.float32):
        return pltpu.VMEM(shape, dtype)

    half = functools.partial(room, dtype=jnp.bfloat16)

    def outside(array):
        return pltpu.with_memory_space_constraint(array, pltpu.HBM)

    vocab_slice = word_table.shape[0]
    local_ids = tokens.reshape(-1) - dst_place * vocab_slice
    onehot = (local_ids[:, None] == jnp.arange(vocab_slice, dtype=jnp.int32)[None, :]).astype(
        jnp.bfloat16
    )
    looked = jnp.dot(onehot, word_table, preferred_element_type=jnp.float32)
    share = piece // dst_count
    gathered, masks, emission, last_weights, alpha_moved = pl.pallas_call(
        functools.partial(gather_kernel, lines, group, piece),
        out_shape=(
            pltpu.HBM((dst_count, dst_count, share, emb_width), jnp.bfloat16),
            jax.ShapeDtypeStruct((src_count,) + block_mask.shape, jnp.int32),
            pltpu.HBM((STEPS * traces, col_count), jnp.float32),
            pltpu.HBM((traces, col_count), jnp.bfloat16),
            pltpu.HBM((traces, piece), jnp.float32),
        ),
        in_specs=[hbm, vmem, vmem, hbm, hbm, hbm, hbm],
        out_specs=(hbm, vmem, hbm, hbm, hbm),
        scratch_shapes=[
            half(dst_count, dst_count, share, emb_width),
            half(dst_count, STEPS * traces, emb_width),
            half(col_count, emb_width),
            room(1, col_count),
            room(traces, col_count),
            room(STEPS * traces, col_count),
            half(traces, col_count),
            on_src,
            pltpu.SemaphoreType.DMA((3,)),
            pltpu.SemaphoreType.DMA((3,)),
        ]
        + [on_src, on_src, on_dst, on_dst, on_src, on_src]
        + [on_chips] * 4,
        compiler_params=pltpu.CompilerParams(
            collective_id=3, has_side_effects=True, vmem_limit_bytes=TABLE_BYTES
        ),
        name="gather",
    )(
        outside(src_emb.reshape(group, src_count, dst_count, share, emb_width)),
        block_mask, looked.astype(jnp.bfloat16), outside(out_emb),
        outside(log_norm[None, :]), outside(beta_end), outside(alpha_start),
    )
    whole_mask = masks.reshape(src_count * block_mask.shape[0], cols)
    unit_index = jnp.arange(units, dtype=jnp.int32)
    per_piece = piece // unit
    unit_state = (
        (unit_index // per_piece) * col_count + src_place * piece + (unit_index % per_piece) * unit
    )
    unit_block = unit_state // BLK
    owner = unit_block[:, None] == jnp.arange(whole_mask.shape[0], dtype=jnp.int32)[None, :]
    mask = jnp.sum(jnp.where(owner[:, :, None], whole_mask[None], 0), axis=1)
    flat = (mask == 1).reshape(places)
    index = jnp.arange(places, dtype=jnp.int32)
    before = jnp.sum(
        jnp.where((index[None, :] < index[:, None]) & flat[None, :], 1, 0), axis=1
    )
    ids = jnp.sum(
        jnp.where((before[None, :] == index[:, None]) & flat[None, :], index[None, :], 0), axis=1
    ).astype(jnp.int32)
    number = jnp.sum(flat.astype(jnp.int32)).reshape(1)

    guess = places // 5 + 1
    held = min(places, HELD_BYTES // (BLK * unit * 2))
    params = pltpu.CompilerParams(vmem_limit_bytes=VMEM_BYTES)
    top, mass, near, far = pl.pallas_call(
        functools.partial(table_kernel, unit, cols, held),
        out_shape=(
            f32(cols, row_count),
            f32(cols, row_count),
            half(held, BLK, unit),
            jax.ShapeDtypeStruct((max(places - held, 1), BLK, unit), jnp.bfloat16),
        ),
        in_specs=[smem, smem, hbm, hbm],
        out_specs=(vmem, vmem, vmem, anywhere),
        scratch_shapes=[
            half(dst_count, dst_count, share, emb_width),
            half(col_count, emb_width),
            pltpu.SemaphoreType.DMA((2,)),
            half(WRITES, BLK, unit),
        ]
        + [pltpu.VMEM((BLK, unit), jnp.float32)] * 2
        + [pltpu.VMEM((1, unit), jnp.float32)] * 2
        + [pltpu.SemaphoreType.DMA((WRITES,))],
        compiler_params=pltpu.CompilerParams(vmem_limit_bytes=TABLE_BYTES),
        cost_estimate=pl.CostEstimate(
            flops=guess * BLK * unit * emb_width * 2,
            bytes_accessed=guess * BLK * unit,
            transcendentals=guess * BLK * unit,
        ),
        name="table",
    )(ids, number, outside(gathered), outside(dst_emb))
    near = pltpu.with_memory_space_constraint(near, pltpu.VMEM)

    factor, alpha_rows = pl.pallas_call(
        functools.partial(stats_kernel, lines, piece),
        out_shape=(f32(cols, row_count), f32(traces, row_count)),
        in_specs=[vmem] * 4,
        out_specs=(vmem,) * 2,
        scratch_shapes=[
            room(dst_count, 1, piece),
            room(dst_count, 1, piece),
            room(1, piece),
            room(dst_count, 1, piece),
            half(traces, piece),
            half(dst_count, traces, piece),
        ]
        + [on_dst] * 6,
        compiler_params=pltpu.CompilerParams(
            collective_id=0, has_side_effects=True, vmem_limit_bytes=VMEM_BYTES
        ),
        name="stats",
    )(top, mass, alpha_moved, near)

    lanes = -(-cols // LANES) * LANES

    def sweep(kind, alphas, weights):
        outs = [f32(traces, col_count), f32(traces, row_count)]
        if kind:
            outs.append(f32(kind, units, traces, lanes))
        return pl.pallas_call(
            functools.partial(sweep_kernel, unit, cols, held, traces, kind),
            out_shape=tuple(outs),
            in_specs=[smem, smem] + [vmem] * (len(alphas) + 2 + len(weights)) + [anywhere],
            out_specs=(vmem,) * len(outs),
            scratch_shapes=[
                pltpu.VMEM((DEPTH, BLK, unit), jnp.bfloat16),
                pltpu.SemaphoreType.DMA((DEPTH,)),
            ],
            compiler_params=params,
            cost_estimate=pl.CostEstimate(
                flops=guess * BLK * unit * traces * 4,
                bytes_accessed=guess * BLK * unit,
                transcendentals=0,
            ),
            name="sweep%d" % kind,
        )(ids, number, *alphas, factor, *weights, near, far)

    def exchange(ahead, behind, step, later):
        width = piece + LANES
        return pl.pallas_call(
            functools.partial(exchange_kernel, lines, piece, states, step, later),
            out_shape=(f32(traces, row_count), bf16(traces, col_count)),
            in_specs=[hbm] * 3 + [vmem],
            out_specs=(vmem, vmem),
            scratch_shapes=[
                room(traces, col_count),
                room(traces, row_count),
                room(traces, col_count),
                room(traces, col_count),
                pltpu.SemaphoreType.DMA((4,)),
                half(src_count, traces, width),
                half(dst_count, traces, width),
                half(src_count, traces, width),
                half(dst_count, traces, width),
                half(traces, width),
                half(traces, width),
                half(dst_count, traces, width),
                half(src_count, traces, width),
            ]
            + [on_src, on_dst, on_src, on_dst, on_dst, on_src, on_dst, on_src],
            compiler_params=pltpu.CompilerParams(
                collective_id=1 + 3 * step, has_side_effects=True, vmem_limit_bytes=VMEM_BYTES
            ),
            name="exchange",
        )(outside(ahead), outside(behind), outside(emission), near)

    pred, carried = sweep(0, [alpha_rows], [last_weights])
    alpha_1, weights_2 = exchange(pred, carried, 0, 1)
    pred, carried, middle_terms = sweep(1, [alpha_1], [weights_2])
    alpha_2, weights_1 = exchange(pred, carried, 1, 0)
    pred, carried, end_terms = sweep(2, [alpha_2, alpha_rows], [weights_1, last_weights])

    mask_rows = block_mask.shape[0]
    index = np.arange(units)
    all_state = (index // per_piece * col_count + index % per_piece * unit)[None, :] + (
        np.arange(src_count)[:, None] * piece
    )
    unit_blocks = jnp.asarray((all_state // BLK)[:, None, :], jnp.int32)
    norm = mask_rows * src_count * cols * dst_count / (STEPS * traces)
    alpha_end, beta_start, block_counts = pl.pallas_call(
        functools.partial(final_kernel, lines, piece, states, norm),
        out_shape=(
            f32(traces, col_count), f32(traces, row_count), f32(mask_rows, lanes),
        ),
        in_specs=[hbm] * 5 + [vmem],
        out_specs=(vmem,) * 3,
        scratch_shapes=[
            room(traces, col_count),
            room(traces, row_count),
            room(traces, col_count),
            room(1, units, traces, lanes),
            room(2, units, traces, lanes),
            pltpu.SemaphoreType.DMA((5,)),
            room(src_count, traces, piece),
            room(src_count, traces, piece),
            room(traces, piece),
            room(src_count, traces, piece),
            room(dst_count, traces, piece),
            room(dst_count, traces, piece),
            room(traces, piece),
            room(traces, piece),
            room(dst_count, traces, piece),
            room(2 + STEPS, traces, LANES),
            room(src_count, 2 + STEPS, traces, LANES),
            room(2 + STEPS, traces, LANES),
            room(dst_count, 2 + STEPS, traces, LANES),
            room(units, lanes),
            room(src_count, units, lanes),
        ]
        + [on_src, on_src, on_dst, on_dst, on_src, on_src, on_dst, on_dst, on_src, on_src]
        + [pltpu.SemaphoreType.DMA((2,)), on_src, on_src, on_dst, on_dst],
        compiler_params=pltpu.CompilerParams(
            collective_id=2, has_side_effects=True, vmem_limit_bytes=VMEM_BYTES
        ),
        name="final",
    )(
        outside(pred), outside(carried), outside(emission), outside(middle_terms),
        outside(end_terms), unit_blocks,
    )
    return (alpha_end, beta_start, block_counts[:, :cols])


def solution(mesh):
    return jax.shard_map(
        local,
        mesh=mesh,
        in_specs=(
            P("src", None),
            P("dst", None),
            P("dst", None),
            P("dst", None),
            P("dst"),
            P("src", "dst"),
            P(),
            P(None, "src"),
            P(None, "dst"),
        ),
        out_specs=(P(None, "dst"), P(None, "src"), P("src", "dst")),
        check_vma=False,
    )
```

```python
import functools

import jax
import jax.numpy as jnp
import numpy as np
from jax import lax
from jax.experimental import pallas as pl
from jax.experimental.pallas import tpu as pltpu
from jax.sharding import PartitionSpec as P

BLK = 512
STEPS = 3
LANES = 128
DEPTH = 8
WRITES = 4
very_negative = -1e30
GROUP = 6
HELD_BYTES = 48 * 1024 * 1024
TABLE_BYTES = 14 * 1024 * 1024
VMEM_BYTES = 14 * 1024 * 1024


def table_kernel(
    unit, cols, held, ids, count, src_far, dst_far, top, mass, near, far, src, dst, load_sems,
    buf, scores_0, scores_1, best_0, best_1, sems,
):
    number = count[0]
    loads = fetch([(src_far, src), (dst_far, dst)], load_sems)
    src = src.reshape(top.shape[1], src.shape[-1])
    chunk = min(256, unit)
    tall = BLK // 4
    blocks = [
        (slice(q * tall, (q + 1) * tall), slice(c * chunk, (c + 1) * chunk))
        for c in range(unit // chunk)
        for q in range(BLK // tall)
    ]
    top[...] = jnp.full_like(top, very_negative)
    mass[...] = jnp.zeros_like(mass)
    for copy in loads:
        copy.wait()

    def place(slot):
        entry = ids[slot]
        return lax.div(entry, cols), lax.rem(entry, cols)

    def fold(values, join):
        merged = {}
        for (_, span), value in zip(blocks, values):
            old = merged.get(span.start)
            merged[span.start] = value if old is None else join(old, value)
        return list(merged.values())

    def score(slot, scores, where):
        i, j = place(slot)
        down, span = where
        d = dst[pl.ds(pl.multiple_of(j * BLK + down.start, tall), tall), :]
        value = lax.dot_general(
            d, src[pl.ds(pl.multiple_of(i * unit + span.start, chunk), chunk), :],
            (((1,), (1,)), ((), ())), preferred_element_type=jnp.float32,
        )
        scores[down, span] = value
        return jnp.max(value.reshape(tall // 8, 8, chunk), axis=0)

    def settle(best, tops):
        tops = [jnp.max(t, axis=0, keepdims=True) for t in fold(tops, jnp.maximum)]
        best[...] = jnp.concatenate(tops, axis=1)

    def phase(slot, scores, best, later, scores_next, best_next, put):
        level = best[...]
        tops, sums = [], []
        for where in blocks:
            tops.append(score(later, scores_next, where))
            risen = jnp.exp(scores[where] - level[:, where[1]])
            put(where, risen.astype(jnp.bfloat16))
            sums.append(jnp.sum(risen.reshape(tall // 8, 8, chunk), axis=0))
        i, j = place(slot)
        rows = pl.ds(pl.multiple_of(i * unit, unit), unit)
        top[pl.ds(j, 1), rows] = level
        sums = [jnp.sum(t, axis=0, keepdims=True) for t in fold(sums, jnp.add)]
        mass[pl.ds(j, 1), rows] = jnp.concatenate(sums, axis=1)
        settle(best_next, tops)

    def run(low, high, out):
        settle(best_0, [score(low, scores_0, where) for where in blocks])

        def body(p, carry):
            even = low + 2 * p
            odd = jnp.minimum(even + 1, high - 1)
            after = jnp.minimum(even + 2, high - 1)
            with_even, with_odd = out(p, even, odd, high)
            with_even(lambda put: phase(even, scores_0, best_0, odd, scores_1, best_1, put))
            with_odd(lambda put: phase(odd, scores_1, best_1, after, scores_0, best_0, put))
            return carry

        lax.fori_loop(0, lax.div(high - low + 1, 2), body, 0)

    def keep(p, even, odd, high):
        def store(slot):
            def put(where, value):
                near[(slot, *where)] = value

            return put

        return lambda go: go(store(even)), lambda go: go(store(odd))

    def copy(slot):
        b = lax.rem(slot - held, WRITES)
        return pltpu.make_async_copy(buf.at[b], far.at[slot - held], sems.at[b])

    def send(p, even, odd, high):
        def through(slot, live):
            b = lax.rem(slot - held, WRITES)

            def put(where, value):
                buf[(b, *where)] = value

            def go(step):
                @pl.when(slot - held >= WRITES)
                def _():
                    copy(slot - WRITES).wait()

                step(put)

                @pl.when(live)
                def _():
                    copy(slot).start()

            return go

        return through(even, even < high), through(even + 1, even + 1 < high)

    @pl.when(number > held)
    def _():
        run(held, number, send)

    @pl.when(number > 0)
    def _():
        run(0, jnp.minimum(number, held), keep)

    sent = number - held + lax.rem(jnp.maximum(number - held, 0), 2)
    for back in range(1, WRITES + 1):

        @pl.when((number > held) & (sent - back >= 0) & (sent - back < number - held))
        def _():
            copy(held + sent - back).wait()


def sweep_kernel(unit, cols, held, traces, kind, ids, count, *refs):
    if kind == 2:
        alpha, early, factor, weight, last, near, far, pred, carried, terms, buf, sems = refs
    elif kind == 1:
        alpha, factor, weight, near, far, pred, carried, terms, buf, sems = refs
    else:
        alpha, factor, weight, near, far, pred, carried, buf, sems = refs
    number = count[0]
    pred[...] = jnp.zeros_like(pred)
    carried[...] = jnp.zeros_like(carried)
    if kind:
        terms[...] = jnp.zeros_like(terms)

    def copy(slot):
        b = lax.rem(slot - held, DEPTH)
        return pltpu.make_async_copy(far.at[slot - held], buf.at[b], sems.at[b])

    for p in range(DEPTH):

        @pl.when(held + p < number)
        def _():
            copy(held + p).start()

    def group(slots, high, tile):
        begun, found = [], []
        for slot in slots:
            real = jnp.minimum(slot, high - 1)
            entry = ids[real]
            i = lax.div(entry, cols)
            j = lax.rem(entry, cols)
            rows = pl.ds(pl.multiple_of(i * unit, unit), unit)
            places = pl.ds(pl.multiple_of(j * BLK, BLK), BLK)
            share = factor[pl.ds(j, 1), rows] * jnp.where(slot < high, 1.0, 0.0)
            mix = (alpha[:, rows] * share).astype(jnp.bfloat16)
            block = tile(real)
            spread = jnp.dot(weight[:, places], block, preferred_element_type=jnp.float32)
            begun.append((i, j, rows, places, share, mix, block, spread))
        for i, j, rows, places, share, mix, block, spread in begun:
            ahead = lax.dot_general(
                mix, block, (((1,), (1,)), ((), ())), preferred_element_type=jnp.float32
            )
            values = []
            if kind == 1:
                values.append(mix.astype(jnp.float32) * spread)
            elif kind == 2:
                first = (early[:, rows] * share).astype(jnp.bfloat16)
                values.append(first.astype(jnp.float32) * spread)
                values.append(last[:, places].astype(jnp.float32) * ahead)
            values = [jnp.sum(v, axis=1, keepdims=True) for v in values]
            found.append((i, j, rows, places, ahead, share * spread, values))
        for i, j, rows, places, ahead, behind, values in found:
            pred[:, places] += ahead
            carried[:, rows] += behind
            for t, value in enumerate(values):
                hit = lax.broadcasted_iota(jnp.int32, terms.shape[2:], 1) == j
                terms[t, i] += jnp.where(hit, value, 0.0)

    near_count = jnp.minimum(number, held)

    def near_body(g, carry):
        group([g * GROUP + u for u in range(GROUP)], near_count, lambda slot: near[slot])
        return carry

    lax.fori_loop(0, lax.div(near_count + GROUP - 1, GROUP), near_body, 0)

    def far_body(g, carry):
        slots = [held + g * GROUP + u for u in range(GROUP)]
        for slot in slots:

            @pl.when(slot < number)
            def _():
                copy(slot).wait()

        group(slots, number, lambda slot: buf[lax.rem(slot - held, DEPTH)])
        for slot in slots:

            @pl.when(slot + DEPTH < number)
            def _():
                copy(slot + DEPTH).start()

        return carry

    far_count = number - near_count
    lax.fori_loop(0, lax.div(far_count + GROUP - 1, GROUP), far_body, 0)


class Lines:
    def __init__(self, lines):
        self.lines = lines
        self.place = {name: lax.axis_index(name) for name in lines}

    def peer(self, name, k):
        return lax.rem(self.place[name] + k, self.lines[name])

    def origin(self, name, k):
        return lax.rem(self.place[name] + self.lines[name] - k, self.lines[name])

    def greet(self):
        barrier = pltpu.get_barrier_semaphore()
        for name in self.lines:
            for k in range(1, self.lines[name]):
                pl.semaphore_signal(
                    barrier, inc=1, device_id={name: self.peer(name, k)},
                    device_id_type=pl.DeviceIdType.MESH,
                )

    def gather_in(self, more=0):
        total = sum(self.lines.values()) - len(self.lines) + more
        pl.semaphore_wait(pltpu.get_barrier_semaphore(), total)

    def send(self, name, source, landing, send, recv):
        copies = []
        for k in range(1, self.lines[name]):
            copy = pltpu.make_async_remote_copy(
                src_ref=source(self.peer(name, k)),
                dst_ref=landing.at[k],
                send_sem=send.at[k],
                recv_sem=recv.at[k],
                device_id={name: self.peer(name, k)},
                device_id_type=pl.DeviceIdType.MESH,
            )
            copy.start()
            copies.append(copy)
        return copies


def fetch(pairs, sems):
    copies = [
        pltpu.make_async_copy(source, target, sems.at[n])
        for n, (source, target) in enumerate(pairs)
    ]
    for copy in copies:
        copy.start()
    return copies


def gather_kernel(
    lines, group, piece, source, mask, looked, out_far, norm_far, end_far, start,
    rows_far, masks, emission_far, last_far, moved, rows, land_w, out_emb, log_norm, end, emission, last,
    local_sems, alpha_sems, load_sems, *sems,
):
    net = Lines(lines)
    net.greet()
    loads = fetch([(out_far, out_emb), (norm_far, log_norm), (end_far, end)], load_sems)
    src, dst = lines["src"], lines["dst"]
    z, d = net.place["src"], net.place["dst"]
    chips = dst // 2
    sibling = d + 1 - 2 * lax.rem(d, 2)
    held = z * dst + d
    to_dst, to_src = lax.div(held, src), lax.rem(held, src)
    number = d * src + z
    from_src, from_dst = lax.div(number, dst), lax.rem(number, dst)
    away = (to_src != z) | (to_dst != d)
    barrier = pltpu.get_barrier_semaphore()
    mesh_ids = pl.DeviceIdType.MESH
    mine = start.at[:, pl.ds(pl.multiple_of(d * piece, piece), piece)]

    @pl.when(away)
    def _():
        for s, t in ((to_src, to_dst), (from_src, from_dst)):
            pl.semaphore_signal(
                barrier, inc=1, device_id={"src": s, "dst": t}, device_id_type=mesh_ids
            )
        net.gather_in(2)

    @pl.when(jnp.logical_not(away))
    def _():
        net.gather_in()

    def plane(value):
        return pl.ds(value * group, group)

    def pass_on(source_ref, target_ref, send, recv, device):
        copy = pltpu.make_async_remote_copy(
            src_ref=source_ref, dst_ref=target_ref, send_sem=send, recv_sem=recv,
            device_id=device, device_id_type=mesh_ids,
        )
        copy.start()
        return copy

    order = sorted(range(1, src), key=lambda k: min(k, src - k))
    along = []

    def next_round():
        k = order[len(along)]
        other = net.peer("src", k)
        along.append(
            pass_on(
                source.at[:, other, d], rows.at[plane(z), d],
                sems[0].at[k], sems[1].at[k], {"src": other},
            )
        )

    next_round()
    words = net.send("dst", lambda peer: looked, land_w, sems[2], sems[3])
    masks[z] = mask[...]
    marks = [
        pass_on(
            mask, masks.at[z], sems[4].at[k], sems[5].at[k], {"src": net.peer("src", k)}
        )
        for k in range(1, src)
    ]
    move = pltpu.make_async_remote_copy(
        src_ref=mine, dst_ref=moved, send_sem=alpha_sems.at[0], recv_sem=alpha_sems.at[1],
        device_id={"src": to_src, "dst": to_dst}, device_id_type=mesh_ids,
    )
    stay = pltpu.make_async_copy(mine, moved, alpha_sems.at[2])

    @pl.when(away)
    def _():
        move.start()

    @pl.when(jnp.logical_not(away))
    def _():
        stay.start()

    own = pltpu.make_async_copy(source.at[:, z], rows.at[plane(z)], local_sems.at[0])
    own.start()

    across, beside = [], []
    for n, k in enumerate(order):
        along[n].wait_recv()
        if n + 1 < len(order):
            next_round()
        here = plane(net.origin("src", k))
        block = rows.at[here, d]
        for m in range(1, chips):
            across.append(
                pass_on(
                    block, block, sems[6].at[k, m], sems[7].at[k, m],
                    {"dst": lax.rem(d + 2 * m, dst)},
                )
            )
        beside.append(
            pass_on(block, block, sems[8].at[k, 0], sems[9].at[k, 0], {"dst": sibling})
        )
        if n == 0:
            total = looked[...].astype(jnp.float32)
            for w in range(1, dst):
                words[w - 1].wait_recv()
                total = total + land_w[w].astype(jnp.float32)
            total = total.astype(jnp.bfloat16)
            for copy in loads:
                copy.wait()
            cols = out_emb.shape[0]
            width = min(cols, 1024)
            for c in range(0, cols, width):
                logits = lax.dot_general(
                    total, out_emb[c:c + width, :], (((1,), (1,)), ((), ())),
                    preferred_element_type=jnp.float32,
                )
                risen = jnp.exp(logits - log_norm[:, c:c + width])
                emission[:, c:c + width] = risen
                tail = risen[risen.shape[0] - end.shape[0]:]
                last[:, c:c + width] = (tail * end[:, c:c + width]).astype(jnp.bfloat16)
            stores = fetch([(emission, emission_far), (last, last_far)], load_sems)
    for n, k in enumerate(order):
        here = plane(net.origin("src", k))
        for m in range(1, chips):
            across[n * (chips - 1) + m - 1].wait_recv()
            block = rows.at[here, lax.rem(d + dst - 2 * m, dst)]
            beside.append(
                pass_on(block, block, sems[8].at[k, m], sems[9].at[k, m], {"dst": sibling})
            )
    own.wait()
    out = [pltpu.make_async_copy(rows.at[plane(z)], rows_far.at[plane(z)], local_sems.at[0])]
    out[0].start()
    for n, k in enumerate(order):
        here = plane(net.origin("src", k))
        beside[n].wait_recv()
        first = len(order) + n * (chips - 1)
        for copy in beside[first:first + chips - 1]:
            copy.wait_recv()
        copy = pltpu.make_async_copy(rows.at[here], rows_far.at[here], local_sems.at[n + 1])
        copy.start()
        out.append(copy)
    for copy in stores:
        copy.wait()
    for copy in marks:
        copy.wait_recv()

    @pl.when(away)
    def _():
        move.wait_recv()
        move.wait_send()

    @pl.when(jnp.logical_not(away))
    def _():
        stay.wait()

    for copy in out:
        copy.wait()
    for copies in (along, words, marks, across, beside):
        for copy in copies:
            copy.wait_send()


def stats_kernel(
    lines, piece, top_far, mass_far, alpha, near, factor, spread_alpha,
    top, mass, load_sems, parts, land, merged, land_2, own, land_a, *sems,
):
    net = Lines(lines)
    net.greet()
    count = lines["dst"]
    loads = fetch([(top_far, top), (mass_far, mass)], load_sems)
    own[...] = alpha[...].astype(jnp.bfloat16)
    for copy in loads:
        copy.wait()
    for p in range(count):
        rows = slice(p * piece, (p + 1) * piece)
        best = jnp.max(top[:, rows], axis=0, keepdims=True)
        total = jnp.sum(mass[:, rows] * jnp.exp(top[:, rows] - best), axis=0, keepdims=True)
        parts[p] = jnp.where(
            total > 0.0, best + jnp.log(jnp.maximum(total, 1e-37)), very_negative
        )
    net.gather_in()
    first = net.send("dst", lambda peer: parts.at[peer], land, sems[0], sems[1])
    sent = net.send("dst", lambda peer: own, land_a, sems[4], sems[5])
    land[0] = parts[net.place["dst"]]
    for copy in first:
        copy.wait_recv()
    best = land[0]
    for k in range(1, count):
        best = jnp.maximum(best, land[k])
    total = jnp.zeros_like(best)
    for k in range(count):
        total = total + jnp.exp(land[k] - best)
    merged[...] = best + jnp.log(total)
    second = net.send("dst", lambda peer: merged, land_2, sems[2], sems[3])

    def finish(k, level):
        rows = pl.ds(pl.multiple_of(net.origin("dst", k) * piece, piece), piece)
        factor[:, rows] = jnp.exp(top[:, rows] - level)

    finish(0, merged[...])
    for k in range(count):
        rows = pl.ds(pl.multiple_of(net.origin("dst", k) * piece, piece), piece)
        if k:
            sent[k - 1].wait_recv()
        spread_alpha[:, rows] = (own[...] if k == 0 else land_a[k]).astype(jnp.float32)
    for k in range(1, count):
        second[k - 1].wait_recv()
        finish(k, land_2[k])
    for copy in first + second + sent:
        copy.wait_send()


def exchange_kernel(
    lines, piece, states, step, later, pred_far, carried_far, emission, near, alpha, weights,
    pred, carried, glow, glow_next, load_sems,
    out_f, out_b, in_f, in_b, red_f, red_b, land_f, land_b, *sems,
):
    net = Lines(lines)
    traces = pred.shape[0]
    net.greet()
    loads = fetch(
        [
            (pred_far, pred),
            (emission.at[pl.ds(step * traces, traces)], glow),
            (carried_far, carried),
            (emission.at[pl.ds(later * traces, traces)], glow_next),
        ],
        load_sems,
    )
    for copy in loads:
        copy.wait()
    shape = (pred.shape[0], LANES)
    total_f = jnp.broadcast_to(
        jnp.sum(pred[...] * glow[...], axis=1, keepdims=True), shape
    ).astype(jnp.bfloat16)
    total_b = jnp.broadcast_to(
        jnp.sum(carried[...], axis=1, keepdims=True), shape
    ).astype(jnp.bfloat16)
    payload = {"src": (out_f, pred, total_f), "dst": (out_b, carried, total_b)}
    for name, (out, value, total) in payload.items():
        for p in range(lines[name]):
            out[p, :, :piece] = value[:, p * piece:(p + 1) * piece].astype(jnp.bfloat16)
            out[p, :, piece:] = total
    net.gather_in()
    landing = {"src": in_f, "dst": in_b}
    first = {}
    for n, name in enumerate(("src", "dst")):
        out = payload[name][0]
        first[name] = net.send(
            name, lambda peer, out=out: out.at[peer], landing[name], sems[n], sems[2 + n]
        )
    second = {}
    order = (("src", "dst", red_f, land_f), ("dst", "src", red_b, land_b))
    for n, (name, other, red, land) in enumerate(order):
        value = payload[name][0][net.place[name]].astype(jnp.float32)
        for k in range(1, lines[name]):
            first[name][k - 1].wait_recv()
            value = value + landing[name][k].astype(jnp.float32)
        part, total = value[:, :piece], value[:, piece:]
        if name == "src":
            start = pl.multiple_of(net.place["src"] * piece, piece)
            part = part * glow[:, pl.ds(start, piece)]
        red[:, :piece] = part.astype(jnp.bfloat16)
        red[:, piece:] = total.astype(jnp.bfloat16)
        second[other] = net.send(
            other, lambda peer, red=red: red, land, sems[4 + n], sems[6 + n]
        )
    for name, red, land in (("dst", red_f, land_f), ("src", red_b, land_b)):
        total = red[:, piece:piece + 1].astype(jnp.float32)
        for k in range(1, lines[name]):
            second[name][k - 1].wait_recv()
            total = total + land[k, :, piece:piece + 1].astype(jnp.float32)
        scale = states / total
        for k in range(lines[name]):
            part = red[:, :piece] if k == 0 else land[k, :, :piece]
            start = pl.multiple_of(net.origin(name, k) * piece, piece)
            part = part.astype(jnp.float32) * scale
            if name == "dst":
                alpha[:, pl.ds(start, piece)] = part
            else:
                part = part * glow_next[:, pl.ds(start, piece)]
                weights[:, pl.ds(start, piece)] = part.astype(jnp.bfloat16)
    for copies in (*first.values(), *second.values()):
        for copy in copies:
            copy.wait_send()


def final_kernel(
    lines, piece, states, norm, pred_far, carried_far, emission, mid_far, end_far, owner,
    alpha, beta, counts, pred, carried, glow, mid_terms, end_terms, load_sems,
    out_f, in_f, red_f, land_f, out_b, in_b, red_b, natural, land_b,
    sums, in_s, red_s, land_s, mine, in_c, *sems,
):
    net = Lines(lines)
    net.greet()
    src, dst = lines["src"], lines["dst"]
    traces = pred.shape[0]
    loads = fetch(
        [
            (carried_far, carried),
            (pred_far, pred),
            (emission.at[pl.ds((STEPS - 1) * traces, traces)], glow),
            (mid_far, mid_terms),
            (end_far, end_terms),
        ],
        load_sems,
    )
    shape = (traces, LANES)
    number = net.place["dst"] * src + net.place["src"]
    to_src, to_dst = lax.div(number, dst), lax.rem(number, dst)
    held = net.place["src"] * dst + net.place["dst"]
    from_dst, from_src = lax.div(held, src), lax.rem(held, src)
    away = (to_src != net.place["src"]) | (to_dst != net.place["dst"])
    barrier = pltpu.get_barrier_semaphore()

    @pl.when(away)
    def _():
        for s, d in ((to_src, to_dst), (from_src, from_dst)):
            pl.semaphore_signal(
                barrier, inc=1, device_id={"src": s, "dst": d},
                device_id_type=pl.DeviceIdType.MESH,
            )

    for copy in loads:
        copy.wait()
    terms = [mid_terms[0], end_terms[0], end_terms[1]]
    rows = [jnp.sum(pred[...] * glow[...], axis=1, keepdims=True)]
    rows.append(jnp.sum(carried[...], axis=1, keepdims=True))
    for t in terms:
        rows.append(jnp.sum(jnp.sum(t, axis=0), axis=1, keepdims=True))
    for n, row in enumerate(rows):
        sums[n] = jnp.broadcast_to(row, shape)
    for p in range(src):
        out_f[p] = pred[:, p * piece:(p + 1) * piece]
    for p in range(dst):
        out_b[p] = carried[:, p * piece:(p + 1) * piece]

    @pl.when(away)
    def _():
        net.gather_in(2)

    @pl.when(jnp.logical_not(away))
    def _():
        net.gather_in()

    first_s = net.send("src", lambda peer: sums, in_s, sems[0], sems[1])
    first_b = net.send("dst", lambda peer: out_b.at[peer], in_b, sems[2], sems[3])
    first_f = net.send("src", lambda peer: out_f.at[peer], in_f, sems[4], sems[5])

    total = sums[...]
    for k in range(1, src):
        first_s[k - 1].wait_recv()
        total = total + in_s[k]
    red_s[...] = total
    second_s = net.send("dst", lambda peer: red_s, land_s, sems[6], sems[7])

    value = out_b[net.place["dst"]]
    for k in range(1, dst):
        first_b[k - 1].wait_recv()
        value = value + in_b[k]
    red_b[...] = value
    move = pltpu.make_async_remote_copy(
        src_ref=red_b, dst_ref=natural, send_sem=sems[10].at[0], recv_sem=sems[10].at[1],
        device_id={"src": to_src, "dst": to_dst}, device_id_type=pl.DeviceIdType.MESH,
    )

    @pl.when(away)
    def _():
        move.start()

    value = out_f[net.place["src"]]
    for k in range(1, src):
        first_f[k - 1].wait_recv()
        value = value + in_f[k]
    start = pl.multiple_of(net.place["src"] * piece, piece)
    red_f[...] = value * glow[:, pl.ds(start, piece)]
    total = red_s[...]
    for k in range(1, dst):
        second_s[k - 1].wait_recv()
        total = total + land_s[k]
    level = jnp.zeros(mine.shape, jnp.float32)
    for t in range(len(terms)):
        share = norm / total[2 + t]
        level = level + jnp.sum(terms[t] * share[None], axis=1)
    mine[...] = level
    third_c = net.send("src", lambda peer: mine, in_c, sems[11], sems[12])

    @pl.when(away)
    def _():
        move.wait_recv()

    @pl.when(jnp.logical_not(away))
    def _():
        natural[...] = red_b[...]

    third_b = net.send("dst", lambda peer: natural, land_b, sems[13], sems[14])
    second_f = net.send("src", lambda peer: red_f, land_f, sems[8], sems[9])

    scale = states / total[0][:, :1]
    for k in range(src):
        if k:
            second_f[k - 1].wait_recv()
        part = red_f[...] if k == 0 else land_f[k]
        begin = pl.multiple_of(net.origin("src", k) * piece, piece)
        alpha[:, pl.ds(begin, piece)] = part * scale
    value = jnp.zeros(counts.shape, jnp.float32)
    blocks = counts.shape[0]
    wanted = net.place["src"] * blocks + lax.broadcasted_iota(
        jnp.int32, (blocks, owner.shape[2]), 0
    )
    for k in range(src):
        if k:
            third_c[k - 1].wait_recv()
        owned = (owner[net.origin("src", k)] == wanted).astype(jnp.float32)
        value = value + jnp.dot(
            owned, mine[...] if k == 0 else in_c[k],
            precision=lax.Precision.HIGHEST, preferred_element_type=jnp.float32,
        )
    counts[...] = value
    scale = states / total[1][:, :1]
    for k in range(dst):
        if k:
            third_b[k - 1].wait_recv()
        part = natural[...] if k == 0 else land_b[k]
        begin = pl.multiple_of(net.origin("dst", k) * piece, piece)
        beta[:, pl.ds(begin, piece)] = part * scale

    @pl.when(away)
    def _():
        move.wait_send()

    for copies in (first_s, first_b, first_f, second_s, second_f, third_c, third_b):
        for copy in copies:
            copy.wait_send()


def local(
    src_emb, dst_emb, out_emb, word_table, log_norm, block_mask, tokens, alpha_start, beta_end
):
    row_count, emb_width = src_emb.shape
    col_count = dst_emb.shape[0]
    traces = alpha_start.shape[0]
    src_count = lax.axis_size("src")
    dst_count = lax.axis_size("dst")
    states = row_count * src_count
    group = dst_count // src_count
    piece = col_count // src_count
    unit = min(BLK, piece)
    units = row_count // unit
    cols = col_count // BLK
    places = units * cols
    src_place = lax.axis_index("src")
    dst_place = lax.axis_index("dst")
    smem = pl.BlockSpec(memory_space=pltpu.SMEM)
    vmem = pl.BlockSpec(memory_space=pltpu.VMEM)
    anywhere = pl.BlockSpec(memory_space=pl.ANY)
    hbm = pl.BlockSpec(memory_space=pltpu.HBM)
    lines = {"src": src_count, "dst": dst_count}
    on_src = pltpu.SemaphoreType.DMA((src_count,))
    on_dst = pltpu.SemaphoreType.DMA((dst_count,))
    on_chips = pltpu.SemaphoreType.DMA((src_count, dst_count // 2))

    def f32(*shape):
        return jax.ShapeDtypeStruct(shape, jnp.float32)

    def bf16(*shape):
        return jax.ShapeDtypeStruct(shape, jnp.bfloat16)

    def room(*shape, dtype=jnp.float32):
        return pltpu.VMEM(shape, dtype)

    half = functools.partial(room, dtype=jnp.bfloat16)

    def outside(array):
        return pltpu.with_memory_space_constraint(array, pltpu.HBM)

    vocab_slice = word_table.shape[0]
    local_ids = tokens.reshape(-1) - dst_place * vocab_slice
    onehot = (local_ids[:, None] == jnp.arange(vocab_slice, dtype=jnp.int32)[None, :]).astype(
        jnp.bfloat16
    )
    looked = jnp.dot(onehot, word_table, preferred_element_type=jnp.float32)
    share = piece // dst_count
    gathered, masks, emission, last_weights, alpha_moved = pl.pallas_call(
        functools.partial(gather_kernel, lines, group, piece),
        out_shape=(
            pltpu.HBM((dst_count, dst_count, share, emb_width), jnp.bfloat16),
            jax.ShapeDtypeStruct((src_count,) + block_mask.shape, jnp.int32),
            pltpu.HBM((STEPS * traces, col_count), jnp.float32),
            pltpu.HBM((traces, col_count), jnp.bfloat16),
            pltpu.HBM((traces, piece), jnp.float32),
        ),
        in_specs=[hbm, vmem, vmem, hbm, hbm, hbm, hbm],
        out_specs=(hbm, vmem, hbm, hbm, hbm),
        scratch_shapes=[
            half(dst_count, dst_count, share, emb_width),
            half(dst_count, STEPS * traces, emb_width),
            half(col_count, emb_width),
            room(1, col_count),
            room(traces, col_count),
            room(STEPS * traces, col_count),
            half(traces, col_count),
            on_src,
            pltpu.SemaphoreType.DMA((3,)),
            pltpu.SemaphoreType.DMA((3,)),
        ]
        + [on_src, on_src, on_dst, on_dst, on_src, on_src]
        + [on_chips] * 4,
        compiler_params=pltpu.CompilerParams(
            collective_id=3, has_side_effects=True, vmem_limit_bytes=TABLE_BYTES
        ),
        name="gather",
    )(
        outside(src_emb.reshape(group, src_count, dst_count, share, emb_width)),
        block_mask, looked.astype(jnp.bfloat16), outside(out_emb),
        outside(log_norm[None, :]), outside(beta_end), outside(alpha_start),
    )
    whole_mask = masks.reshape(src_count * block_mask.shape[0], cols)
    unit_index = jnp.arange(units, dtype=jnp.int32)
    per_piece = piece // unit
    unit_state = (
        (unit_index // per_piece) * col_count + src_place * piece + (unit_index % per_piece) * unit
    )
    unit_block = unit_state // BLK
    owner = unit_block[:, None] == jnp.arange(whole_mask.shape[0], dtype=jnp.int32)[None, :]
    mask = jnp.sum(jnp.where(owner[:, :, None], whole_mask[None], 0), axis=1)
    flat = (mask == 1).reshape(places)
    index = jnp.arange(places, dtype=jnp.int32)
    before = jnp.sum(
        jnp.where((index[None, :] < index[:, None]) & flat[None, :], 1, 0), axis=1
    )
    ids = jnp.sum(
        jnp.where((before[None, :] == index[:, None]) & flat[None, :], index[None, :], 0), axis=1
    ).astype(jnp.int32)
    number = jnp.sum(flat.astype(jnp.int32)).reshape(1)

    guess = places // 5 + 1
    held = min(places, HELD_BYTES // (BLK * unit * 2))
    params = pltpu.CompilerParams(vmem_limit_bytes=VMEM_BYTES)
    top, mass, near, far = pl.pallas_call(
        functools.partial(table_kernel, unit, cols, held),
        out_shape=(
            f32(cols, row_count),
            f32(cols, row_count),
            half(held, BLK, unit),
            jax.ShapeDtypeStruct((max(places - held, 1), BLK, unit), jnp.bfloat16),
        ),
        in_specs=[smem, smem, hbm, hbm],
        out_specs=(vmem, vmem, vmem, anywhere),
        scratch_shapes=[
            half(dst_count, dst_count, share, emb_width),
            half(col_count, emb_width),
            pltpu.SemaphoreType.DMA((2,)),
            half(WRITES, BLK, unit),
        ]
        + [pltpu.VMEM((BLK, unit), jnp.float32)] * 2
        + [pltpu.VMEM((1, unit), jnp.float32)] * 2
        + [pltpu.SemaphoreType.DMA((WRITES,))],
        compiler_params=pltpu.CompilerParams(vmem_limit_bytes=TABLE_BYTES),
        cost_estimate=pl.CostEstimate(
            flops=guess * BLK * unit * emb_width * 2,
            bytes_accessed=guess * BLK * unit,
            transcendentals=guess * BLK * unit,
        ),
        name="table",
    )(ids, number, outside(gathered), outside(dst_emb))
    near = pltpu.with_memory_space_constraint(near, pltpu.VMEM)

    factor, alpha_rows = pl.pallas_call(
        functools.partial(stats_kernel, lines, piece),
        out_shape=(f32(cols, row_count), f32(traces, row_count)),
        in_specs=[hbm, hbm, vmem, vmem],
        out_specs=(vmem,) * 2,
        scratch_shapes=[
            room(cols, row_count),
            room(cols, row_count),
            pltpu.SemaphoreType.DMA((2,)),
            room(dst_count, 1, piece),
            room(dst_count, 1, piece),
            room(1, piece),
            room(dst_count, 1, piece),
            half(traces, piece),
            half(dst_count, traces, piece),
        ]
        + [on_dst] * 6,
        compiler_params=pltpu.CompilerParams(
            collective_id=0, has_side_effects=True, vmem_limit_bytes=VMEM_BYTES
        ),
        name="stats",
    )(outside(top), outside(mass), alpha_moved, near)

    lanes = -(-cols // LANES) * LANES

    def sweep(kind, alphas, weights):
        outs = [f32(traces, col_count), f32(traces, row_count)]
        if kind:
            outs.append(f32(kind, units, traces, lanes))
        return pl.pallas_call(
            functools.partial(sweep_kernel, unit, cols, held, traces, kind),
            out_shape=tuple(outs),
            in_specs=[smem, smem] + [vmem] * (len(alphas) + 2 + len(weights)) + [anywhere],
            out_specs=(vmem,) * len(outs),
            scratch_shapes=[
                pltpu.VMEM((DEPTH, BLK, unit), jnp.bfloat16),
                pltpu.SemaphoreType.DMA((DEPTH,)),
            ],
            compiler_params=params,
            cost_estimate=pl.CostEstimate(
                flops=guess * BLK * unit * traces * 4,
                bytes_accessed=guess * BLK * unit,
                transcendentals=0,
            ),
            name="sweep%d" % kind,
        )(ids, number, *alphas, factor, *weights, near, far)

    def exchange(ahead, behind, step, later):
        width = piece + LANES
        return pl.pallas_call(
            functools.partial(exchange_kernel, lines, piece, states, step, later),
            out_shape=(f32(traces, row_count), bf16(traces, col_count)),
            in_specs=[hbm] * 3 + [vmem],
            out_specs=(vmem, vmem),
            scratch_shapes=[
                room(traces, col_count),
                room(traces, row_count),
                room(traces, col_count),
                room(traces, col_count),
                pltpu.SemaphoreType.DMA((4,)),
                half(src_count, traces, width),
                half(dst_count, traces, width),
                half(src_count, traces, width),
                half(dst_count, traces, width),
                half(traces, width),
                half(traces, width),
                half(dst_count, traces, width),
                half(src_count, traces, width),
            ]
            + [on_src, on_dst, on_src, on_dst, on_dst, on_src, on_dst, on_src],
            compiler_params=pltpu.CompilerParams(
                collective_id=1 + 3 * step, has_side_effects=True, vmem_limit_bytes=VMEM_BYTES
            ),
            name="exchange",
        )(outside(ahead), outside(behind), outside(emission), near)

    pred, carried = sweep(0, [alpha_rows], [last_weights])
    alpha_1, weights_2 = exchange(pred, carried, 0, 1)
    pred, carried, middle_terms = sweep(1, [alpha_1], [weights_2])
    alpha_2, weights_1 = exchange(pred, carried, 1, 0)
    pred, carried, end_terms = sweep(2, [alpha_2, alpha_rows], [weights_1, last_weights])

    mask_rows = block_mask.shape[0]
    index = np.arange(units)
    all_state = (index // per_piece * col_count + index % per_piece * unit)[None, :] + (
        np.arange(src_count)[:, None] * piece
    )
    unit_blocks = jnp.asarray((all_state // BLK)[:, None, :], jnp.int32)
    norm = mask_rows * src_count * cols * dst_count / (STEPS * traces)
    alpha_end, beta_start, block_counts = pl.pallas_call(
        functools.partial(final_kernel, lines, piece, states, norm),
        out_shape=(
            f32(traces, col_count), f32(traces, row_count), f32(mask_rows, lanes),
        ),
        in_specs=[hbm] * 5 + [vmem],
        out_specs=(vmem,) * 3,
        scratch_shapes=[
            room(traces, col_count),
            room(traces, row_count),
            room(traces, col_count),
            room(1, units, traces, lanes),
            room(2, units, traces, lanes),
            pltpu.SemaphoreType.DMA((5,)),
            room(src_count, traces, piece),
            room(src_count, traces, piece),
            room(traces, piece),
            room(src_count, traces, piece),
            room(dst_count, traces, piece),
            room(dst_count, traces, piece),
            room(traces, piece),
            room(traces, piece),
            room(dst_count, traces, piece),
            room(2 + STEPS, traces, LANES),
            room(src_count, 2 + STEPS, traces, LANES),
            room(2 + STEPS, traces, LANES),
            room(dst_count, 2 + STEPS, traces, LANES),
            room(units, lanes),
            room(src_count, units, lanes),
        ]
        + [on_src, on_src, on_dst, on_dst, on_src, on_src, on_dst, on_dst, on_src, on_src]
        + [pltpu.SemaphoreType.DMA((2,)), on_src, on_src, on_dst, on_dst],
        compiler_params=pltpu.CompilerParams(
            collective_id=2, has_side_effects=True, vmem_limit_bytes=VMEM_BYTES
        ),
        name="final",
    )(
        outside(pred), outside(carried), outside(emission), outside(middle_terms),
        outside(end_terms), unit_blocks,
    )
    return (alpha_end, beta_start, block_counts[:, :cols])


def solution(mesh):
    return jax.shard_map(
        local,
        mesh=mesh,
        in_specs=(
            P("src", None),
            P("dst", None),
            P("dst", None),
            P("dst", None),
            P("dst"),
            P("src", "dst"),
            P(),
            P(None, "src"),
            P(None, "dst"),
        ),
        out_specs=(P(None, "dst"), P(None, "src"), P("src", "dst")),
        check_vma=False,
    )
```
